32 devices in a mesh: section: 4 (over y, x), dp: 8 (over z, core).
Axes of the slice: x: 2, y: 2, z: 4, core: 2. Of those that a mesh axis runs over, the one named last changes fastest.
Arguments:
- block_input: bfloat16 [48, 202, 768], P('dp'), may hold values from -6 to 6
- cotangent: bfloat16 [48, 202, 768], P('dp'), may hold values from -6 to 6
- lengths: int32 [48], P('dp'), may hold values from 1 to 202, 4848 in all
- predicted: int32 [48, 202], P('dp'), may hold values from 0 to 1, as said below
- slab: bfloat16 [4, 768, 4608], P('section')
- in_bias: float32 [4, 3072], P('section'), may hold values from -1.2 to 1.2
- norm_gain: float32 [4, 768], P('section'), may hold values from 0.5 to 1.5
- norm_bias: float32 [4, 768], P('section'), may hold values from -1.8 to 1.8
- feature_draws: int32 [12, 64, 32], replicated, may hold values from -4 to 4
Outputs:
- section_out: bfloat16 [4, 48, 202, 768], P('section', 'dp')
- section_grad: bfloat16 [4, 48, 202, 768], P('section', 'dp')
- slab_grad: float32 [4, 768, 4608], P('section', 'dp')
- bias_grad: float32 [4, 3072], P('section', 'dp')
- gain_grad: float32 [4, 768], P('section', 'dp')
- shift_grad: float32 [4, 768], P('section', 'dp')
The draws below stay inside these ranges and needn't reach their ends.
Inputs may be any that keep to these rules, and one draw needn't show every extreme that they name: `lengths`: a molecule's tokens fill its first positions; padding positions are never read as keys. `predicted`: 1 marks a masked-prediction position; marks at padding positions count for nothing; some molecules have none.
All inputs are finite; a program needn't handle non-finite values. No bound on the sum of `lengths` on one device may be relied on, other than what follows from the above.
Results may differ from the reference program's by a relative error of at most 0.01.
Values may be sent and summed in bfloat16 or wider, within the bound.
A program may use at most 192 MiB of HBM per device.

```python
import math
import jax
import jax.numpy as jnp
import numpy as np
from jax import lax

D = 768
H = 12
FF = 3072
FEATURES = 32
HD = 64
LEN = 202
MOLECULES = 48
N_DP = 8


def draw_slab(key, part):
    shape = (4, D, 6 * D)
    section_index = lax.broadcasted_iota(jnp.int32, shape, 0)
    column = lax.broadcasted_iota(jnp.int32, shape, 2)
    base = jax.random.normal(key, shape, jnp.float32)
    model_scale = D ** (-0.5)
    output_scale = jnp.where(section_index % 2 == 0, 4.0 * model_scale, model_scale)
    scale = jnp.where(column < 3 * D, model_scale, jnp.where(column < 4 * D, output_scale, FF ** (-0.5)))
    return (base * scale).astype(jnp.bfloat16)


def draw_predicted(key, part):
    first_key, second_key = jax.random.split(jax.random.fold_in(key, 17))
    chosen = jax.random.randint(first_key, (MOLECULES, 1), 0, 4) > 0
    marked = jax.random.randint(second_key, (MOLECULES, LEN), 0, 20) < 3
    return (chosen & marked).astype(jnp.int32)


def with_ends(drawn, key, low, top_value):
    shape = drawn.shape
    index_at = [jax.random.randint(jax.random.fold_in(key, axis), (), 0, shape[axis]) for axis in range(len(shape))]
    drawn = drawn.at[tuple(index_at)].set(low)
    longest = shape.index(max(shape))
    index_at[longest] = (index_at[longest] + 1) % shape[longest]
    return drawn.at[tuple(index_at)].set(top_value)


def level_of(own_key, shape, shards, low, high):
    factor_of = 1.0
    for dim, shards_of in shards:
        heights = jax.random.uniform(jax.random.fold_in(jax.random.fold_in(own_key, 6), dim), (shards_of,), jnp.float32, low / len(shards), high / len(shards))
        factor_of = factor_of * jnp.repeat(jnp.exp(heights), shape[dim] // shards_of).reshape((-1,) + (1,) * (len(shape) - 1 - dim))
    return factor_of


def split_up(amount, total, bound, lean):
    loads = [(1 << 20) // math.isqrt(rank ** lean) + 1 for rank in range(2, amount + 1)]
    surplus, given = total - bound - (amount - 1), [1] * (amount - 1)
    while surplus > 0:
        movable = [i for i in range(amount - 1) if given[i] < bound]
        pool, remaining = sum([loads[i] for i in movable]), surplus
        for i in movable:
            more = min(bound - given[i], max(1, remaining * loads[i] // pool), surplus)
            given[i] = given[i] + more
            surplus = surplus - more
    return np.array([bound] + given)


def ragged_sizes(rng, amount, total, bound, skew):
    if amount == 2:
        one = jax.random.randint(rng, (), max(1, total - bound), min(bound, total - 1) + 1)
        return jnp.stack([one, total - one])
    tallies = jnp.asarray(split_up(amount, total, bound, skew), jnp.int32)
    pairs = (amount - 1) // 2
    giver, receiver = tallies[1:1 + 2 * pairs:2], tallies[2:2 + 2 * pairs:2]
    room = jnp.minimum(giver - 1, bound - receiver)
    passed = jax.random.randint(jax.random.fold_in(rng, 1), (pairs,), 0, 1 << 20) % (room + 1)
    tallies = tallies.at[1:1 + 2 * pairs:2].set(giver - passed).at[2:2 + 2 * pairs:2].set(receiver + passed)
    return tallies[jax.random.permutation(jax.random.fold_in(rng, 2), amount)]


def gaussian(own_key, extent, spread, reach, cuts=(), held_as=jnp.bfloat16):
    result = jax.random.normal(own_key, extent, jnp.float32) * spread
    if len(cuts) > 0:
        result = level_of(own_key, extent, cuts, -0.22, 0.18) * result
    return jnp.clip(result, min=-reach, max=reach).astype(held_as)


def setup_inputs(seed: int = 0) -> dict:
    seeds = jax.random.split(jax.random.key(seed), 10)
    block_input = gaussian(seeds[0], (MOLECULES, LEN, D), 1.0, 6.0, ((0, 8),))
    cotangent = gaussian(seeds[1], (MOLECULES, LEN, D), 1.0, 6.0, ((0, 8),))
    lengths = ragged_sizes(seeds[2], MOLECULES, MOLECULES * LEN // 2, LEN, 1).astype(jnp.int32)
    predicted = draw_predicted(jax.random.fold_in(seeds[9], 71), 0)
    slab = draw_slab(jax.random.fold_in(seeds[9], 71), 0)
    in_bias = gaussian(seeds[5], (4, FF), 0.2, 1.2, ((0, 4),), jnp.float32)
    norm_gain = jnp.clip(1.0 + 0.1 * jax.random.normal(seeds[6], (4, D), jnp.float32), 0.5, 1.5)
    norm_bias = gaussian(seeds[7], (4, D), 0.3, 1.8, ((0, 4),), jnp.float32)
    feature_draws = with_ends(jax.random.randint(seeds[8], (H, HD, FEATURES), -4, 5), jax.random.fold_in(seeds[8], 1), -4, 4).astype(jnp.int32)
    return {"block_input": block_input, "cotangent": cotangent, "lengths": lengths, "predicted": predicted, "slab": slab, "in_bias": in_bias, "norm_gain": norm_gain, "norm_bias": norm_bias, "feature_draws": feature_draws}


highest = lax.Precision.HIGHEST
norm_epsilon = 1e-05

@jax.custom_vjp
def low(v):
    return lax.optimization_barrier(v.astype(jnp.bfloat16)).astype(jnp.float32)

@jax.custom_vjp
def low_back(v):
    return v

def low_keep(v):
    return (low(v), None)

def low_pass(kept, grad):
    return (grad,)

def back_keep(v):
    return (v, None)

def back_low(kept, grad):
    return (low(grad),)
low.defvjp(low_keep, low_pass)
low_back.defvjp(back_keep, back_low)

def matmul(left, right):
    return jnp.dot(left, right, precision=highest, preferred_element_type=jnp.float32)

def layer_norm(residual_sum, scale_row, shift_row):
    centered = residual_sum - lax.optimization_barrier(jnp.mean(residual_sum, axis=-1, keepdims=True))
    variance = lax.optimization_barrier(jnp.mean(centered * centered, axis=-1, keepdims=True))
    return centered * lax.rsqrt(variance + norm_epsilon) * scale_row + shift_row

def linear_mix(projected, valid_mask, feature_map):
    head_count, head_dim = (feature_map.shape[0], feature_map.shape[1])
    model_width = projected.shape[-1] // 3
    split_shape = projected.shape[:2] + (head_count, head_dim)
    queries = projected[..., :model_width].reshape(split_shape)
    keys_part = projected[..., model_width:2 * model_width].reshape(split_shape)
    values_part = projected[..., 2 * model_width:].reshape(split_shape)
    query_feat = jax.nn.softplus(jnp.einsum('mlhd,hdf->mlhf', queries, feature_map, precision=highest))
    key_feat = jax.nn.softplus(jnp.einsum('mlhd,hdf->mlhf', keys_part, feature_map, precision=highest))
    key_feat = key_feat * valid_mask[:, :, None, None]
    summary = jnp.einsum('mlhf,mlhd->mhfd', key_feat, values_part, precision=highest)
    totals = lax.optimization_barrier(jnp.sum(key_feat, axis=1))
    numerator = jnp.einsum('mlhf,mhfd->mlhd', query_feat, summary, precision=highest)
    denominator = jnp.einsum('mlhf,mhf->mlh', query_feat, totals, precision=highest)
    return (numerator / denominator[..., None]).reshape(projected.shape[:2] + (model_width,))

def attention_section(section_input, weight, bias_row, scale_row, shift_row, valid_mask, feature_map):
    mol_count, length, model_width = section_input.shape
    flat_rows = section_input.reshape(mol_count * length, model_width)
    projected = low_back(matmul(flat_rows, weight[:, :3 * model_width]) + bias_row[:3 * model_width])
    mixed_heads = low(linear_mix(projected.reshape(mol_count, length, 3 * model_width), valid_mask, feature_map))
    branch = low_back(matmul(mixed_heads.reshape(mol_count * length, model_width), weight[:, 3 * model_width:4 * model_width].T) + bias_row[3 * model_width:])
    normed = layer_norm(flat_rows + branch, scale_row, shift_row)
    return low_back(low(normed)).reshape(mol_count, length, model_width)

def feed_section(section_input, weight, down_first, bias_row, scale_row, shift_row):
    mol_count, length, model_width = section_input.shape
    flat_rows = section_input.reshape(mol_count * length, model_width)
    hidden_pre = low_back(matmul(flat_rows, weight[:, :4 * model_width]) + bias_row)
    hidden = low(jax.nn.gelu(hidden_pre, approximate=False))
    down_full = jnp.concatenate([down_first, weight[:, 4 * model_width:]], axis=1)
    branch = low_back(matmul(hidden, down_full.T))
    normed = layer_norm(flat_rows + branch, scale_row, shift_row)
    return low_back(low(normed)).reshape(mol_count, length, model_width)

def stack_forward(block_rows, perturb, slab_arg, bias_arg, gain_arg, shift_arg, valid_mask, feature_map):
    model_width = slab_arg.shape[1]
    first = attention_section(block_rows + perturb[0], slab_arg[0], bias_arg[0], gain_arg[0], shift_arg[0], valid_mask, feature_map)
    second = feed_section(first + perturb[1], slab_arg[1], slab_arg[0][:, 4 * model_width:], bias_arg[1], gain_arg[1], shift_arg[1])
    third = attention_section(second + perturb[2], slab_arg[2], bias_arg[2], gain_arg[2], shift_arg[2], valid_mask, feature_map)
    fourth = feed_section(third + perturb[3], slab_arg[3], slab_arg[2][:, 4 * model_width:], bias_arg[3], gain_arg[3], shift_arg[3])
    return (first, second, third, fourth)

def reference(block_input, cotangent, lengths, predicted, slab, in_bias, norm_gain, norm_bias, feature_draws):
    molecules, length, model_width = block_input.shape
    head_dim = feature_draws.shape[1]
    feature_map = feature_draws.astype(jnp.float32) * jnp.sqrt(3.0 / (20.0 * head_dim))
    positions = jnp.arange(length, dtype=jnp.int32)
    valid_all = (positions[None, :] < lengths[:, None]).astype(jnp.float32)
    targets = cotangent.astype(jnp.float32) * (valid_all * predicted.astype(jnp.float32))[:, :, None]
    group_count = N_DP
    per_group = molecules // group_count
    blocks = block_input.astype(jnp.float32).reshape(group_count, per_group, length, model_width)
    valids = valid_all.reshape(group_count, per_group, length)
    target_groups = targets.reshape(group_count, per_group, length, model_width)
    slab_full = slab.astype(jnp.float32)
    bias_full = in_bias.astype(jnp.float32)
    gain_full = norm_gain.astype(jnp.float32)
    shift_full = norm_bias.astype(jnp.float32)

    def group_step(totals, pieces):
        block_rows, valid_mask, target_rows = pieces
        perturb = jnp.zeros((4,) + block_rows.shape, jnp.float32)

        def run(perturb_arg, slab_arg, bias_arg, gain_arg, shift_arg):
            return stack_forward(block_rows, perturb_arg, slab_arg, bias_arg, gain_arg, shift_arg, valid_mask, feature_map)
        outputs, pullback = jax.vjp(run, perturb, slab_full, bias_full, gain_full, shift_full)
        zero_rows = jnp.zeros_like(target_rows)
        back_perturb, back_slab, back_bias, back_gain, back_shift = pullback((zero_rows, zero_rows, zero_rows, target_rows))
        totals = jax.tree.map(jnp.add, totals, (back_slab, back_bias, back_gain, back_shift))
        return (totals, (jnp.stack(outputs).astype(jnp.bfloat16), back_perturb.astype(jnp.bfloat16)))
    start = (jnp.zeros_like(slab_full), jnp.zeros_like(bias_full), jnp.zeros_like(gain_full), jnp.zeros_like(shift_full))
    totals, (outs_all, grads_all) = lax.scan(group_step, start, (blocks, valids, target_groups))
    section_out = jnp.moveaxis(outs_all, 1, 0).reshape(4, molecules, length, model_width)
    section_grad = jnp.moveaxis(grads_all, 1, 0).reshape(4, molecules, length, model_width)
    return (section_out, section_grad, totals[0], totals[1], totals[2], totals[3])
```

```python
import functools

import jax
import jax.numpy as jnp
from jax import lax
from jax.experimental import pallas as pl
from jax.experimental.pallas import tpu as pltpu
from jax.sharding import PartitionSpec as P

MESH = pl.DeviceIdType.MESH
norm_epsilon = 1e-05
bf16 = jnp.bfloat16
f32 = jnp.float32


def dot(a, b):
    return lax.dot_general(a, b, (((1,), (0,)), ((), ())), preferred_element_type=f32)


def dot_cols(a, b):
    return lax.dot_general(a, b, (((1,), (1,)), ((), ())), preferred_element_type=f32)


def dot_rows(a, b):
    return lax.dot_general(a, b, (((0,), (0,)), ((), ())), preferred_element_type=f32)


def softplus(u):
    return jnp.maximum(u, 0.0) + jnp.log1p(jnp.exp(-jnp.abs(u)))


def block_mask(feature_rows, value_cols, features, head_dim):
    r = lax.broadcasted_iota(jnp.int32, (feature_rows, value_cols), 0) // features
    c = lax.broadcasted_iota(jnp.int32, (feature_rows, value_cols), 1) // head_dim
    return r == c


def pipeline_kernel(
    cfg,
    len_ref,
    x_hbm,
    cot_hbm,
    pred_ref,
    slab_hbm,
    bias_ref,
    gain_ref,
    shift_ref,
    fmap_ref,
    out_hbm,
    grad_hbm,
    g1_hbm,
    g2_hbm,
    bias_grad_ref,
    gain_grad_ref,
    shift_grad_ref,
    w,
    u,
    xin,
    out,
    dyin,
    dxo,
    dbr,
    nbuf,
    rbuf,
    buf_a,
    buf_b,
    szbuf,
    stage,
    land,
    load_sem,
    x_sem,
    cot_sem,
    u_send,
    u_recv,
    f_send,
    f_recv,
    b_send,
    b_recv,
    out_sem,
    grad_sem,
    g_sem,
):
    M, L, LP, D, FF, HD, FE, NS, ND, fscale = cfg
    HALF = FF // 2
    GH = 256 // HD
    G = D // 256
    GF = GH * FE
    s = lax.axis_index("section")
    d = lax.axis_index("dp")
    odd = lax.rem(s, 2)
    is_attn = odd == 0
    is_ff = odd == 1
    first = s == 0
    last = s == NS - 1
    sib = d + 1 - 2 * lax.rem(d, 2)
    mate = d + 2 - 4 * lax.rem(d // 2, 2)
    quarter = D // 4

    barrier = pltpu.get_barrier_semaphore()

    def greet(cond, ts, td):
        @pl.when(cond)
        def _():
            pl.semaphore_signal(barrier, inc=1, device_id=(ts, td), device_id_type=MESH)

    always = s >= 0
    greet(always, s, sib)
    greet(always, s, mate)
    greet(s > 0, s - 1, d)
    greet(s < NS - 1, s + 1, d)

    w_copy = pltpu.make_async_copy(slab_hbm.at[0, :, pl.ds(0, FF)], w, load_sem.at[0])
    u_copy = pltpu.make_async_copy(
        slab_hbm.at[0, :, pl.ds(FF, HALF)], u.at[:, pl.ds(HALF, HALF)], load_sem.at[1]
    )
    w_copy.start()

    @pl.when(first)
    def _():
        for m in range(M):
            pltpu.make_async_copy(x_hbm.at[m], land.at[m], x_sem.at[m]).start()

    @pl.when(last)
    def _():
        for m in range(M):
            pltpu.make_async_copy(cot_hbm.at[m], land.at[m], x_sem.at[m]).start()

    @pl.when(is_ff)
    def _():
        u_copy.start()

    bias_grad_ref[...] = jnp.zeros_like(bias_grad_ref)
    gain_grad_ref[...] = jnp.zeros_like(gain_grad_ref)
    shift_grad_ref[...] = jnp.zeros_like(shift_grad_ref)

    @pl.when(first | last)
    def _():
        pl.semaphore_wait(barrier, 3)

    @pl.when((s > 0) & (s < NS - 1))
    def _():
        pl.semaphore_wait(barrier, 4)

    q0 = lax.rem(d, 4)
    q_own = pl.ds(pl.multiple_of(q0 * quarter, quarter), quarter)
    q_mate = pl.ds(pl.multiple_of((q0 + 2 - 4 * (q0 // 2)) * quarter, quarter), quarter)
    left = pl.ds(0, HALF)

    def u_from_section():
        return pltpu.make_async_remote_copy(
            slab_hbm.at[0, q_own, pl.ds(FF, HALF)],
            u.at[q_own, left],
            u_send.at[0],
            u_recv.at[0],
            device_id=(s + 1, d),
            device_id_type=MESH,
        )

    def u_copy_to(rows, k, td):
        return pltpu.make_async_remote_copy(
            u.at[rows, left],
            u.at[rows, left],
            u_send.at[k],
            u_recv.at[k],
            device_id=(s, td),
            device_id_type=MESH,
        )

    @pl.when(is_attn & (s < NS - 1))
    def _():
        u_from_section().start()

    w_copy.wait()

    @pl.when(is_ff)
    def _():
        u_from_section().wait_recv()
        u_copy_to(q_own, 1, mate).start()
        u_copy_to(q_own, 2, sib).start()
        u_copy_to(q_own, 1, mate).wait_recv()
        u_copy_to(q_mate, 3, sib).start()
        u_copy_to(q_own, 2, sib).wait_recv()
        u_copy_to(q_mate, 3, sib).wait_recv()
        u_copy.wait()

    g_row = gain_ref[...]
    b_row = shift_ref[...]
    row_id = lax.broadcasted_iota(jnp.int32, (LP, GF), 0)
    head_mask = block_mask(GF, 256, FE, HD)
    pair_mask = jnp.concatenate([head_mask, head_mask], axis=1)
    ones_cols = jnp.ones((LP, 256), bf16)

    def norm_forward(m, pre):
        mean = jnp.mean(pre, axis=-1, keepdims=True)
        cen = pre - mean
        r = lax.rsqrt(jnp.mean(cen * cen, axis=-1, keepdims=True) + norm_epsilon)
        n = cen * r
        nbuf[m] = n
        rbuf[m] = r
        out[m] = (n * g_row + b_row).astype(bf16)

    def norm_backward(m):
        dy = dyin[m].astype(f32)
        n = nbuf[m]
        dn = dy * g_row
        dyn = dy * n
        m1 = jnp.mean(dn, axis=-1, keepdims=True)
        m2 = jnp.mean(dn * n, axis=-1, keepdims=True)
        gain_grad_ref[...] += jnp.sum(dyn, axis=0, keepdims=True)
        shift_grad_ref[...] += jnp.sum(dy, axis=0, keepdims=True)
        dpre = rbuf[m] * (dn - m1 - n * m2)
        dbr[m] = dpre.astype(bf16)
        return dpre

    def attend_forward(m):
        x = xin[m]
        valid = row_id < len_ref[m]
        for g in range(G):
            cols = [pl.ds(k * D + 256 * g, 256) for k in range(3)]
            qkv = [
                (dot(x, w[:, c]) + bias_ref[:, c]).astype(bf16) for c in cols
            ]
            fq = softplus(dot(qkv[0], fmap_ref[g]) * fscale).astype(bf16)
            fk = softplus(dot(qkv[1], fmap_ref[g]) * fscale)
            fk = jnp.where(valid, fk, 0.0).astype(bf16)
            buf_a[m, :, pl.ds(256 * g, 256)] = qkv[2]
            buf_a[m, :, pl.ds(D + GF * g, GF)] = fq
            buf_a[m, :, pl.ds(D + GF * (G + g), GF)] = fk
            sz = dot_rows(fk, jnp.concatenate([qkv[2], ones_cols], axis=1))
            sz = jnp.where(pair_mask, sz, 0.0).astype(bf16)
            szbuf[m, g] = sz
            nd = dot(fq, sz)
            buf_a[m, :, pl.ds(3 * D + 256 * g, 256)] = (nd[:, :256] / nd[:, 256:]).astype(bf16)
        branch = dot_cols(buf_a[m, :, pl.ds(3 * D, D)], w[:, pl.ds(3 * D, D)])
        norm_forward(m, x.astype(f32) + (branch + bias_ref[:, pl.ds(3 * D, D)]))

    def feed_forward(m):
        x = xin[m]
        tile = 512
        for j in range(FF // tile):
            c = pl.ds(j * tile, tile)
            a = dot(x, w[:, c]) + bias_ref[:, c]
            cdf = 0.5 + 0.5 * lax.erf(a * 0.7071067811865476)
            pdf = jnp.exp(a * a * -0.5) * 0.3989422804014327
            buf_a[m, :, c] = (a * cdf).astype(bf16)
            buf_b[m, :, c] = (cdf + a * pdf).astype(bf16)
        branch = dot_cols(buf_a[m], u[...])
        norm_forward(m, x.astype(f32) + branch)

    def attend_backward(m):
        dpre = norm_backward(m)
        db = dbr[m]
        valid = row_id < len_ref[m]
        ocols = pl.ds(3 * D, D)
        bias_grad_ref[:, ocols] += jnp.sum(db.astype(f32), axis=0, keepdims=True)
        for g in range(G):
            dmix = dot(db, w[:, pl.ds(3 * D + 256 * g, 256)])
            v = buf_a[m, :, pl.ds(256 * g, 256)]
            fq = buf_a[m, :, pl.ds(D + GF * g, GF)]
            fk = buf_a[m, :, pl.ds(D + GF * (G + g), GF)]
            sz = szbuf[m, g]
            nd = dot(fq, sz)
            rden = 1.0 / nd[:, 256:]
            dnum = dmix * rden
            dden = -dnum * (nd[:, :256] * rden)
            de = jnp.concatenate([dnum, dden], axis=1).astype(bf16)
            dfq = dot_cols(de, sz)
            dsz = jnp.where(pair_mask, dot_rows(fq, de), 0.0).astype(bf16)
            dfk = dot_cols(jnp.concatenate([v, ones_cols], axis=1), dsz)
            dv = dot(fk, dsz[:, :256]).astype(bf16)
            duq = dfq * (1.0 - jnp.exp(-fq.astype(f32)))
            duk = jnp.where(valid, dfk, 0.0) * (1.0 - jnp.exp(-fk.astype(f32)))
            dq = (dot_cols(duq.astype(bf16), fmap_ref[g]) * fscale).astype(bf16)
            dk = (dot_cols(duk.astype(bf16), fmap_ref[g]) * fscale).astype(bf16)
            for k, val in enumerate((dq, dk, dv)):
                c = pl.ds(k * D + 256 * g, 256)
                buf_b[m, :, c] = val
                bias_grad_ref[:, c] += jnp.sum(val.astype(f32), axis=0, keepdims=True)
        dx = dpre + dot_cols(buf_b[m, :, pl.ds(0, 3 * D)], w[:, pl.ds(0, 3 * D)])
        dxo[m] = dx.astype(bf16)

    def feed_backward(m):
        dpre = norm_backward(m)
        db = dbr[m]
        tile = 512
        for j in range(FF // tile):
            c = pl.ds(j * tile, tile)
            da = (dot(db, u[:, c]) * buf_b[m, :, c].astype(f32)).astype(bf16)
            buf_b[m, :, c] = da
            bias_grad_ref[:, c] += jnp.sum(da.astype(f32), axis=0, keepdims=True)
        dx = dpre + dot_cols(buf_b[m], w[...])
        dxo[m] = dx.astype(bf16)

    def next_copy(m):
        return pltpu.make_async_remote_copy(
            out.at[m],
            xin.at[m],
            f_send.at[m],
            f_recv.at[m],
            device_id=(s + 1, d),
            device_id_type=MESH,
        )

    def back_copy(m):
        return pltpu.make_async_remote_copy(
            dxo.at[m],
            dyin.at[m],
            b_send.at[m],
            b_recv.at[m],
            device_id=(s - 1, d),
            device_id_type=MESH,
        )

    def out_copy(m):
        return pltpu.make_async_copy(out.at[m], out_hbm.at[m], out_sem.at[m])

    def grad_copy(m):
        return pltpu.make_async_copy(dxo.at[m], grad_hbm.at[m], grad_sem.at[m])

    def land_copy(m):
        return pltpu.make_async_copy(x_hbm.at[m], land.at[m], x_sem.at[m])

    pad_zero = jnp.zeros((LP - L, D), bf16)
    eye = lax.broadcasted_iota(jnp.int32, (L, L), 0) == lax.broadcasted_iota(jnp.int32, (L, L), 1)

    def forward_step(m):
        @pl.when(first)
        def _():
            land_copy(m).wait()
            xin[m] = jnp.concatenate([land[m], pad_zero], axis=0)

        @pl.when(s > 0)
        def _():
            next_copy(m).wait_recv()

        @pl.when(is_attn)
        def _():
            attend_forward(m)

        @pl.when(is_ff)
        def _():
            feed_forward(m)

        @pl.when(s < NS - 1)
        def _():
            next_copy(m).start()

        out_copy(m).start()

    def backward_step(m):
        @pl.when(last)
        def _():
            land_copy(m).wait()
            row = jnp.where(
                lax.broadcasted_iota(jnp.int32, (1, L), 1) < len_ref[m],
                pred_ref[pl.ds(m, 1), :].astype(f32),
                0.0,
            )
            col = jnp.sum(jnp.where(eye, row, 0.0), axis=1, keepdims=True)
            masked = (land[m].astype(f32) * col).astype(bf16)
            dyin[m] = jnp.concatenate([masked, pad_zero], axis=0)

        @pl.when(s < NS - 1)
        def _():
            back_copy(m).wait_recv()

        @pl.when(is_attn)
        def _():
            attend_backward(m)

        @pl.when(is_ff)
        def _():
            feed_backward(m)

        @pl.when(s > 0)
        def _():
            back_copy(m).start()

        grad_copy(m).start()

    back_start = 6 - (s * s) // 3

    def tick(t, carry):
        mf = t - s
        mb = t - back_start

        @pl.when((mf >= 0) & (mf < M))
        def _():
            forward_step(mf)

        @pl.when((mb >= 0) & (mb < M))
        def _():
            backward_step(mb)

        return carry

    lax.fori_loop(0, 6 + M, tick, 0)

    def flat(ref, c):
        return ref[:, :, c].reshape(M * LP, c.size)

    @pl.when(is_ff)
    def _():
        for k in range(2):
            src = (xin, dbr)[k]
            rhs = (buf_b, buf_a)[k]
            dst = (g1_hbm, g2_hbm)[k]
            for j in range(FF // D):
                c = pl.ds(j * D, D)
                if j + k > 0:
                    cp.wait()
                stage[...] = dot_rows(flat(src, pl.ds(0, D)), flat(rhs, c))
                cp = pltpu.make_async_copy(stage, dst.at[:, c], g_sem.at[0])
                cp.start()
        cp.wait()

    @pl.when(is_attn)
    def _():
        for j in range(FF // D):
            c = pl.ds(j * D, D)
            if j > 0:
                cp.wait()
            if j < 3:
                stage[...] = dot_rows(flat(xin, pl.ds(0, D)), flat(buf_b, c))
            else:
                stage[...] = dot_rows(flat(dbr, pl.ds(0, D)), flat(buf_a, c))
            cp = pltpu.make_async_copy(stage, g1_hbm.at[:, c], g_sem.at[0])
            cp.start()
        cp.wait()
        stage[...] = jnp.zeros_like(stage)
        for j in range(FF // D):
            cp = pltpu.make_async_copy(stage, g2_hbm.at[:, pl.ds(j * D, D)], g_sem.at[0])
            cp.start()
            cp.wait()

    @pl.when(is_attn & (s < NS - 1))
    def _():
        u_from_section().wait_send()

    @pl.when(is_ff)
    def _():
        u_copy_to(q_own, 1, mate).wait_send()
        u_copy_to(q_own, 2, sib).wait_send()
        u_copy_to(q_mate, 3, sib).wait_send()

    for m in range(M):
        @pl.when(s < NS - 1)
        def _():
            next_copy(m).wait_send()

        @pl.when(s > 0)
        def _():
            back_copy(m).wait_send()

        out_copy(m).wait()
        grad_copy(m).wait()


def shards(
    block_input, cotangent, lengths, predicted, slab, in_bias, norm_gain, norm_bias, feature_draws
):
    NS = lax.axis_size("section")
    ND = lax.axis_size("dp")
    M, L, D = block_input.shape
    FF = in_bias.shape[1]
    H, HD, FE = feature_draws.shape
    LP = (L + 15) // 16 * 16
    GH = 256 // HD
    G = D // 256
    GF = GH * FE
    fscale = float((3.0 / (20.0 * HD)) ** 0.5)
    draws = feature_draws.astype(bf16).reshape(G, GH, HD, FE)
    same = jnp.eye(GH, dtype=bf16)
    fmap = (draws[:, :, :, None, :] * same[None, :, None, :, None]).reshape(G, GH * HD, GF)
    cfg = (M, L, LP, D, FF, HD, FE, NS, ND, fscale)
    hbm = pl.BlockSpec(memory_space=pl.ANY)
    vmem = pl.BlockSpec(memory_space=pltpu.VMEM)
    smem = pl.BlockSpec(memory_space=pltpu.SMEM)
    dma = pltpu.SemaphoreType.DMA
    rows_bf = pltpu.VMEM((M, LP, D), bf16)
    wide_bf = pltpu.VMEM((M, LP, FF), bf16)
    outs = pl.pallas_call(
        functools.partial(pipeline_kernel, cfg),
        out_shape=[
            jax.ShapeDtypeStruct((M, LP, D), bf16),
            jax.ShapeDtypeStruct((M, LP, D), bf16),
            jax.ShapeDtypeStruct((D, FF), f32),
            jax.ShapeDtypeStruct((D, FF), f32),
            jax.ShapeDtypeStruct((1, FF), f32),
            jax.ShapeDtypeStruct((1, D), f32),
            jax.ShapeDtypeStruct((1, D), f32),
        ],
        in_specs=[smem, hbm, hbm, vmem, hbm, vmem, vmem, vmem, vmem],
        out_specs=[hbm, hbm, hbm, hbm, vmem, vmem, vmem],
        scratch_shapes=[
            pltpu.VMEM((D, FF), bf16),
            pltpu.VMEM((D, FF), bf16),
            rows_bf,
            rows_bf,
            rows_bf,
            rows_bf,
            rows_bf,
            pltpu.VMEM((M, LP, D), f32),
            pltpu.VMEM((M, LP, 1), f32),
            wide_bf,
            wide_bf,
            pltpu.VMEM((M, G, GF, 512), bf16),
            pltpu.VMEM((D, D), f32),
            pltpu.VMEM((M, L, D), bf16),
            dma((2,)),
            dma((M,)),
            dma((M,)),
            dma((4,)),
            dma((4,)),
            dma((M,)),
            dma((M,)),
            dma((M,)),
            dma((M,)),
            dma((M,)),
            dma((M,)),
            dma((1,)),
        ],
        compiler_params=pltpu.CompilerParams(
            collective_id=0, has_side_effects=True, vmem_limit_bytes=60 * 2**20
        ),
        name="pipeline",
    )(
        lengths,
        block_input,
        cotangent,
        predicted,
        slab,
        in_bias,
        norm_gain,
        norm_bias,
        fmap,
    )
    section_out, section_grad, g1, g2, bias_grad, gain_grad, shift_grad = outs
    HALF = FF // 2

    def scatter(value):
        return lax.psum_scatter(value, "dp", scatter_dimension=0, tiled=True)

    both = scatter(jnp.concatenate([g1, g2], axis=1))
    pairs = [(i, i - 1) for i in range(1, NS, 2)]
    arrived = lax.ppermute(both[:, FF : FF + HALF], "section", pairs)
    is_attention = lax.axis_index("section") % 2 == 0
    rest = jnp.where(is_attention, arrived, both[:, FF + HALF :])
    own = jnp.concatenate([both[:, :FF], rest], axis=1)
    return (
        section_out[None, :, :L],
        section_grad[None, :, :L],
        own[None],
        scatter(bias_grad[0])[None],
        scatter(gain_grad[0])[None],
        scatter(shift_grad[0])[None],
    )


def solution(mesh):
    placed = (
        P("dp", None, None),
        P("dp", None, None),
        P("dp"),
        P("dp", None),
        P("section", None, None),
        P("section", None),
        P("section", None),
        P("section", None),
        P(),
    )
    return jax.shard_map(
        shards,
        mesh=mesh,
        in_specs=placed,
        out_specs=(
            P("section", "dp", None, None),
            P("section", "dp", None, None),
            P("section", "dp", None),
            P("section", "dp"),
            P("section", "dp"),
            P("section", "dp"),
        ),
        check_vma=False,
    )
```

```python
import functools

import jax
import jax.numpy as jnp
from jax import lax
from jax.experimental import pallas as pl
from jax.experimental.pallas import tpu as pltpu
from jax.sharding import PartitionSpec as P

MESH = pl.DeviceIdType.MESH
norm_epsilon = 1e-05
bf16 = jnp.bfloat16
f32 = jnp.float32


def dot(a, b):
    return lax.dot_general(a, b, (((1,), (0,)), ((), ())), preferred_element_type=f32)


def dot_cols(a, b):
    return lax.dot_general(a, b, (((1,), (1,)), ((), ())), preferred_element_type=f32)


def dot_rows(a, b):
    return lax.dot_general(a, b, (((0,), (0,)), ((), ())), preferred_element_type=f32)


def softplus(u):
    return jnp.maximum(u, 0.0) + jnp.log1p(jnp.exp(-jnp.abs(u)))


def block_mask(feature_rows, value_cols, features, head_dim):
    r = lax.broadcasted_iota(jnp.int32, (feature_rows, value_cols), 0) // features
    c = lax.broadcasted_iota(jnp.int32, (feature_rows, value_cols), 1) // head_dim
    return r == c


def chunk_columns(cfg, odd):
    D, FF = cfg[3], cfg[4]
    wide = FF // D
    first_kind = 1 + (wide - 1) * odd
    count = wide + wide * odd
    return first_kind, count


def flat(ref, c):
    return ref[:, :, c].reshape(ref.shape[0] * ref.shape[1], c.size)


def plain_gradients(cfg, odd, xin, dbr, buf_a, buf_b, g_hbm, g_sem, stage):
    D, FF = cfg[3], cfg[4]
    first_kind, count = chunk_columns(cfg, odd)
    wide = FF // D

    def column(k):
        return pl.ds(pl.multiple_of(k * D, D), D)

    def store(k):
        cp = pltpu.make_async_copy(stage, g_hbm.at[:, column(k)], g_sem.at[0])
        cp.start()
        cp.wait()

    def one(k, carry):
        @pl.when(k < first_kind)
        def _():
            src = column(k + (wide - 1) * (1 - odd))
            stage[...] = dot_rows(flat(dbr, pl.ds(0, D)), flat(buf_a, src))
            store(k)

        @pl.when(k >= first_kind)
        def _():
            stage[...] = dot_rows(flat(xin, pl.ds(0, D)), flat(buf_b, column(k - first_kind)))
            store(k)

        return carry

    lax.fori_loop(0, count, one, 0)

    @pl.when(odd == 0)
    def _():
        stage[...] = jnp.zeros_like(stage)

        def rest(k, carry):
            store(k)
            return carry

        lax.fori_loop(wide, 2 * wide, rest, 0)


def reduce_gradients(
    cfg,
    s,
    d,
    odd,
    w,
    u,
    xin,
    dbr,
    buf_a,
    buf_b,
    g_hbm,
    small_ref,
    ready,
    tx,
    td,
    keep,
    core_out,
    line_out,
    line_down,
    final,
    small_in,
    core_send,
    core_recv,
    line_send,
    up_recv,
    down_recv,
    final_sem,
    cross_send,
    cross_recv,
    small_send,
    small_recv,
):
    M, L, LP, D, FF, HD, FE, NS, ND, fscale, in_kernel = cfg
    Z = ND // 2
    B = D // ND
    R = Z * B
    wide = FF // D
    keeps = keep.shape[0]
    p = lax.rem(d, 2)
    z = d // 2
    sib = d + 1 - 2 * p
    first_kind, count = chunk_columns(cfg, odd)
    dma_to = functools.partial(pltpu.make_async_remote_copy, device_id_type=MESH)

    pl.semaphore_signal(ready.at[0], inc=1, device_id=(s, sib), device_id_type=MESH)

    @pl.when(z > 0)
    def _():
        pl.semaphore_signal(ready.at[2], inc=1, device_id=(s, d - 2), device_id_type=MESH)

    @pl.when(z < Z - 1)
    def _():
        pl.semaphore_signal(ready.at[1], inc=1, device_id=(s, d + 2), device_id_type=MESH)

    def small_copy(o):
        return dma_to(
            small_ref,
            small_in.at[d],
            small_send.at[o],
            small_recv.at[d],
            device_id=(s, lax.rem(d + o, ND)),
        )

    def small_wait(o):
        j = lax.rem(d + o, ND)
        return dma_to(
            small_ref,
            small_in.at[j],
            small_send.at[o],
            small_recv.at[j],
            device_id=(s, j),
        )

    for o in range(1, ND):
        small_copy(o).start()
    small_in[d] = small_ref[...]

    for src, dst in ((dbr, td), (xin, tx)):
        for i in range(D // 256):
            turned = flat(src, pl.ds(256 * i, 256)).T
            for q in range(8):
                t = 8 * i + q
                block = t * 32 // B
                at = block // 2 * B + t * 32 - block * B
                dst[block % 2, pl.ds(at, 32), :] = turned[32 * q : 32 * q + 32]

    def column(k):
        return pl.ds(pl.multiple_of(k * D, D), D)

    def slot(c, zt):
        r = pl.multiple_of(lax.rem(c, 2) * R + zt * B, 16)
        return (pl.ds(r, B), column(c // 2))

    def core_place(c):
        return (pl.ds(pl.multiple_of(lax.rem(c, 2) * R, 16), R), column(c // 2))

    def core_copy(c):
        return dma_to(
            core_out.at[lax.rem(c, 2)],
            w.at[core_place(c)],
            core_send.at[lax.rem(c, 2)],
            core_recv.at[c],
            device_id=(s, sib),
        )

    def up_copy(c, zt):
        return dma_to(
            line_out.at[lax.rem(c, 2), zt],
            u.at[slot(c, zt)],
            line_send.at[lax.rem(c, 2), zt],
            up_recv.at[c, zt],
            device_id=(s, d + 2),
        )

    def down_copy(c, zt):
        return dma_to(
            line_out.at[lax.rem(c, 2), zt],
            line_down.at[c, zt],
            line_send.at[lax.rem(c, 2), zt],
            down_recv.at[c, zt],
            device_id=(s, d - 2),
        )

    def place(c):
        own = c - first_kind
        early = c + 2 + (1 - odd)
        return column(jnp.where(c < first_kind, early, own))

    def own_copy(c):
        return pltpu.make_async_copy(
            final.at[lax.rem(c, 2)], g_hbm.at[:, place(c)], final_sem.at[lax.rem(c, 2)]
        )

    def cross_copy(c):
        return dma_to(
            final.at[lax.rem(c, 2)],
            g_hbm.at[:, column(c + wide)],
            cross_send.at[lax.rem(c, 2)],
            cross_recv.at[lax.rem(c, 2)],
            device_id=(s - 1, d),
        )

    crossing = 2 * odd

    def final_wait(c):
        @pl.when((c >= 0) & (c < crossing))
        def _():
            cross_copy(c).wait_send()

        @pl.when(c >= crossing)
        def _():
            own_copy(c).wait()

    def total(c, zt):
        return keep[lax.rem(c, keeps), pl.ds(zt * B, B), :] + w[slot(c, zt)].astype(f32)

    near = jnp.minimum(z, Z - 1 - z)
    far = jnp.maximum(z, Z - 1 - z)

    def step(k, carry):
        @pl.when(k < count)
        def _():
            sl = lax.rem(k, 2)

            def products(left, right):
                @pl.when(k >= 2)
                def _():
                    core_copy(k - 2).wait_send()

                core_out[sl] = dot(left[1 - p], right).astype(bf16)

                @pl.when(k == 0)
                def _():
                    pl.semaphore_wait(ready.at[0], 1)

                core_copy(k).start()
                keep[lax.rem(k, keeps)] = dot(left[p], right)

            @pl.when(k < first_kind)
            def _():
                products(td, flat(buf_a, column(k + (wide - 1) * (1 - odd))))

            @pl.when(k >= first_kind)
            def _():
                products(tx, flat(buf_b, column(k - first_kind)))

        c_near = k - 1 - near

        @pl.when((c_near >= 0) & (c_near < count))
        def _():
            core_copy(c_near).wait_recv()

        c_up = k - 1 - z

        @pl.when((c_up >= 0) & (c_up < count) & (z < Z - 1))
        def _():
            @pl.when(c_up == 0)
            def _():
                pl.semaphore_wait(ready.at[2], 1)

            for zt in range(Z - 1, 0, -1):
                @pl.when(zt > z)
                def _():
                    @pl.when(c_up >= 2)
                    def _():
                        up_copy(c_up - 2, zt).wait_send()

                    @pl.when(z > 0)
                    def _():
                        up_copy(c_up, zt).wait_recv()
                        line_out[lax.rem(c_up, 2), zt] = (
                            total(c_up, zt) + u[slot(c_up, zt)].astype(f32)
                        ).astype(bf16)

                    @pl.when(z == 0)
                    def _():
                        line_out[lax.rem(c_up, 2), zt] = total(c_up, zt).astype(bf16)

                    up_copy(c_up, zt).start()

        c_down = k - 1 - (Z - 1 - z)

        @pl.when((c_down >= 0) & (c_down < count) & (z > 0))
        def _():
            @pl.when(c_down == 0)
            def _():
                pl.semaphore_wait(ready.at[1], 1)

            for zt in range(Z - 1):
                @pl.when(zt < z)
                def _():
                    @pl.when(c_down >= 2)
                    def _():
                        down_copy(c_down - 2, zt).wait_send()

                    @pl.when(z < Z - 1)
                    def _():
                        down_copy(c_down, zt).wait_recv()
                        line_out[lax.rem(c_down, 2), zt] = (
                            total(c_down, zt) + line_down[c_down, zt].astype(f32)
                        ).astype(bf16)

                    @pl.when(z == Z - 1)
                    def _():
                        line_out[lax.rem(c_down, 2), zt] = total(c_down, zt).astype(bf16)

                    down_copy(c_down, zt).start()

        c_own = k - 1 - far

        @pl.when((c_own >= 0) & (c_own < count))
        def _():
            sl = lax.rem(c_own, 2)
            final_wait(c_own - 2)
            final[sl] = total(c_own, z)

            @pl.when(z > 0)
            def _():
                up_copy(c_own, z).wait_recv()
                final[sl] += u[slot(c_own, z)].astype(f32)

            @pl.when(z < Z - 1)
            def _():
                down_copy(c_own, z).wait_recv()
                final[sl] += line_down[c_own, z].astype(f32)

            @pl.when(c_own < crossing)
            def _():
                cross_copy(c_own).start()

            @pl.when(c_own >= crossing)
            def _():
                own_copy(c_own).start()

        return carry

    lax.fori_loop(0, count + 1 + far, step, 0)

    for back in (2, 1):
        c = count - back
        core_copy(c).wait_send()
        for zt in range(Z):
            @pl.when(zt > z)
            def _():
                up_copy(c, zt).wait_send()

            @pl.when(zt < z)
            def _():
                down_copy(c, zt).wait_send()

        own_copy(c).wait()

    @pl.when((odd == 0) & (s < NS - 1))
    def _():
        for c in range(2):
            cross_copy(c).wait_recv()

    for o in range(1, ND):
        small_wait(o).wait_recv()
        small_copy(o).wait_send()
    acc = small_in[0]
    for j in range(1, ND):
        acc = acc + small_in[j]
    small_ref[...] = acc


def pipeline_kernel(
    cfg,
    len_ref,
    x_hbm,
    cot_hbm,
    pred_ref,
    slab_hbm,
    bias_ref,
    gain_ref,
    shift_ref,
    fmap_ref,
    out_hbm,
    grad_hbm,
    g_hbm,
    small_ref,
    w,
    u,
    xin,
    out,
    dyin,
    dxo,
    dbr,
    nbuf,
    rbuf,
    buf_a,
    buf_b,
    land,
    out_stage,
    grad_stage,
    load_sem,
    x_sem,
    u_send,
    u_recv,
    f_send,
    f_recv,
    b_send,
    b_recv,
    out_sem,
    grad_sem,
    g_sem,
    *reduce_refs,
):
    M, L, LP, D, FF, HD, FE, NS, ND, fscale, in_kernel = cfg
    HALF = FF // 2
    GH = 256 // HD
    G = D // 256
    GF = GH * FE
    s = lax.axis_index("section")
    d = lax.axis_index("dp")
    odd = lax.rem(s, 2)
    is_attn = odd == 0
    is_ff = odd == 1
    first = s == 0
    last = s == NS - 1
    sib = d + 1 - 2 * lax.rem(d, 2)
    mate = d + 2 - 4 * lax.rem(d // 2, 2)
    quarter = D // 4

    barrier = pltpu.get_barrier_semaphore()

    def greet(cond, ts, td):
        @pl.when(cond)
        def _():
            pl.semaphore_signal(barrier, inc=1, device_id=(ts, td), device_id_type=MESH)

    always = s >= 0
    partners = 2
    if in_kernel:
        partners = ND - 1
        for o in range(1, ND):
            greet(always, s, lax.rem(d + o, ND))
    else:
        greet(always, s, sib)
        greet(always, s, mate)
    greet(s > 0, s - 1, d)
    greet(s < NS - 1, s + 1, d)

    w_copy = pltpu.make_async_copy(slab_hbm.at[0, :, pl.ds(0, FF)], w, load_sem.at[0])
    u_copy = pltpu.make_async_copy(
        slab_hbm.at[0, :, pl.ds(FF, HALF)], u.at[:, pl.ds(HALF, HALF)], load_sem.at[1]
    )
    w_copy.start()

    @pl.when(first)
    def _():
        for m in range(2):
            pltpu.make_async_copy(x_hbm.at[m], land.at[m], x_sem.at[m]).start()

    @pl.when(last)
    def _():
        for m in range(2):
            pltpu.make_async_copy(cot_hbm.at[m], land.at[m], x_sem.at[m]).start()

    @pl.when(is_ff)
    def _():
        u_copy.start()

    small_ref[...] = jnp.zeros_like(small_ref)
    bias_grad_ref = small_ref.at[:, pl.ds(0, FF)]
    gain_grad_ref = small_ref.at[:, pl.ds(FF, D)]
    shift_grad_ref = small_ref.at[:, pl.ds(FF + D, D)]
    pad_zero = jnp.zeros((LP - L, D), bf16)

    @pl.when(first | last)
    def _():
        pl.semaphore_wait(barrier, partners + 1)

    @pl.when((s > 0) & (s < NS - 1))
    def _():
        pl.semaphore_wait(barrier, partners + 2)

    q0 = lax.rem(d, 4)
    q_own = pl.ds(pl.multiple_of(q0 * quarter, quarter), quarter)
    q_mate = pl.ds(pl.multiple_of((q0 + 2 - 4 * (q0 // 2)) * quarter, quarter), quarter)
    left = pl.ds(0, HALF)

    def u_from_section():
        return pltpu.make_async_remote_copy(
            slab_hbm.at[0, q_own, pl.ds(FF, HALF)],
            u.at[q_own, left],
            u_send.at[0],
            u_recv.at[0],
            device_id=(s + 1, d),
            device_id_type=MESH,
        )

    def u_copy_to(rows, k, td):
        return pltpu.make_async_remote_copy(
            u.at[rows, left],
            u.at[rows, left],
            u_send.at[k],
            u_recv.at[k],
            device_id=(s, td),
            device_id_type=MESH,
        )

    @pl.when(is_attn & (s < NS - 1))
    def _():
        u_from_section().start()

    w_copy.wait()

    @pl.when(is_ff)
    def _():
        u_from_section().wait_recv()
        u_copy_to(q_own, 1, mate).start()
        u_copy_to(q_own, 2, sib).start()
        u_copy_to(q_own, 1, mate).wait_recv()
        u_copy_to(q_mate, 3, sib).start()
        u_copy_to(q_own, 2, sib).wait_recv()
        u_copy_to(q_mate, 3, sib).wait_recv()
        u_copy.wait()

    g_row = gain_ref[...]
    b_row = shift_ref[...]
    row_id = lax.broadcasted_iota(jnp.int32, (LP, GF), 0)
    head_mask = block_mask(GF, 256, FE, HD)
    pair_mask = jnp.concatenate([head_mask, head_mask], axis=1)
    ones_cols = jnp.ones((LP, 256), bf16)


    def sz_at(m, g):
        slot = m * G + g
        r = pl.multiple_of(lax.rem(slot, D // GF) * GF, GF)
        c = pl.multiple_of(slot // (D // GF) * 512, 512)
        return (pl.ds(r, GF), pl.ds(c, 512))

    def norm_forward(m, pre):
        mean = jnp.mean(pre, axis=-1, keepdims=True)
        cen = pre - mean
        r = lax.rsqrt(jnp.mean(cen * cen, axis=-1, keepdims=True) + norm_epsilon)
        n = cen * r
        nbuf[m] = n
        rbuf[m] = r
        out[m] = (n * g_row + b_row).astype(bf16)

    def norm_backward(m):
        dy = dyin[m].astype(f32)
        n = nbuf[m]
        dn = dy * g_row
        dyn = dy * n
        m1 = jnp.mean(dn, axis=-1, keepdims=True)
        m2 = jnp.mean(dn * n, axis=-1, keepdims=True)
        gain_grad_ref[...] += jnp.sum(dyn, axis=0, keepdims=True)
        shift_grad_ref[...] += jnp.sum(dy, axis=0, keepdims=True)
        dpre = rbuf[m] * (dn - m1 - n * m2)
        dbr[m] = dpre.astype(bf16)
        return dpre

    def attend_forward(m):
        x = xin[m]
        valid = row_id < len_ref[m]
        for g in range(G):
            cols = [pl.ds(k * D + 256 * g, 256) for k in range(3)]
            qkv = [
                (dot(x, w[:, c]) + bias_ref[:, c]).astype(bf16) for c in cols
            ]
            fq = softplus(dot(qkv[0], fmap_ref[g]) * fscale).astype(bf16)
            fk = softplus(dot(qkv[1], fmap_ref[g]) * fscale)
            fk = jnp.where(valid, fk, 0.0).astype(bf16)
            buf_a[m, :, pl.ds(256 * g, 256)] = qkv[2]
            buf_a[m, :, pl.ds(D + GF * g, GF)] = fq
            buf_a[m, :, pl.ds(D + GF * (G + g), GF)] = fk
            sz = dot_rows(fk, jnp.concatenate([qkv[2], ones_cols], axis=1))
            sz = jnp.where(pair_mask, sz, 0.0).astype(bf16)
            u[sz_at(m, g)] = sz
            nd = dot(fq, sz)
            buf_a[m, :, pl.ds(3 * D + 256 * g, 256)] = (nd[:, :256] / nd[:, 256:]).astype(bf16)
        branch = dot_cols(buf_a[m, :, pl.ds(3 * D, D)], w[:, pl.ds(3 * D, D)])
        norm_forward(m, x.astype(f32) + (branch + bias_ref[:, pl.ds(3 * D, D)]))

    def feed_forward(m):
        x = xin[m]
        tile = 512
        for j in range(FF // tile):
            c = pl.ds(j * tile, tile)
            a = dot(x, w[:, c]) + bias_ref[:, c]
            cdf = 0.5 + 0.5 * lax.erf(a * 0.7071067811865476)
            pdf = jnp.exp(a * a * -0.5) * 0.3989422804014327
            buf_a[m, :, c] = (a * cdf).astype(bf16)
            buf_b[m, :, c] = (cdf + a * pdf).astype(bf16)
        branch = dot_cols(buf_a[m], u[...])
        norm_forward(m, x.astype(f32) + branch)

    def attend_backward(m):
        dpre = norm_backward(m)
        db = dbr[m]
        valid = row_id < len_ref[m]
        ocols = pl.ds(3 * D, D)
        bias_grad_ref[:, ocols] += jnp.sum(db.astype(f32), axis=0, keepdims=True)
        for g in range(G):
            dmix = dot(db, w[:, pl.ds(3 * D + 256 * g, 256)])
            v = buf_a[m, :, pl.ds(256 * g, 256)]
            fq = buf_a[m, :, pl.ds(D + GF * g, GF)]
            fk = buf_a[m, :, pl.ds(D + GF * (G + g), GF)]
            sz = u[sz_at(m, g)]
            nd = dot(fq, sz)
            rden = 1.0 / nd[:, 256:]
            dnum = dmix * rden
            dden = -dnum * (nd[:, :256] * rden)
            de = jnp.concatenate([dnum, dden], axis=1).astype(bf16)
            dfq = dot_cols(de, sz)
            dsz = jnp.where(pair_mask, dot_rows(fq, de), 0.0).astype(bf16)
            dfk = dot_cols(jnp.concatenate([v, ones_cols], axis=1), dsz)
            dv = dot(fk, dsz[:, :256]).astype(bf16)
            duq = dfq * (1.0 - jnp.exp(-fq.astype(f32)))
            duk = jnp.where(valid, dfk, 0.0) * (1.0 - jnp.exp(-fk.astype(f32)))
            dq = (dot_cols(duq.astype(bf16), fmap_ref[g]) * fscale).astype(bf16)
            dk = (dot_cols(duk.astype(bf16), fmap_ref[g]) * fscale).astype(bf16)
            for k, val in enumerate((dq, dk, dv)):
                c = pl.ds(k * D + 256 * g, 256)
                buf_b[m, :, c] = val
                bias_grad_ref[:, c] += jnp.sum(val.astype(f32), axis=0, keepdims=True)
        dx = dpre + dot_cols(buf_b[m, :, pl.ds(0, 3 * D)], w[:, pl.ds(0, 3 * D)])
        dxo[m] = dx.astype(bf16)

    def feed_backward(m):
        dpre = norm_backward(m)
        db = dbr[m]
        tile = 512
        for j in range(FF // tile):
            c = pl.ds(j * tile, tile)
            da = (dot(db, u[:, c]) * buf_b[m, :, c].astype(f32)).astype(bf16)
            buf_b[m, :, c] = da
            bias_grad_ref[:, c] += jnp.sum(da.astype(f32), axis=0, keepdims=True)
        dx = dpre + dot_cols(buf_b[m], w[...])
        dxo[m] = dx.astype(bf16)

    def next_copy(m):
        return pltpu.make_async_remote_copy(
            out.at[m],
            xin.at[m],
            f_send.at[m],
            f_recv.at[m],
            device_id=(s + 1, d),
            device_id_type=MESH,
        )

    def back_copy(m):
        return pltpu.make_async_remote_copy(
            dxo.at[m],
            dyin.at[m],
            b_send.at[m],
            b_recv.at[m],
            device_id=(s - 1, d),
            device_id_type=MESH,
        )

    def out_copy(m):
        sl = lax.rem(m, 2)
        return pltpu.make_async_copy(out_stage.at[sl], out_hbm.at[m], out_sem.at[sl])

    def grad_copy(m):
        sl = lax.rem(m, 2)
        return pltpu.make_async_copy(grad_stage.at[sl], grad_hbm.at[m], grad_sem.at[sl])

    def land_copy(ref, m):
        sl = lax.rem(m, 2)
        return pltpu.make_async_copy(ref.at[m], land.at[sl], x_sem.at[sl])

    def write_out(copy, rows, staged, m):
        @pl.when(m >= 2)
        def _():
            copy(m - 2).wait()

        staged[lax.rem(m, 2)] = rows[m, pl.ds(0, L), :]
        copy(m).start()

    eye = lax.broadcasted_iota(jnp.int32, (L, L), 0) == lax.broadcasted_iota(jnp.int32, (L, L), 1)

    def forward_step(m):
        @pl.when(first)
        def _():
            land_copy(x_hbm, m).wait()
            xin[m] = jnp.concatenate([land[lax.rem(m, 2)], pad_zero], axis=0)

            @pl.when(m + 2 < M)
            def _():
                land_copy(x_hbm, m + 2).start()

        @pl.when(s > 0)
        def _():
            next_copy(m).wait_recv()

        @pl.when(is_attn)
        def _():
            attend_forward(m)

        @pl.when(is_ff)
        def _():
            feed_forward(m)

        @pl.when(s < NS - 1)
        def _():
            next_copy(m).start()

        write_out(out_copy, out, out_stage, m)

    def backward_step(m):
        @pl.when(last)
        def _():
            land_copy(cot_hbm, m).wait()
            row = jnp.where(
                lax.broadcasted_iota(jnp.int32, (1, L), 1) < len_ref[m],
                pred_ref[pl.ds(m, 1), :].astype(f32),
                0.0,
            )
            col = jnp.sum(jnp.where(eye, row, 0.0), axis=1, keepdims=True)
            masked = (land[lax.rem(m, 2)].astype(f32) * col).astype(bf16)
            dyin[m] = jnp.concatenate([masked, pad_zero], axis=0)

            @pl.when(m + 2 < M)
            def _():
                land_copy(cot_hbm, m + 2).start()

        @pl.when(s < NS - 1)
        def _():
            back_copy(m).wait_recv()

        @pl.when(is_attn)
        def _():
            attend_backward(m)

        @pl.when(is_ff)
        def _():
            feed_backward(m)

        @pl.when(s > 0)
        def _():
            back_copy(m).start()

        write_out(grad_copy, dxo, grad_stage, m)

    back_start = 6 - (s * s) // 3

    def tick(t, carry):
        mf = t - s
        mb = t - back_start

        @pl.when((mf >= 0) & (mf < M))
        def _():
            forward_step(mf)

        @pl.when((mb >= 0) & (mb < M))
        def _():
            backward_step(mb)

        return carry

    lax.fori_loop(0, 6 + M, tick, 0)

    @pl.when(is_ff)
    def _():
        u_copy_to(q_own, 1, mate).wait_send()
        u_copy_to(q_own, 2, sib).wait_send()
        u_copy_to(q_mate, 3, sib).wait_send()

    if in_kernel:
        reduce_gradients(
            cfg, s, d, odd, w, u, xin, dbr, buf_a, buf_b, g_hbm, small_ref, *reduce_refs
        )
    else:
        plain_gradients(cfg, odd, xin, dbr, buf_a, buf_b, g_hbm, g_sem, *reduce_refs)

    @pl.when(is_attn & (s < NS - 1))
    def _():
        u_from_section().wait_send()

    for m in range(M):
        @pl.when(s < NS - 1)
        def _():
            next_copy(m).wait_send()

        @pl.when(s > 0)
        def _():
            back_copy(m).wait_send()

    for m in range(M - 2, M):
        out_copy(m).wait()
        grad_copy(m).wait()


def shards(
    block_input, cotangent, lengths, predicted, slab, in_bias, norm_gain, norm_bias, feature_draws
):
    NS = lax.axis_size("section")
    ND = lax.axis_size("dp")
    M, L, D = block_input.shape
    FF = in_bias.shape[1]
    H, HD, FE = feature_draws.shape
    LP = (L + 15) // 16 * 16
    GH = 256 // HD
    G = D // 256
    GF = GH * FE
    fscale = float((3.0 / (20.0 * HD)) ** 0.5)
    draws = feature_draws.astype(bf16).reshape(G, GH, HD, FE)
    same = jnp.eye(GH, dtype=bf16)
    fmap = (draws[:, :, :, None, :] * same[None, :, None, :, None]).reshape(G, GH * HD, GF)
    in_kernel = D // ND % 32 == 0
    cfg = (M, L, LP, D, FF, HD, FE, NS, ND, fscale, in_kernel)
    hbm = pl.BlockSpec(memory_space=pl.ANY)
    vmem = pl.BlockSpec(memory_space=pltpu.VMEM)
    smem = pl.BlockSpec(memory_space=pltpu.SMEM)
    dma = pltpu.SemaphoreType.DMA
    rows_bf = pltpu.VMEM((M, LP, D), bf16)
    wide_bf = pltpu.VMEM((M, LP, FF), bf16)
    small_size = FF + 2 * D
    scratch = [
        pltpu.VMEM((D, FF), bf16),
        pltpu.VMEM((D, FF), bf16),
        rows_bf,
        rows_bf,
        rows_bf,
        rows_bf,
        rows_bf,
        pltpu.VMEM((M, LP, D), f32),
        pltpu.VMEM((M, LP, 1), f32),
        wide_bf,
        wide_bf,
        pltpu.VMEM((2, L, D), bf16),
        pltpu.VMEM((2, L, D), bf16),
        pltpu.VMEM((2, L, D), bf16),
        dma((2,)),
        dma((2,)),
        dma((4,)),
        dma((4,)),
        dma((M,)),
        dma((M,)),
        dma((M,)),
        dma((M,)),
        dma((2,)),
        dma((2,)),
        dma((1,)),
    ]
    if in_kernel:
        Z, B, chunks = ND // 2, D // ND, 2 * FF // D
        scratch += [
            pltpu.SemaphoreType.REGULAR((3,)),
            pltpu.VMEM((2, Z * B, M * LP), bf16),
            pltpu.VMEM((2, Z * B, M * LP), bf16),
            pltpu.VMEM((Z + 1, Z * B, D), f32),
            pltpu.VMEM((2, Z * B, D), bf16),
            pltpu.VMEM((2, Z, B, D), bf16),
            pltpu.VMEM((chunks, Z, B, D), bf16),
            pltpu.VMEM((2, B, D), f32),
            pltpu.VMEM((ND, 1, small_size), f32),
            dma((2,)),
            dma((chunks,)),
            dma((2, Z)),
            dma((chunks, Z)),
            dma((chunks, Z)),
            dma((2,)),
            dma((2,)),
            dma((2,)),
            dma((ND,)),
            dma((ND,)),
        ]
        g_shape = (B, FF + FF // 2)
    else:
        scratch += [pltpu.VMEM((D, D), f32)]
        g_shape = (D, 2 * FF)
    section_out, section_grad, grads, small = pl.pallas_call(
        functools.partial(pipeline_kernel, cfg),
        out_shape=[
            jax.ShapeDtypeStruct((M, L, D), bf16),
            jax.ShapeDtypeStruct((M, L, D), bf16),
            jax.ShapeDtypeStruct(g_shape, f32),
            jax.ShapeDtypeStruct((1, small_size), f32),
        ],
        in_specs=[smem, hbm, hbm, vmem, hbm, vmem, vmem, vmem, vmem],
        out_specs=[hbm, hbm, hbm, vmem],
        scratch_shapes=scratch,
        compiler_params=pltpu.CompilerParams(
            collective_id=0, has_side_effects=True, vmem_limit_bytes=60 * 2**20
        ),
        name="pipeline",
    )(
        lengths,
        block_input,
        cotangent,
        predicted,
        slab,
        in_bias,
        norm_gain,
        norm_bias,
        fmap,
    )
    parts = [small[0, :FF], small[0, FF : FF + D], small[0, FF + D :]]
    if in_kernel:
        own = grads
        d = lax.axis_index("dp")
        parts = [lax.dynamic_slice_in_dim(v, d * (v.size // ND), v.size // ND) for v in parts]
    else:
        def scatter(value):
            return lax.psum_scatter(value, "dp", scatter_dimension=0, tiled=True)

        HALF = FF // 2
        both = scatter(grads)
        parts = [scatter(v) for v in parts]
        is_attention = lax.axis_index("section") % 2 == 0
        turned = jnp.where(
            is_attention,
            jnp.concatenate([both[:, D:FF], both[:, :D], both[:, FF:]], axis=1),
            jnp.concatenate([both[:, FF:], both[:, :FF]], axis=1),
        )
        pairs = [(i, i - 1) for i in range(1, NS, 2)]
        arrived = lax.ppermute(turned[:, FF : FF + HALF], "section", pairs)
        rest = jnp.where(is_attention, arrived, turned[:, FF + HALF :])
        own = jnp.concatenate([turned[:, :FF], rest], axis=1)
    return (
        section_out[None],
        section_grad[None],
        own[None],
        parts[0][None],
        parts[1][None],
        parts[2][None],
    )


def solution(mesh):
    placed = (
        P("dp", None, None),
        P("dp", None, None),
        P("dp"),
        P("dp", None),
        P("section", None, None),
        P("section", None),
        P("section", None),
        P("section", None),
        P(),
    )
    return jax.shard_map(
        shards,
        mesh=mesh,
        in_specs=placed,
        out_specs=(
            P("section", "dp", None, None),
            P("section", "dp", None, None),
            P("section", "dp", None),
            P("section", "dp"),
            P("section", "dp"),
            P("section", "dp"),
        ),
        check_vma=False,
    )
```

```python
import functools

import jax
import jax.numpy as jnp
from jax import lax
from jax.experimental import pallas as pl
from jax.experimental.pallas import tpu as pltpu
from jax.sharding import PartitionSpec as P

MESH = pl.DeviceIdType.MESH
RELAYED = (0, 3)
SPLIT = (-1, -1)
norm_epsilon = 1e-05
bf16 = jnp.bfloat16
f32 = jnp.float32


def dot(a, b):
    return lax.dot_general(a, b, (((1,), (0,)), ((), ())), preferred_element_type=f32)


def dot_cols(a, b):
    return lax.dot_general(a, b, (((1,), (1,)), ((), ())), preferred_element_type=f32)


def dot_rows(a, b):
    return lax.dot_general(a, b, (((0,), (0,)), ((), ())), preferred_element_type=f32)


def softplus(u):
    return jnp.maximum(u, 0.0) + jnp.log1p(jnp.exp(-jnp.abs(u)))


def block_mask(feature_rows, value_cols, features, head_dim):
    r = lax.broadcasted_iota(jnp.int32, (feature_rows, value_cols), 0) // features
    c = lax.broadcasted_iota(jnp.int32, (feature_rows, value_cols), 1) // head_dim
    return r == c


def flat(ref, c):
    return ref[:, :, c].reshape(ref.shape[0] * ref.shape[1], c.size)


def column(k, D):
    return pl.ds(pl.multiple_of(k * D, D), D)


def chunk_counts(cfg, odd):
    D, FF = cfg[3], cfg[4]
    wide = FF // D
    return 1 + (wide - 1) * odd, wide + wide * odd


def plain_gradients(cfg, odd, xin, dbr, buf_a, buf_b, g_hbm, g_sem, stage):
    D, FF = cfg[3], cfg[4]
    first_kind, count = chunk_counts(cfg, odd)
    wide = FF // D

    def store(k):
        cp = pltpu.make_async_copy(stage, g_hbm.at[:, column(k, D)], g_sem.at[0])
        cp.start()
        cp.wait()

    def one(k, carry):
        @pl.when(k < first_kind)
        def _():
            src = column(k + (wide - 1) * (1 - odd), D)
            stage[...] = dot_rows(flat(dbr, pl.ds(0, D)), flat(buf_a, src))
            store(k)

        @pl.when(k >= first_kind)
        def _():
            stage[...] = dot_rows(flat(xin, pl.ds(0, D)), flat(buf_b, column(k - first_kind, D)))
            store(k)

        return carry

    lax.fori_loop(0, count, one, 0)

    @pl.when(odd == 0)
    def _():
        stage[...] = jnp.zeros_like(stage)

        def rest(k, carry):
            store(k)
            return carry

        lax.fori_loop(wide, 2 * wide, rest, 0)


def reduce_gradients(
    cfg,
    s,
    d,
    odd,
    w,
    u,
    wt,
    ut,
    xin,
    dbr,
    buf_a,
    buf_b,
    g_hbm,
    small_ref,
    small_outs,
    ready,
    keep,
    core_out,
    cross_out,
    line_out,
    final,
    small_in,
    core_send,
    core_recv,
    line_send,
    up_recv,
    down_recv,
    final_sem,
    cross_send,
    cross_recv,
    away_send,
    away_recv,
    small_send,
    small_recv,
):
    M, L, LP, D, FF, HD, FE, NS, ND, fscale, in_kernel = cfg
    Z = ND // 2
    B = D // ND
    R = Z * B
    K = M * LP
    wide = FF // D
    keeps = keep.shape[0]
    p = lax.rem(d, 2)
    z = d // 2
    sib = d + 1 - 2 * p
    first_kind, count = chunk_counts(cfg, odd)
    cross = wide // 2
    pre = jnp.where(s == 1, cross, 0)
    came = jnp.where(s == 2, cross, 0)
    lines = count - pre + came
    dma_to = functools.partial(pltpu.make_async_remote_copy, device_id_type=MESH)

    pl.semaphore_signal(ready.at[0], inc=1, device_id=(s, sib), device_id_type=MESH)

    @pl.when(z > 0)
    def _():
        pl.semaphore_signal(ready.at[2], inc=1, device_id=(s, d - 2), device_id_type=MESH)

    @pl.when(z < Z - 1)
    def _():
        pl.semaphore_signal(ready.at[1], inc=1, device_id=(s, d + 2), device_id_type=MESH)

    def small_copy(o):
        return dma_to(
            small_ref,
            small_in.at[d],
            small_send.at[o],
            small_recv.at[d],
            device_id=(s, lax.rem(d + o, ND)),
        )

    def small_wait(o):
        j = lax.rem(d + o, ND)
        return dma_to(
            small_ref, small_in.at[j], small_send.at[o], small_recv.at[j], device_id=(s, j)
        )

    for o in range(1, ND):
        small_copy(o).start()
    small_in[d] = small_ref[...]

    place_d = pl.ds(0, K)
    place_x = pl.ds((K + 127) // 128 * 128, K)
    for src, at_cols in ((dbr, place_d), (xin, place_x)):
        for i in range(D // 256):
            turned = flat(src, pl.ds(256 * i, 256)).T
            for q in range(8):
                t = 8 * i + q
                block = t * 32 // B
                at = block % 2 * R + block // 2 * B + t * 32 - block * B
                u[pl.ds(at, 32), at_cols] = turned[32 * q : 32 * q + 32]

    def slot(j):
        return (pl.ds(pl.multiple_of(lax.rem(j, 2) * R, 16), R), column(j // 2, D))

    def slot_block(j, zt):
        r = pl.multiple_of(lax.rem(j, 2) * R + zt * B, 16)
        return (pl.ds(r, B), column(j // 2, D))

    def line_place(n, zt):
        return (pl.ds(pl.multiple_of(n * R + zt * B, 16), B), pl.ds(0, D))

    def cross_place(c):
        return (pl.ds(pl.multiple_of((2 * wide - cross + c) * R, 16), R), pl.ds(0, D))

    def core_copy(j):
        return dma_to(
            core_out.at[lax.rem(j, 2)],
            w.at[slot(j)],
            core_send.at[lax.rem(j, 2)],
            core_recv.at[j],
            device_id=(s, sib),
        )

    def cross_copy(c):
        return dma_to(
            cross_out.at[c],
            ut.at[cross_place(c)],
            cross_send.at[c],
            cross_recv.at[c],
            device_id=(2, d),
        )

    def up_copy(n, zt):
        return dma_to(
            line_out.at[lax.rem(n, 2), zt],
            ut.at[line_place(n, zt)],
            line_send.at[lax.rem(n, 2), zt],
            up_recv.at[n, zt],
            device_id=(s, d + 2),
        )

    def down_copy(n, zt):
        return dma_to(
            line_out.at[lax.rem(n, 2), zt],
            wt.at[line_place(n, zt)],
            line_send.at[lax.rem(n, 2), zt],
            down_recv.at[n, zt],
            device_id=(s, d - 2),
        )

    def final_copy(n):
        j = n + pre
        early = j + cross * odd + (wide - 1) * (1 - odd)
        at = jnp.where(j < first_kind, early, j - first_kind)
        return pltpu.make_async_copy(
            final.at[lax.rem(n, 2)], g_hbm.at[:, column(at, D)], final_sem.at[lax.rem(n, 2)]
        )

    def away(n):
        return ((s == 3) & (n < cross)) | ((s == 2) & (n >= count))

    def away_copy(n):
        c = lax.rem(n, 2)
        return dma_to(
            final.at[c],
            g_hbm.at[:, column(wide + c, D)],
            away_send.at[c],
            away_recv.at[c],
            device_id=(jnp.where(s == 3, 2, 0), d),
        )

    def final_wait(n):
        @pl.when(away(n))
        def _():
            away_copy(n).wait_send()

        @pl.when(jnp.logical_not(away(n)))
        def _():
            final_copy(n).wait()

    def total(n, zt):
        j = n + pre
        return keep[lax.rem(j, keeps), pl.ds(zt * B, B), :] + w[slot_block(j, zt)].astype(f32)

    near = jnp.minimum(z, Z - 1 - z)
    far = jnp.maximum(z, Z - 1 - z)

    def step(lo, hi, k, carry):
        @pl.when(k < count)
        def _():
            sl = lax.rem(k, 2)

            def products(place, right):
                @pl.when(k >= 2)
                def _():
                    core_copy(k - 2).wait_send()

                theirs = pl.ds(pl.multiple_of((1 - p) * R, 16), R)
                mine = pl.ds(pl.multiple_of(p * R, 16), R)
                core_out[sl] = dot(u[theirs, place], right).astype(bf16)

                @pl.when(k == 0)
                def _():
                    pl.semaphore_wait(ready.at[0], 1)

                core_copy(k).start()
                keep[lax.rem(k, keeps)] = dot(u[mine, place], right)

            @pl.when(k < first_kind)
            def _():
                products(place_d, flat(buf_a, column(k + (wide - 1) * (1 - odd), D)))

            @pl.when(k >= first_kind)
            def _():
                products(place_x, flat(buf_b, column(k - first_kind, D)))

        @pl.when((lo >= count) & (k < count + came))
        def _():
            c = k - count
            cross_copy(c).wait_recv()
            keep[lax.rem(k, keeps)] = ut[cross_place(c)].astype(f32)
            w[slot(k)] = jnp.zeros((R, D), bf16)

        c_cross = k - 1

        @pl.when((c_cross >= 0) & (c_cross < pre))
        def _():
            core_copy(c_cross).wait_recv()
            both = keep[lax.rem(c_cross, keeps)] + w[slot(c_cross)].astype(f32)
            cross_out[c_cross] = both.astype(bf16)
            cross_copy(c_cross).start()

        n_near = k - 1 - pre - near

        @pl.when((n_near >= lo) & (n_near < hi) & (n_near + pre < count))
        def _():
            core_copy(n_near + pre).wait_recv()

        n_up = k - 1 - pre - z

        @pl.when((n_up >= lo) & (n_up < hi) & (z < Z - 1))
        def _():
            @pl.when(n_up == 0)
            def _():
                pl.semaphore_wait(ready.at[2], 1)

            for zt in range(Z - 1, 0, -1):
                @pl.when(zt > z)
                def _():
                    @pl.when(n_up >= 2)
                    def _():
                        up_copy(n_up - 2, zt).wait_send()

                    @pl.when(z > 0)
                    def _():
                        up_copy(n_up, zt).wait_recv()
                        line_out[lax.rem(n_up, 2), zt] = (
                            total(n_up, zt) + ut[line_place(n_up, zt)].astype(f32)
                        ).astype(bf16)

                    @pl.when(z == 0)
                    def _():
                        line_out[lax.rem(n_up, 2), zt] = total(n_up, zt).astype(bf16)

                    up_copy(n_up, zt).start()

        n_down = k - 1 - pre - (Z - 1 - z)

        @pl.when((n_down >= lo) & (n_down < hi) & (z > 0))
        def _():
            @pl.when(n_down == 0)
            def _():
                pl.semaphore_wait(ready.at[1], 1)

            for zt in range(Z - 1):
                @pl.when(zt < z)
                def _():
                    @pl.when(n_down >= 2)
                    def _():
                        down_copy(n_down - 2, zt).wait_send()

                    @pl.when(z < Z - 1)
                    def _():
                        down_copy(n_down, zt).wait_recv()
                        line_out[lax.rem(n_down, 2), zt] = (
                            total(n_down, zt) + wt[line_place(n_down, zt)].astype(f32)
                        ).astype(bf16)

                    @pl.when(z == Z - 1)
                    def _():
                        line_out[lax.rem(n_down, 2), zt] = total(n_down, zt).astype(bf16)

                    down_copy(n_down, zt).start()

        n_own = k - 1 - pre - far

        @pl.when((n_own >= lo) & (n_own < hi))
        def _():
            sl = lax.rem(n_own, 2)

            @pl.when(n_own >= 2)
            def _():
                final_wait(n_own - 2)

            final[sl] = total(n_own, z)

            @pl.when(z > 0)
            def _():
                up_copy(n_own, z).wait_recv()
                final[sl] += ut[line_place(n_own, z)].astype(f32)

            @pl.when(z < Z - 1)
            def _():
                down_copy(n_own, z).wait_recv()
                final[sl] += wt[line_place(n_own, z)].astype(f32)

            @pl.when(away(n_own))
            def _():
                away_copy(n_own).start()

            @pl.when(jnp.logical_not(away(n_own)))
            def _():
                final_copy(n_own).start()

        return carry

    own_lines = count - pre
    lax.fori_loop(0, count + 1 + far, functools.partial(step, 0, own_lines), 0)
    later = jnp.where(s == 2, count + came + 1 + far, count)
    lax.fori_loop(count, later, functools.partial(step, count, count + came), 0)

    for back in (2, 1):
        core_copy(count - back).wait_send()
        n = lines - back
        for zt in range(Z):
            @pl.when(zt > z)
            def _():
                up_copy(n, zt).wait_send()

            @pl.when(zt < z)
            def _():
                down_copy(n, zt).wait_send()

        final_wait(n)

    @pl.when(s == 1)
    def _():
        for c in range(cross):
            cross_copy(c).wait_send()

    @pl.when(odd == 0)
    def _():
        for c in range(cross):
            away_copy(c).wait_recv()

    for o in range(1, ND):
        small_wait(o).wait_recv()
        small_copy(o).wait_send()
    acc = small_in[0]
    for j in range(1, ND):
        acc = acc + small_in[j]
    small_ref[...] = acc
    bias_out, gain_out, shift_out = small_outs
    P = FF // ND
    bias_out[...] = small_ref[:, pl.ds(pl.multiple_of(d * P, 128), P)]
    for j in range(ND):
        @pl.when(d == j)
        def _():
            gain_out[...] = acc[:, FF + B * j : FF + B * j + B]
            shift_out[...] = acc[:, FF + D + B * j : FF + D + B * j + B]


def pipeline_kernel(
    cfg,
    len_ref,
    x_hbm,
    cot_hbm,
    pred_ref,
    slab_hbm,
    bias_ref,
    gain_ref,
    shift_ref,
    draws_ref,
    out_hbm,
    grad_hbm,
    g_hbm,
    *refs,
):
    M, L, LP, D, FF, HD, FE, NS, ND, fscale, in_kernel = cfg
    small_outs = refs[:3] if in_kernel else ()
    small_ref = refs[3] if in_kernel else refs[0]
    fmap_ref = refs[4] if in_kernel else refs[1]
    (
        w,
        u,
        wt,
        ut,
        xin,
        out,
        dyin,
        dxo,
        dbr,
        nbuf,
        rbuf,
        buf_a,
        buf_b,
        land,
        out_stage,
        grad_stage,
        load_sem,
        x_sem,
        u_send,
        u_recv,
        f_send,
        f_recv,
        b_send,
        b_recv,
        stage_sem,
        g_sem,
        *reduce_refs,
    ) = refs[5:] if in_kernel else refs[2:]
    HALF = FF // 2
    GH = 256 // HD
    G = D // 256
    GF = GH * FE
    top = (LP // 2 + 15) // 16 * 16
    halves = (pl.ds(0, top), pl.ds(top, LP - top))
    whole = pl.ds(0, LP)
    relay_lo, relay_hi = RELAYED if NS == 4 else (0, 0)
    relayed = relay_hi - relay_lo
    s = lax.axis_index("section")
    d = lax.axis_index("dp")
    odd = lax.rem(s, 2)
    is_attn = odd == 0
    is_ff = odd == 1
    first = s == 0
    last = s == NS - 1
    sib = d + 1 - 2 * lax.rem(d, 2)
    mate = d + 2 - 4 * lax.rem(d // 2, 2)
    quarter = D // 4
    pieces = 3
    piece = quarter // pieces

    barrier = pltpu.get_barrier_semaphore()

    def greet(cond, ts, td):
        @pl.when(cond)
        def _():
            pl.semaphore_signal(barrier, inc=1, device_id=(ts, td), device_id_type=MESH)

    always = s >= 0
    partners = 2
    if in_kernel:
        partners = ND - 1
        for o in range(1, ND):
            greet(always, s, lax.rem(d + o, ND))
    else:
        greet(always, s, sib)
        greet(always, s, mate)
    greet(s > 0, s - 1, d)
    greet(s < NS - 1, s + 1, d)
    if relayed > 0 or in_kernel:
        greet(s == 0, 2, d)
        greet(s == 2, 0, d)
        extra = jnp.where(lax.rem(s, 2) == 0, 1, 0)
    else:
        extra = 0

    w_copy = pltpu.make_async_copy(slab_hbm.at[0, :, pl.ds(0, FF)], w, load_sem.at[0])
    u_copy = pltpu.make_async_copy(
        slab_hbm.at[0, :, pl.ds(FF, HALF)], u.at[:, pl.ds(HALF, HALF)], load_sem.at[1]
    )
    w_copy.start()

    def land_copy(ref, m):
        sl = lax.rem(m, 2)
        return pltpu.make_async_copy(ref.at[m], land.at[sl], x_sem.at[sl])

    @pl.when(first)
    def _():
        for m in range(2):
            land_copy(x_hbm, m).start()

    @pl.when(last)
    def _():
        for m in range(2):
            land_copy(cot_hbm, m).start()

    @pl.when(is_ff)
    def _():
        u_copy.start()

    small_ref[...] = jnp.zeros_like(small_ref)
    bias_grad_ref = small_ref.at[:, pl.ds(0, FF)]
    gain_grad_ref = small_ref.at[:, pl.ds(FF, D)]
    shift_grad_ref = small_ref.at[:, pl.ds(FF + D, D)]

    @pl.when(first | last)
    def _():
        pl.semaphore_wait(barrier, partners + 1 + extra)

    @pl.when((s > 0) & (s < NS - 1))
    def _():
        pl.semaphore_wait(barrier, partners + 2 + extra)

    q0 = lax.rem(d, 4)
    q1 = q0 + 2 - 4 * (q0 // 2)
    left = pl.ds(0, HALF)

    def u_rows(q, i):
        return pl.ds(pl.multiple_of(q * quarter + i * piece, piece), piece)

    def u_from_section(i):
        return pltpu.make_async_remote_copy(
            slab_hbm.at[0, u_rows(q0, i), pl.ds(FF, HALF)],
            u.at[u_rows(q0, i), left],
            u_send.at[0, i],
            u_recv.at[0, i],
            device_id=(s + 1, d),
            device_id_type=MESH,
        )

    def u_copy_to(q, i, k, to):
        return pltpu.make_async_remote_copy(
            u.at[u_rows(q, i), left],
            u.at[u_rows(q, i), left],
            u_send.at[k, i],
            u_recv.at[k, i],
            device_id=(s, to),
            device_id_type=MESH,
        )

    @pl.when(is_attn & (s < NS - 1))
    def _():
        for i in range(pieces):
            u_from_section(i).start()

    def turn(src, dst, start, count):
        for i in range(start, start + count):
            dst[pl.ds(256 * i, 256), :] = src[:, pl.ds(256 * i, 256)].T

    w_copy.wait()
    late_turn = first

    @pl.when(is_attn)
    def _():
        turn(w, wt, 3 * D // 256, D // 256)
        f_row = lax.broadcasted_iota(jnp.int32, (FE, GF), 0)
        f_col = lax.broadcasted_iota(jnp.int32, (FE, GF), 1)
        for n in range(G * GH):
            shift = jnp.where(f_col == f_row + n % GH * FE, 1.0, 0.0).astype(bf16)
            spread = dot(draws_ref[n].astype(f32).astype(bf16), shift)
            fmap_ref[n // GH, pl.ds(n % GH * HD, HD), :] = spread.astype(bf16)

    @pl.when(s == 2)
    def _():
        turn(w, wt, 0, 3 * D // 256)

    @pl.when(is_ff)
    def _():
        turn(w, wt, 0, FF // 256)
        u_copy.wait()
        turn(u, ut, HALF // 256, HALF // 256)
        for i in range(pieces):
            u_from_section(i).wait_recv()
            u_copy_to(q0, i, 1, mate).start()
            u_copy_to(q0, i, 2, sib).start()
            if i > 0:
                u_copy_to(q0, i - 1, 1, mate).wait_recv()
                u_copy_to(q1, i - 1, 3, sib).start()
        u_copy_to(q0, pieces - 1, 1, mate).wait_recv()
        u_copy_to(q1, pieces - 1, 3, sib).start()
        for i in range(pieces):
            u_copy_to(q0, i, 2, sib).wait_recv()
            u_copy_to(q1, i, 3, sib).wait_recv()
        turn(u, ut, 0, HALF // 256)

    g_row = gain_ref[...]
    b_row = shift_ref[...]
    head_mask = block_mask(GF, 256, FE, HD)
    pair_mask = jnp.concatenate([head_mask, head_mask], axis=1)

    def sz_at(m, g):
        n = m * G + g
        r = pl.multiple_of(lax.rem(n, D // GF) * GF, GF)
        c = pl.multiple_of(n // (D // GF) * 512, 512)
        return (pl.ds(r, GF), pl.ds(c, 512))

    def valid_rows(m, rows):
        at = lax.broadcasted_iota(jnp.int32, (rows.size, GF), 0) + rows.start
        return at < len_ref[m]

    def with_ones(v):
        return jnp.concatenate([v, jnp.ones(v.shape, bf16)], axis=1)

    def norm_forward(m, rows, pre):
        mean = jnp.mean(pre, axis=-1, keepdims=True)
        cen = pre - mean
        r = lax.rsqrt(jnp.mean(cen * cen, axis=-1, keepdims=True) + norm_epsilon)
        n = cen * r
        nbuf[m, rows, :] = n
        rbuf[m, rows, :] = r
        out[m, rows, :] = (n * g_row + b_row).astype(bf16)

    def norm_backward(m, rows):
        dy = dyin[m, rows, :].astype(f32)
        n = nbuf[m, rows, :]
        dn = dy * g_row
        m1 = jnp.mean(dn, axis=-1, keepdims=True)
        m2 = jnp.mean(dn * n, axis=-1, keepdims=True)
        gain_grad_ref[...] += jnp.sum(dy * n, axis=0, keepdims=True)
        shift_grad_ref[...] += jnp.sum(dy, axis=0, keepdims=True)
        dpre = rbuf[m, rows, :] * (dn - m1 - n * m2)
        dbr[m, rows, :] = dpre.astype(bf16)
        return dpre

    def next_copy(m, h):
        return pltpu.make_async_remote_copy(
            out.at[m, halves[h]],
            xin.at[m, halves[h]],
            f_send.at[m, h],
            f_recv.at[m, h],
            device_id=(s + 1, d),
            device_id_type=MESH,
        )

    def back_copy(m, h):
        return pltpu.make_async_remote_copy(
            dxo.at[m, halves[h]],
            dyin.at[m, halves[h]],
            b_send.at[m, h],
            b_recv.at[m, h],
            device_id=(s - 1, d),
            device_id_type=MESH,
        )

    def relay_at(m, h):
        start = pl.multiple_of(m * LP + halves[h].start, 16)
        return ut.at[pl.ds(start, halves[h].size)]

    def relay_in(m, h):
        return pltpu.make_async_remote_copy(
            dxo.at[m, halves[h]],
            relay_at(m, h),
            b_send.at[m, h],
            f_recv.at[m, h],
            device_id=(0, d),
            device_id_type=MESH,
        )

    def relay_on(m, h):
        return pltpu.make_async_remote_copy(
            relay_at(m, h),
            dyin.at[m, halves[h]],
            b_send.at[m, h],
            b_recv.at[m, h],
            device_id=(1, d),
            device_id_type=MESH,
        )

    def send_next(m, h):
        if h == 0:
            @pl.when(is_attn & (m == 0))
            def _():
                for i in range(pieces):
                    u_from_section(i).wait_send()

        @pl.when(s < NS - 1)
        def _():
            next_copy(m, h).start()

    def by_relay(m):
        return (s == 2) & (m >= relay_lo) & (m < relay_hi)

    def send_back(m, h):
        @pl.when((s > 0) & jnp.logical_not(by_relay(m)))
        def _():
            back_copy(m, h).start()

        @pl.when(by_relay(m))
        def _():
            relay_in(m, h).start()

    v_at = [pl.ds(256 * g, 256) for g in range(G)]
    fq_at = [pl.ds(D + GF * g, GF) for g in range(G)]
    fk_at = [pl.ds(D + GF * (G + g), GF) for g in range(G)]
    out_at = pl.ds(3 * D, D)

    def attend_features(m, rows):
        x = xin[m, rows, :]
        valid = valid_rows(m, rows)
        for g in range(G):
            qkv = [
                (dot(x, w[:, c]) + bias_ref[:, c]).astype(bf16)
                for c in (pl.ds(k * D + 256 * g, 256) for k in range(3))
            ]
            fq = softplus(dot(qkv[0], fmap_ref[g]) * fscale).astype(bf16)
            fk = softplus(dot(qkv[1], fmap_ref[g]) * fscale)
            buf_a[m, rows, v_at[g]] = qkv[2]
            buf_a[m, rows, fq_at[g]] = fq
            buf_a[m, rows, fk_at[g]] = jnp.where(valid, fk, 0.0).astype(bf16)

    def summaries(m):
        for g in range(G):
            sz = dot_rows(buf_a[m, :, fk_at[g]], with_ones(buf_a[m, :, v_at[g]]))
            u[sz_at(m, g)] = jnp.where(pair_mask, sz, 0.0).astype(bf16)

    def attend_mix(m, rows):
        for g in range(G):
            nd = dot(buf_a[m, rows, fq_at[g]], u[sz_at(m, g)])
            mixed = (nd[:, :256] / nd[:, 256:]).astype(bf16)
            buf_a[m, rows, pl.ds(3 * D + 256 * g, 256)] = mixed
        branch = dot(buf_a[m, rows, out_at], wt[out_at, :]) + bias_ref[:, out_at]
        norm_forward(m, rows, xin[m, rows, :].astype(f32) + branch)

    def attend_forward(m, mode):
        if mode == 2:
            attend_features(m, whole)
            summaries(m)
            attend_mix(m, whole)
            send_next(m, 0)
            send_next(m, 1)
            return
        attend_features(m, halves[mode])
        if mode == 1:
            summaries(m)
            for part, rows in enumerate(halves):
                attend_mix(m, rows)
                send_next(m, part)

    def feed_forward(m, mode):
        rows = (halves + (whole,))[mode]
        x = xin[m, rows, :]
        tile = 512
        for j in range(FF // tile):
            c = pl.ds(j * tile, tile)
            a = dot(x, w[:, c]) + bias_ref[:, c]
            cdf = 0.5 + 0.5 * lax.erf(a * 0.7071067811865476)
            pdf = jnp.exp(a * a * -0.5) * 0.3989422804014327
            buf_a[m, rows, c] = (a * cdf).astype(bf16)
            buf_b[m, rows, c] = (cdf + a * pdf).astype(bf16)
        branch = dot(buf_a[m, rows, :], ut[...])
        norm_forward(m, rows, x.astype(f32) + branch)
        for h in (mode,) if mode < 2 else (0, 1):
            send_next(m, h)

    def attend_backward(m, mode):
        rows = (halves + (whole,))[mode]
        dpre = norm_backward(m, rows)
        nbuf[m, rows, :] = dpre
        db = dbr[m, rows, :]
        bias_grad_ref[:, out_at] += jnp.sum(db.astype(f32), axis=0, keepdims=True)

        def store(rows, k, g, val):
            c = pl.ds(k * D + 256 * g, 256)
            buf_b[m, rows, c] = val
            bias_grad_ref[:, c] += jnp.sum(val.astype(f32), axis=0, keepdims=True)

        for g in range(G):
            dmix = dot(db, w[:, pl.ds(3 * D + 256 * g, 256)])
            fq = buf_a[m, rows, fq_at[g]]
            sz = u[sz_at(m, g)]
            nd = dot(fq, sz)
            rden = 1.0 / nd[:, 256:]
            dnum = dmix * rden
            dden = -dnum * (nd[:, :256] * rden)
            de = jnp.concatenate([dnum, dden], axis=1).astype(bf16)
            buf_b[m, rows, pl.ds(D + 512 * g, 512)] = de
            duq = dot_cols(de, sz) * (1.0 - jnp.exp(-fq.astype(f32)))
            dq = (dot_cols(duq.astype(bf16), fmap_ref[g]) * fscale).astype(bf16)
            store(rows, 0, g, dq)
        if mode == 0:
            return
        for g in range(G):
            dsz = dot_rows(buf_a[m, :, fq_at[g]], buf_b[m, :, pl.ds(D + 512 * g, 512)])
            u[sz_at(m, g)] = jnp.where(pair_mask, dsz, 0.0).astype(bf16)
        for part, rows in enumerate(halves if mode == 1 else (whole,)):
            valid = valid_rows(m, rows)
            for g in range(G):
                dsz = u[sz_at(m, g)]
                fk = buf_a[m, rows, fk_at[g]]
                dfk = dot_cols(with_ones(buf_a[m, rows, v_at[g]]), dsz)
                duk = jnp.where(valid, dfk, 0.0) * (1.0 - jnp.exp(-fk.astype(f32)))
                dk = (dot_cols(duk.astype(bf16), fmap_ref[g]) * fscale).astype(bf16)
                store(rows, 1, g, dk)
                store(rows, 2, g, dot(fk, dsz[:, :256]).astype(bf16))
            inner = pl.ds(0, 3 * D)
            dx = nbuf[m, rows, :] + dot(buf_b[m, rows, inner], wt[inner, :])
            dxo[m, rows, :] = dx.astype(bf16)
            for h in (part,) if mode == 1 else (0, 1):
                send_back(m, h)

    def feed_backward(m, mode):
        rows = (halves + (whole,))[mode]
        dpre = norm_backward(m, rows)
        db = dbr[m, rows, :]
        tile = 512
        for j in range(FF // tile):
            c = pl.ds(j * tile, tile)
            da = (dot(db, u[:, c]) * buf_b[m, rows, c].astype(f32)).astype(bf16)
            buf_b[m, rows, c] = da
            bias_grad_ref[:, c] += jnp.sum(da.astype(f32), axis=0, keepdims=True)
        dx = dpre + dot(buf_b[m, rows, :], wt[...])
        dxo[m, rows, :] = dx.astype(bf16)
        for h in (mode,) if mode < 2 else (0, 1):
            send_back(m, h)

    def out_copy(m):
        return pltpu.make_async_copy(out_stage, out_hbm.at[m], stage_sem.at[0])

    def grad_copy(m):
        return pltpu.make_async_copy(grad_stage, grad_hbm.at[m], stage_sem.at[1])

    def write_out(copy, rows, staged, m):
        @pl.when(m >= 1)
        def _():
            copy(m - 1).wait()

        staged[...] = rows[m, pl.ds(0, L), :]
        copy(m).start()

    pad_zero = jnp.zeros((LP - L, D), bf16)
    eye = lax.broadcasted_iota(jnp.int32, (L, L), 0) == lax.broadcasted_iota(jnp.int32, (L, L), 1)

    def forward_step(m, mode):
        if mode != 1:
            @pl.when(first)
            def _():
                land_copy(x_hbm, m).wait()
                xin[m] = jnp.concatenate([land[lax.rem(m, 2)], pad_zero], axis=0)

                @pl.when(m + 2 < M)
                def _():
                    land_copy(x_hbm, m + 2).start()

        @pl.when(s > 0)
        def _():
            for h in (mode,) if mode < 2 else (0, 1):
                next_copy(m, h).wait_recv()

        @pl.when(is_attn)
        def _():
            attend_forward(m, mode)

        @pl.when(is_ff)
        def _():
            feed_forward(m, mode)

        if mode > 0:
            write_out(out_copy, out, out_stage, m)
        if mode == 1:
            @pl.when(first & (m == M - 1))
            def _():
                turn(w, wt, 0, 3 * D // 256)

    def backward_step(m, mode):
        if mode != 1:
            @pl.when(last)
            def _():
                land_copy(cot_hbm, m).wait()
                row = jnp.where(
                    lax.broadcasted_iota(jnp.int32, (1, L), 1) < len_ref[m],
                    pred_ref[pl.ds(m, 1), :].astype(f32),
                    0.0,
                )
                col = jnp.sum(jnp.where(eye, row, 0.0), axis=1, keepdims=True)
                masked = (land[lax.rem(m, 2)].astype(f32) * col).astype(bf16)
                dyin[m] = jnp.concatenate([masked, pad_zero], axis=0)

                @pl.when(m + 2 < M)
                def _():
                    land_copy(cot_hbm, m + 2).start()

        @pl.when(s < NS - 1)
        def _():
            for h in (mode,) if mode < 2 else (0, 1):
                back_copy(m, h).wait_recv()

        @pl.when(is_attn)
        def _():
            attend_backward(m, mode)

        @pl.when(is_ff)
        def _():
            feed_backward(m, mode)

        if mode > 0:
            write_out(grad_copy, dxo, grad_stage, m)

    back_start = jnp.where(s == 0, 16, jnp.where(s == 1, 12, jnp.where(s == 2, 10, 6)))
    relay_start = 12

    def when_due(start, act):
        def at(t):
            i = t - start
            m = i // 2

            apart = i < 0
            for n in SPLIT:
                apart = apart | (m == n % M)
            here = (i >= 0) & (i < 2 * M)

            @pl.when(here & jnp.logical_not(apart) & (lax.rem(i, 2) == 1))
            def _():
                act(m, 2)

            for h in range(2):
                @pl.when(here & apart & (lax.rem(i, 2) == h))
                def _():
                    act(m, h)

        return at

    forward_at = when_due(2 * s, forward_step)
    backward_at = when_due(back_start, backward_step)

    def tick(t, carry):
        forward_at(t)
        if relayed > 0:
            i = t - relay_start
            for h in range(2):
                @pl.when((s == 0) & (i >= 0) & (i < 2 * relayed) & (lax.rem(i, 2) == h))
                def _():
                    relay_in(relay_lo + i // 2, h).wait_recv()
                    relay_on(relay_lo + i // 2, h).start()
        backward_at(t)
        return carry

    lax.fori_loop(0, 28, tick, 0)

    if relayed > 0:
        @pl.when(s == 0)
        def _():
            for m in range(relay_lo, relay_hi):
                for h in range(2):
                    relay_on(m, h).wait_send()

    @pl.when(is_ff)
    def _():
        for i in range(pieces):
            u_copy_to(q0, i, 1, mate).wait_send()
            u_copy_to(q0, i, 2, sib).wait_send()
            u_copy_to(q1, i, 3, sib).wait_send()

    if in_kernel:
        reduce_gradients(
            cfg,
            s,
            d,
            odd,
            w,
            u,
            wt,
            ut,
            xin,
            dbr,
            buf_a,
            buf_b,
            g_hbm,
            small_ref,
            small_outs,
            *reduce_refs,
        )
    else:
        plain_gradients(cfg, odd, xin, dbr, buf_a, buf_b, g_hbm, g_sem, *reduce_refs)

    for m in range(M):
        for h in range(2):
            @pl.when(s < NS - 1)
            def _():
                next_copy(m, h).wait_send()

            @pl.when(s > 0)
            def _():
                back_copy(m, h).wait_send()

    out_copy(M - 1).wait()
    grad_copy(M - 1).wait()


def shards(
    block_input, cotangent, lengths, predicted, slab, in_bias, norm_gain, norm_bias, feature_draws
):
    NS = lax.axis_size("section")
    ND = lax.axis_size("dp")
    M, L, D = block_input.shape
    FF = in_bias.shape[1]
    H, HD, FE = feature_draws.shape
    LP = (L + 15) // 16 * 16
    GH = 256 // HD
    G = D // 256
    GF = GH * FE
    fscale = float((3.0 / (20.0 * HD)) ** 0.5)
    in_kernel = D // ND % 32 == 0 and NS == 4
    cfg = (M, L, LP, D, FF, HD, FE, NS, ND, fscale, in_kernel)
    hbm = pl.BlockSpec(memory_space=pl.ANY)
    vmem = pl.BlockSpec(memory_space=pltpu.VMEM)
    smem = pl.BlockSpec(memory_space=pltpu.SMEM)
    dma = pltpu.SemaphoreType.DMA
    rows_bf = pltpu.VMEM((M, LP, D), bf16)
    wide_bf = pltpu.VMEM((M, LP, FF), bf16)
    small_size = FF + 2 * D
    smalls = [FF // ND, D // ND, D // ND] if in_kernel else [small_size]
    scratch = [pltpu.VMEM((1, small_size), f32)] if in_kernel else []
    scratch += [
        pltpu.VMEM((G, GH * HD, GF), bf16),
        pltpu.VMEM((D, FF), bf16),
        pltpu.VMEM((D, FF), bf16),
        pltpu.VMEM((FF, D), bf16),
        pltpu.VMEM((FF, D), bf16),
        rows_bf,
        rows_bf,
        rows_bf,
        rows_bf,
        rows_bf,
        pltpu.VMEM((M, LP, D), f32),
        pltpu.VMEM((M, LP, 1), f32),
        wide_bf,
        wide_bf,
        pltpu.VMEM((2, L, D), bf16),
        pltpu.VMEM((L, D), bf16),
        pltpu.VMEM((L, D), bf16),
        dma((2,)),
        dma((2,)),
        dma((4, 3)),
        dma((4, 3)),
        dma((M, 2)),
        dma((M, 2)),
        dma((M, 2)),
        dma((M, 2)),
        dma((2,)),
        dma((1,)),
    ]
    if in_kernel:
        Z, B, chunks = ND // 2, D // ND, 2 * FF // D
        cross = FF // D // 2
        lines = chunks
        scratch += [
            pltpu.SemaphoreType.REGULAR((3,)),
            pltpu.VMEM((Z + 1, Z * B, D), f32),
            pltpu.VMEM((2, Z * B, D), bf16),
            pltpu.VMEM((cross, Z * B, D), bf16),
            pltpu.VMEM((2, Z, B, D), bf16),
            pltpu.VMEM((2, B, D), f32),
            pltpu.VMEM((ND, 1, small_size), f32),
            dma((2,)),
            dma((chunks,)),
            dma((2, Z)),
            dma((lines, Z)),
            dma((lines, Z)),
            dma((2,)),
            dma((cross,)),
            dma((cross,)),
            dma((cross,)),
            dma((cross,)),
            dma((ND,)),
            dma((ND,)),
        ]
        g_shape = (B, FF + FF // 2)
    else:
        scratch += [pltpu.VMEM((D, D), f32)]
        g_shape = (D, 2 * FF)
    section_out, section_grad, grads, *small = pl.pallas_call(
        functools.partial(pipeline_kernel, cfg),
        out_shape=[
            jax.ShapeDtypeStruct((M, L, D), bf16),
            jax.ShapeDtypeStruct((M, L, D), bf16),
            jax.ShapeDtypeStruct(g_shape, f32),
        ]
        + [jax.ShapeDtypeStruct((1, n), f32) for n in smalls],
        in_specs=[smem, hbm, hbm, vmem, hbm, vmem, vmem, vmem, vmem],
        out_specs=[hbm, hbm, hbm] + [vmem] * len(smalls),
        scratch_shapes=scratch,
        compiler_params=pltpu.CompilerParams(
            collective_id=0, has_side_effects=True, vmem_limit_bytes=62 * 2**20
        ),
        name="pipeline",
    )(
        lengths,
        block_input,
        cotangent,
        predicted,
        slab,
        in_bias,
        norm_gain,
        norm_bias,
        feature_draws,
    )
    if in_kernel:
        own = grads
        parts = small
    else:
        def scatter(value):
            return lax.psum_scatter(value, "dp", scatter_dimension=0, tiled=True)

        HALF = FF // 2
        both = scatter(grads)
        sums = small[0][0]
        parts = [scatter(v)[None] for v in (sums[:FF], sums[FF : FF + D], sums[FF + D :])]
        is_attention = lax.axis_index("section") % 2 == 0
        turned = jnp.where(
            is_attention,
            jnp.concatenate([both[:, D:FF], both[:, :D], both[:, FF:]], axis=1),
            jnp.concatenate([both[:, FF:], both[:, :FF]], axis=1),
        )
        pairs = [(i, i - 1) for i in range(1, NS, 2)]
        arrived = lax.ppermute(turned[:, FF : FF + HALF], "section", pairs)
        rest = jnp.where(is_attention, arrived, turned[:, FF + HALF :])
        own = jnp.concatenate([turned[:, :FF], rest], axis=1)
    return (
        section_out[None],
        section_grad[None],
        own[None],
        *parts,
    )


def solution(mesh):
    placed = (
        P("dp", None, None),
        P("dp", None, None),
        P("dp"),
        P("dp", None),
        P("section", None, None),
        P("section", None),
        P("section", None),
        P("section", None),
        P(),
    )
    return jax.shard_map(
        shards,
        mesh=mesh,
        in_specs=placed,
        out_specs=(
            P("section", "dp", None, None),
            P("section", "dp", None, None),
            P("section", "dp", None),
            P("section", "dp"),
            P("section", "dp"),
            P("section", "dp"),
        ),
        check_vma=False,
    )
```

```python
import functools

import jax
import jax.numpy as jnp
from jax import lax
from jax.experimental import pallas as pl
from jax.experimental.pallas import tpu as pltpu
from jax.sharding import PartitionSpec as P

MESH = pl.DeviceIdType.MESH
CHUNK = 384
RELAYED = (0, 3)
SPLIT = (-1, -1)
norm_epsilon = 1e-05
bf16 = jnp.bfloat16
f32 = jnp.float32


def dot(a, b):
    return lax.dot_general(a, b, (((1,), (0,)), ((), ())), preferred_element_type=f32)


def dot_cols(a, b):
    return lax.dot_general(a, b, (((1,), (1,)), ((), ())), preferred_element_type=f32)


def dot_rows(a, b):
    return lax.dot_general(a, b, (((0,), (0,)), ((), ())), preferred_element_type=f32)


def softplus(u):
    return jnp.maximum(u, 0.0) + jnp.log1p(jnp.exp(-jnp.abs(u)))


def block_mask(feature_rows, value_cols, features, head_dim):
    r = lax.broadcasted_iota(jnp.int32, (feature_rows, value_cols), 0) // features
    c = lax.broadcasted_iota(jnp.int32, (feature_rows, value_cols), 1) // head_dim
    return r == c


def flat(ref, c):
    return ref[:, :, c].reshape(ref.shape[0] * ref.shape[1], c.size)


def column(k, D):
    return pl.ds(pl.multiple_of(k * D, D), D)


def chunk_counts(cfg, odd):
    D, FF, C = cfg[3], cfg[4], cfg[-1]
    wide = FF // C
    return D // C + (wide - D // C) * odd, wide + wide * odd


def plain_gradients(cfg, odd, xin, dbr, buf_a, buf_b, g_hbm, g_sem, stage):
    D, FF, C = cfg[3], cfg[4], cfg[-1]
    first_kind, count = chunk_counts(cfg, odd)
    wide = FF // C
    own = D // C

    def store(k):
        cp = pltpu.make_async_copy(stage, g_hbm.at[:, column(k, C)], g_sem.at[0])
        cp.start()
        cp.wait()

    def one(k, carry):
        @pl.when(k < first_kind)
        def _():
            src = column(k + (wide - own) * (1 - odd), C)
            stage[...] = dot_rows(flat(dbr, pl.ds(0, D)), flat(buf_a, src))
            store(k)

        @pl.when(k >= first_kind)
        def _():
            stage[...] = dot_rows(flat(xin, pl.ds(0, D)), flat(buf_b, column(k - first_kind, C)))
            store(k)

        return carry

    lax.fori_loop(0, count, one, 0)

    @pl.when(odd == 0)
    def _():
        stage[...] = jnp.zeros_like(stage)

        def rest(k, carry):
            store(k)
            return carry

        lax.fori_loop(wide, 2 * wide, rest, 0)


def reduce_gradients(
    cfg,
    s,
    d,
    odd,
    w,
    u,
    wt,
    ut,
    xin,
    dbr,
    buf_a,
    buf_b,
    g_hbm,
    small_ref,
    small_outs,
    ready,
    keep,
    core_out,
    cross_out,
    line_out,
    final,
    small_in,
    core_send,
    core_recv,
    line_send,
    up_recv,
    down_recv,
    final_sem,
    cross_send,
    cross_recv,
    away_send,
    away_recv,
    small_send,
    small_recv,
):
    M, L, LP, D, FF, HD, FE, NS, ND, fscale, in_kernel, C = cfg
    Z = ND // 2
    B = D // ND
    R = Z * B
    K = M * LP
    wide = FF // C
    own = D // C
    fold = D // C
    keeps = keep.shape[0]
    p = lax.rem(d, 2)
    z = d // 2
    sib = d + 1 - 2 * p
    first_kind, count = chunk_counts(cfg, odd)
    cross = wide // 2
    pre = jnp.where(s == 1, cross, 0)
    came = jnp.where(s == 2, cross, 0)
    lines = count - pre + came
    dma_to = functools.partial(pltpu.make_async_remote_copy, device_id_type=MESH)

    pl.semaphore_signal(ready.at[0], inc=1, device_id=(s, sib), device_id_type=MESH)

    @pl.when(z > 0)
    def _():
        pl.semaphore_signal(ready.at[2], inc=1, device_id=(s, d - 2), device_id_type=MESH)

    @pl.when(z < Z - 1)
    def _():
        pl.semaphore_signal(ready.at[1], inc=1, device_id=(s, d + 2), device_id_type=MESH)

    def small_copy(o):
        return dma_to(
            small_ref,
            small_in.at[d],
            small_send.at[o],
            small_recv.at[d],
            device_id=(s, lax.rem(d + o, ND)),
        )

    def small_wait(o):
        j = lax.rem(d + o, ND)
        return dma_to(
            small_ref, small_in.at[j], small_send.at[o], small_recv.at[j], device_id=(s, j)
        )

    for o in range(1, ND):
        small_copy(o).start()
    small_in[d] = small_ref[...]

    place_d = pl.ds(0, K)
    place_x = pl.ds((K + 127) // 128 * 128, K)
    for src, at_cols in ((dbr, place_d), (xin, place_x)):
        for i in range(D // 256):
            turned = flat(src, pl.ds(256 * i, 256)).T
            for q in range(8):
                t = 8 * i + q
                block = t * 32 // B
                at = block % 2 * R + block // 2 * B + t * 32 - block * B
                u[pl.ds(at, 32), at_cols] = turned[32 * q : 32 * q + 32]

    per = D // R

    def slot(j):
        return (pl.ds(pl.multiple_of(lax.rem(j, per) * R, 16), R), column(j // per, C))

    def slot_block(j, zt):
        r = pl.multiple_of(lax.rem(j, per) * R + zt * B, 16)
        return (pl.ds(r, B), column(j // per, C))

    def line_place(n, zt):
        r = pl.multiple_of(n // fold * R + zt * B, 16)
        return (pl.ds(r, B), column(lax.rem(n, fold), C))

    def cross_place(c):
        n = 2 * wide - cross + c
        r = pl.multiple_of(n // fold * R, 16)
        return (pl.ds(r, R), column(lax.rem(n, fold), C))

    def core_copy(j):
        return dma_to(
            core_out.at[lax.rem(j, 2)],
            w.at[slot(j)],
            core_send.at[lax.rem(j, 2)],
            core_recv.at[j],
            device_id=(s, sib),
        )

    def cross_copy(c):
        return dma_to(
            cross_out.at[c],
            ut.at[cross_place(c)],
            cross_send.at[c],
            cross_recv.at[c],
            device_id=(2, d),
        )

    def up_copy(n, zt):
        return dma_to(
            line_out.at[lax.rem(n, 2), zt],
            ut.at[line_place(n, zt)],
            line_send.at[lax.rem(n, 2), zt],
            up_recv.at[n, zt],
            device_id=(s, d + 2),
        )

    def down_copy(n, zt):
        return dma_to(
            line_out.at[lax.rem(n, 2), zt],
            wt.at[line_place(n, zt)],
            line_send.at[lax.rem(n, 2), zt],
            down_recv.at[n, zt],
            device_id=(s, d - 2),
        )

    def final_copy(n):
        j = n + pre
        early = j + cross * odd + (wide - own) * (1 - odd)
        at = jnp.where(j < first_kind, early, j - first_kind)
        return pltpu.make_async_copy(
            final.at[lax.rem(n, 2)], g_hbm.at[:, column(at, C)], final_sem.at[lax.rem(n, 2)]
        )

    def away(n):
        return ((s == 3) & (n < cross)) | ((s == 2) & (n >= count))

    def away_copy(n):
        c = n - jnp.where(s == 2, count, 0)
        return dma_to(
            final.at[lax.rem(n, 2)],
            g_hbm.at[:, column(wide + c, C)],
            away_send.at[lax.rem(n, 2)],
            away_recv.at[c],
            device_id=(jnp.where(s == 3, 2, 0), d),
        )

    def away_arrival(c):
        return dma_to(
            final.at[0],
            g_hbm.at[:, column(wide + c, C)],
            away_send.at[0],
            away_recv.at[c],
            device_id=(jnp.where(s == 3, 2, 0), d),
        )

    def final_wait(n):
        @pl.when(away(n))
        def _():
            away_copy(n).wait_send()

        @pl.when(jnp.logical_not(away(n)))
        def _():
            final_copy(n).wait()

    def total(n, zt):
        j = n + pre
        return keep[lax.rem(j, keeps), pl.ds(zt * B, B), :] + w[slot_block(j, zt)].astype(f32)

    near = jnp.minimum(z, Z - 1 - z)
    far = jnp.maximum(z, Z - 1 - z)

    def step(lo, hi, k, carry):
        @pl.when(k < count)
        def _():
            sl = lax.rem(k, 2)

            def products(place, right):
                @pl.when(k >= 2)
                def _():
                    core_copy(k - 2).wait_send()

                theirs = pl.ds(pl.multiple_of((1 - p) * R, 16), R)
                mine = pl.ds(pl.multiple_of(p * R, 16), R)
                core_out[sl] = dot(u[theirs, place], right).astype(bf16)

                @pl.when(k == 0)
                def _():
                    pl.semaphore_wait(ready.at[0], 1)

                core_copy(k).start()
                keep[lax.rem(k, keeps)] = dot(u[mine, place], right)

            @pl.when(k < first_kind)
            def _():
                products(place_d, flat(buf_a, column(k + (wide - own) * (1 - odd), C)))

            @pl.when(k >= first_kind)
            def _():
                products(place_x, flat(buf_b, column(k - first_kind, C)))

        @pl.when((lo >= count) & (k < count + came))
        def _():
            c = k - count
            cross_copy(c).wait_recv()
            keep[lax.rem(k, keeps)] = ut[cross_place(c)].astype(f32)
            w[slot(k)] = jnp.zeros((R, C), bf16)

        c_cross = k - 1

        @pl.when((c_cross >= 0) & (c_cross < pre))
        def _():
            core_copy(c_cross).wait_recv()
            both = keep[lax.rem(c_cross, keeps)] + w[slot(c_cross)].astype(f32)
            cross_out[c_cross] = both.astype(bf16)
            cross_copy(c_cross).start()

        n_near = k - 1 - pre - near

        @pl.when((n_near >= lo) & (n_near < hi) & (n_near + pre < count))
        def _():
            core_copy(n_near + pre).wait_recv()

        n_up = k - 1 - pre - z

        @pl.when((n_up >= lo) & (n_up < hi) & (z < Z - 1))
        def _():
            @pl.when(n_up == 0)
            def _():
                pl.semaphore_wait(ready.at[2], 1)

            for zt in range(Z - 1, 0, -1):
                @pl.when(zt > z)
                def _():
                    @pl.when(n_up >= 2)
                    def _():
                        up_copy(n_up - 2, zt).wait_send()

                    @pl.when(z > 0)
                    def _():
                        up_copy(n_up, zt).wait_recv()
                        line_out[lax.rem(n_up, 2), zt] = (
                            total(n_up, zt) + ut[line_place(n_up, zt)].astype(f32)
                        ).astype(bf16)

                    @pl.when(z == 0)
                    def _():
                        line_out[lax.rem(n_up, 2), zt] = total(n_up, zt).astype(bf16)

                    up_copy(n_up, zt).start()

        n_down = k - 1 - pre - (Z - 1 - z)

        @pl.when((n_down >= lo) & (n_down < hi) & (z > 0))
        def _():
            @pl.when(n_down == 0)
            def _():
                pl.semaphore_wait(ready.at[1], 1)

            for zt in range(Z - 1):
                @pl.when(zt < z)
                def _():
                    @pl.when(n_down >= 2)
                    def _():
                        down_copy(n_down - 2, zt).wait_send()

                    @pl.when(z < Z - 1)
                    def _():
                        down_copy(n_down, zt).wait_recv()
                        line_out[lax.rem(n_down, 2), zt] = (
                            total(n_down, zt) + wt[line_place(n_down, zt)].astype(f32)
                        ).astype(bf16)

                    @pl.when(z == Z - 1)
                    def _():
                        line_out[lax.rem(n_down, 2), zt] = total(n_down, zt).astype(bf16)

                    down_copy(n_down, zt).start()

        n_own = k - 1 - pre - far

        @pl.when((n_own >= lo) & (n_own < hi))
        def _():
            sl = lax.rem(n_own, 2)

            @pl.when(n_own >= 2)
            def _():
                final_wait(n_own - 2)

            final[sl] = total(n_own, z)

            @pl.when(z > 0)
            def _():
                up_copy(n_own, z).wait_recv()
                final[sl] += ut[line_place(n_own, z)].astype(f32)

            @pl.when(z < Z - 1)
            def _():
                down_copy(n_own, z).wait_recv()
                final[sl] += wt[line_place(n_own, z)].astype(f32)

            @pl.when(away(n_own))
            def _():
                away_copy(n_own).start()

            @pl.when(jnp.logical_not(away(n_own)))
            def _():
                final_copy(n_own).start()

        return carry

    own_lines = count - pre
    lax.fori_loop(0, count + 1 + far, functools.partial(step, 0, own_lines), 0)
    later = jnp.where(s == 2, count + came + 1 + far, count)
    lax.fori_loop(count, later, functools.partial(step, count, count + came), 0)

    for back in (2, 1):
        core_copy(count - back).wait_send()
        n = lines - back
        for zt in range(Z):
            @pl.when(zt > z)
            def _():
                up_copy(n, zt).wait_send()

            @pl.when(zt < z)
            def _():
                down_copy(n, zt).wait_send()

        final_wait(n)

    @pl.when(s == 1)
    def _():
        for c in range(cross):
            cross_copy(c).wait_send()

    @pl.when(odd == 0)
    def _():
        for c in range(cross):
            away_arrival(c).wait_recv()

    for o in range(1, ND):
        small_wait(o).wait_recv()
        small_copy(o).wait_send()
    acc = small_in[0]
    for j in range(1, ND):
        acc = acc + small_in[j]
    small_ref[...] = acc
    bias_out, gain_out, shift_out = small_outs
    P = FF // ND
    bias_out[...] = small_ref[:, pl.ds(pl.multiple_of(d * P, 128), P)]
    for j in range(ND):
        @pl.when(d == j)
        def _():
            gain_out[...] = acc[:, FF + B * j : FF + B * j + B]
            shift_out[...] = acc[:, FF + D + B * j : FF + D + B * j + B]


def pipeline_kernel(
    cfg,
    len_ref,
    x_hbm,
    cot_hbm,
    pred_ref,
    slab_hbm,
    bias_ref,
    gain_ref,
    shift_ref,
    draws_ref,
    out_hbm,
    grad_hbm,
    g_hbm,
    *refs,
):
    M, L, LP, D, FF, HD, FE, NS, ND, fscale, in_kernel, C = cfg
    small_outs = refs[:3] if in_kernel else ()
    small_ref = refs[3] if in_kernel else refs[0]
    fmap_ref = refs[4] if in_kernel else refs[1]
    (
        w,
        u,
        wt,
        ut,
        xin,
        out,
        dyin,
        dxo,
        dbr,
        nbuf,
        rbuf,
        buf_a,
        buf_b,
        land,
        out_stage,
        grad_stage,
        load_sem,
        x_sem,
        u_send,
        u_recv,
        f_send,
        f_recv,
        b_send,
        b_recv,
        stage_sem,
        g_sem,
        *reduce_refs,
    ) = refs[5:] if in_kernel else refs[2:]
    HALF = FF // 2
    GH = 256 // HD
    G = D // 256
    GF = GH * FE
    top = (LP // 2 + 15) // 16 * 16
    halves = (pl.ds(0, top), pl.ds(top, LP - top))
    whole = pl.ds(0, LP)
    relay_lo, relay_hi = RELAYED if NS == 4 else (0, 0)
    relayed = relay_hi - relay_lo
    s = lax.axis_index("section")
    d = lax.axis_index("dp")
    odd = lax.rem(s, 2)
    is_attn = odd == 0
    is_ff = odd == 1
    first = s == 0
    last = s == NS - 1
    sib = d + 1 - 2 * lax.rem(d, 2)
    mate = d + 2 - 4 * lax.rem(d // 2, 2)
    quarter = D // 4
    pieces = 4
    piece = quarter // pieces

    barrier = pltpu.get_barrier_semaphore()

    def greet(cond, ts, td):
        @pl.when(cond)
        def _():
            pl.semaphore_signal(barrier, inc=1, device_id=(ts, td), device_id_type=MESH)

    always = s >= 0
    partners = 2
    if in_kernel:
        partners = ND - 1
        for o in range(1, ND):
            greet(always, s, lax.rem(d + o, ND))
    else:
        greet(always, s, sib)
        greet(always, s, mate)
    greet(s > 0, s - 1, d)
    greet(s < NS - 1, s + 1, d)
    if relayed > 0 or in_kernel:
        greet(s == 0, 2, d)
        greet(s == 2, 0, d)
        extra = jnp.where(lax.rem(s, 2) == 0, 1, 0)
    else:
        extra = 0

    w_copy = pltpu.make_async_copy(slab_hbm.at[0, :, pl.ds(0, FF)], w, load_sem.at[0])
    u_copy = pltpu.make_async_copy(
        slab_hbm.at[0, :, pl.ds(FF, HALF)], u.at[:, pl.ds(HALF, HALF)], load_sem.at[1]
    )
    w_copy.start()

    def land_copy(ref, m):
        sl = lax.rem(m, 2)
        return pltpu.make_async_copy(ref.at[m], land.at[sl], x_sem.at[sl])

    @pl.when(first)
    def _():
        for m in range(2):
            land_copy(x_hbm, m).start()

    @pl.when(last)
    def _():
        for m in range(2):
            land_copy(cot_hbm, m).start()

    @pl.when(is_ff)
    def _():
        u_copy.start()

    small_ref[...] = jnp.zeros_like(small_ref)
    bias_grad_ref = small_ref.at[:, pl.ds(0, FF)]
    gain_grad_ref = small_ref.at[:, pl.ds(FF, D)]
    shift_grad_ref = small_ref.at[:, pl.ds(FF + D, D)]

    @pl.when(first | last)
    def _():
        pl.semaphore_wait(barrier, partners + 1 + extra)

    @pl.when((s > 0) & (s < NS - 1))
    def _():
        pl.semaphore_wait(barrier, partners + 2 + extra)

    q0 = lax.rem(d, 4)
    q1 = q0 + 2 - 4 * (q0 // 2)
    left = pl.ds(0, HALF)

    def u_rows(q, i):
        return pl.ds(pl.multiple_of(q * quarter + i * piece, piece), piece)

    def u_from_section(i):
        return pltpu.make_async_remote_copy(
            slab_hbm.at[0, u_rows(q0, i), pl.ds(FF, HALF)],
            u.at[u_rows(q0, i), left],
            u_send.at[0, i],
            u_recv.at[0, i],
            device_id=(s + 1, d),
            device_id_type=MESH,
        )

    def u_copy_to(q, i, k, to):
        return pltpu.make_async_remote_copy(
            u.at[u_rows(q, i), left],
            u.at[u_rows(q, i), left],
            u_send.at[k, i],
            u_recv.at[k, i],
            device_id=(s, to),
            device_id_type=MESH,
        )

    @pl.when(is_attn & (s < NS - 1))
    def _():
        for i in range(pieces):
            u_from_section(i).start()

    def turn(src, dst, start, count):
        for i in range(start, start + count):
            dst[pl.ds(256 * i, 256), :] = src[:, pl.ds(256 * i, 256)].T

    w_copy.wait()
    late_turn = first

    @pl.when(is_attn)
    def _():
        turn(w, wt, 3 * D // 256, D // 256)
        f_row = lax.broadcasted_iota(jnp.int32, (FE, GF), 0)
        f_col = lax.broadcasted_iota(jnp.int32, (FE, GF), 1)
        for n in range(G * GH):
            shift = jnp.where(f_col == f_row + n % GH * FE, 1.0, 0.0).astype(bf16)
            spread = dot(draws_ref[n].astype(f32).astype(bf16), shift)
            fmap_ref[n // GH, pl.ds(n % GH * HD, HD), :] = spread.astype(bf16)

    @pl.when(s == 2)
    def _():
        turn(w, wt, 0, 3 * D // 256)

    @pl.when(is_ff)
    def _():
        turn(w, wt, 0, FF // 256)
        u_copy.wait()
        turn(u, ut, HALF // 256, HALF // 256)
        for i in range(pieces):
            u_from_section(i).wait_recv()
            u_copy_to(q0, i, 1, mate).start()
            u_copy_to(q0, i, 2, sib).start()
            if i > 0:
                u_copy_to(q0, i - 1, 1, mate).wait_recv()
                u_copy_to(q1, i - 1, 3, sib).start()
        u_copy_to(q0, pieces - 1, 1, mate).wait_recv()
        u_copy_to(q1, pieces - 1, 3, sib).start()
        for i in range(pieces):
            u_copy_to(q0, i, 2, sib).wait_recv()
            u_copy_to(q1, i, 3, sib).wait_recv()
        turn(u, ut, 0, HALF // 256)

    g_row = gain_ref[...]
    b_row = shift_ref[...]
    head_mask = block_mask(GF, 256, FE, HD)
    pair_mask = jnp.concatenate([head_mask, head_mask], axis=1)

    def sz_at(m, g):
        n = m * G + g
        r = pl.multiple_of(lax.rem(n, D // GF) * GF, GF)
        c = pl.multiple_of(n // (D // GF) * 512, 512)
        return (pl.ds(r, GF), pl.ds(c, 512))

    def valid_rows(m, rows):
        at = lax.broadcasted_iota(jnp.int32, (rows.size, GF), 0) + rows.start
        return at < len_ref[m]

    def with_ones(v):
        return jnp.concatenate([v, jnp.ones(v.shape, bf16)], axis=1)

    def norm_forward(m, rows, pre):
        mean = jnp.mean(pre, axis=-1, keepdims=True)
        cen = pre - mean
        r = lax.rsqrt(jnp.mean(cen * cen, axis=-1, keepdims=True) + norm_epsilon)
        n = cen * r
        nbuf[m, rows, :] = n
        rbuf[m, rows, :] = r
        out[m, rows, :] = (n * g_row + b_row).astype(bf16)

    def norm_backward(m, rows):
        dy = dyin[m, rows, :].astype(f32)
        n = nbuf[m, rows, :]
        dn = dy * g_row
        m1 = jnp.mean(dn, axis=-1, keepdims=True)
        m2 = jnp.mean(dn * n, axis=-1, keepdims=True)
        gain_grad_ref[...] += jnp.sum(dy * n, axis=0, keepdims=True)
        shift_grad_ref[...] += jnp.sum(dy, axis=0, keepdims=True)
        dpre = rbuf[m, rows, :] * (dn - m1 - n * m2)
        dbr[m, rows, :] = dpre.astype(bf16)
        return dpre

    def next_copy(m, h):
        return pltpu.make_async_remote_copy(
            out.at[m, halves[h]],
            xin.at[m, halves[h]],
            f_send.at[m, h],
            f_recv.at[m, h],
            device_id=(s + 1, d),
            device_id_type=MESH,
        )

    def back_copy(m, h):
        return pltpu.make_async_remote_copy(
            dxo.at[m, halves[h]],
            dyin.at[m, halves[h]],
            b_send.at[m, h],
            b_recv.at[m, h],
            device_id=(s - 1, d),
            device_id_type=MESH,
        )

    def relay_at(m, h):
        start = pl.multiple_of(m * LP + halves[h].start, 16)
        return ut.at[pl.ds(start, halves[h].size)]

    def relay_in(m, h):
        return pltpu.make_async_remote_copy(
            dxo.at[m, halves[h]],
            relay_at(m, h),
            b_send.at[m, h],
            f_recv.at[m, h],
            device_id=(0, d),
            device_id_type=MESH,
        )

    def relay_on(m, h):
        return pltpu.make_async_remote_copy(
            relay_at(m, h),
            dyin.at[m, halves[h]],
            b_send.at[m, h],
            b_recv.at[m, h],
            device_id=(1, d),
            device_id_type=MESH,
        )

    def send_next(m, h):
        if h == 0:
            @pl.when(is_attn & (m == 0))
            def _():
                for i in range(pieces):
                    u_from_section(i).wait_send()

        @pl.when(s < NS - 1)
        def _():
            next_copy(m, h).start()

    def by_relay(m):
        return (s == 2) & (m >= relay_lo) & (m < relay_hi)

    def send_back(m, h):
        @pl.when((s > 0) & jnp.logical_not(by_relay(m)))
        def _():
            back_copy(m, h).start()

        @pl.when(by_relay(m))
        def _():
            relay_in(m, h).start()

    v_at = [pl.ds(256 * g, 256) for g in range(G)]
    fq_at = [pl.ds(D + GF * g, GF) for g in range(G)]
    fk_at = [pl.ds(D + GF * (G + g), GF) for g in range(G)]
    out_at = pl.ds(3 * D, D)

    def attend_features(m, rows):
        x = xin[m, rows, :]
        valid = valid_rows(m, rows)
        for g in range(G):
            qkv = [
                (dot(x, w[:, c]) + bias_ref[:, c]).astype(bf16)
                for c in (pl.ds(k * D + 256 * g, 256) for k in range(3))
            ]
            fq = softplus(dot(qkv[0], fmap_ref[g]) * fscale).astype(bf16)
            fk = softplus(dot(qkv[1], fmap_ref[g]) * fscale)
            buf_a[m, rows, v_at[g]] = qkv[2]
            buf_a[m, rows, fq_at[g]] = fq
            buf_a[m, rows, fk_at[g]] = jnp.where(valid, fk, 0.0).astype(bf16)

    def summaries(m):
        for g in range(G):
            sz = dot_rows(buf_a[m, :, fk_at[g]], with_ones(buf_a[m, :, v_at[g]]))
            u[sz_at(m, g)] = jnp.where(pair_mask, sz, 0.0).astype(bf16)

    def attend_mix(m, rows):
        for g in range(G):
            nd = dot(buf_a[m, rows, fq_at[g]], u[sz_at(m, g)])
            mixed = (nd[:, :256] / nd[:, 256:]).astype(bf16)
            buf_a[m, rows, pl.ds(3 * D + 256 * g, 256)] = mixed
        branch = dot(buf_a[m, rows, out_at], wt[out_at, :]) + bias_ref[:, out_at]
        norm_forward(m, rows, xin[m, rows, :].astype(f32) + branch)

    def attend_forward(m, mode):
        if mode == 2:
            attend_features(m, whole)
            summaries(m)
            attend_mix(m, whole)
            send_next(m, 0)
            send_next(m, 1)
            return
        attend_features(m, halves[mode])
        if mode == 1:
            summaries(m)
            for part, rows in enumerate(halves):
                attend_mix(m, rows)
                send_next(m, part)

    def feed_forward(m, mode):
        rows = (halves + (whole,))[mode]
        x = xin[m, rows, :]
        tile = 512
        for j in range(FF // tile):
            c = pl.ds(j * tile, tile)
            a = dot(x, w[:, c]) + bias_ref[:, c]
            cdf = 0.5 + 0.5 * lax.erf(a * 0.7071067811865476)
            pdf = jnp.exp(a * a * -0.5) * 0.3989422804014327
            buf_a[m, rows, c] = (a * cdf).astype(bf16)
            buf_b[m, rows, c] = (cdf + a * pdf).astype(bf16)
        branch = dot(buf_a[m, rows, :], ut[...])
        norm_forward(m, rows, x.astype(f32) + branch)
        for h in (mode,) if mode < 2 else (0, 1):
            send_next(m, h)

    def attend_backward(m, mode):
        rows = (halves + (whole,))[mode]
        dpre = norm_backward(m, rows)
        nbuf[m, rows, :] = dpre
        db = dbr[m, rows, :]
        bias_grad_ref[:, out_at] += jnp.sum(db.astype(f32), axis=0, keepdims=True)

        def store(rows, k, g, val):
            c = pl.ds(k * D + 256 * g, 256)
            buf_b[m, rows, c] = val
            bias_grad_ref[:, c] += jnp.sum(val.astype(f32), axis=0, keepdims=True)

        for g in range(G):
            dmix = dot(db, w[:, pl.ds(3 * D + 256 * g, 256)])
            fq = buf_a[m, rows, fq_at[g]]
            sz = u[sz_at(m, g)]
            nd = dot(fq, sz)
            rden = 1.0 / nd[:, 256:]
            dnum = dmix * rden
            dden = -dnum * (nd[:, :256] * rden)
            de = jnp.concatenate([dnum, dden], axis=1).astype(bf16)
            buf_b[m, rows, pl.ds(D + 512 * g, 512)] = de
            duq = dot_cols(de, sz) * (1.0 - jnp.exp(-fq.astype(f32)))
            dq = (dot_cols(duq.astype(bf16), fmap_ref[g]) * fscale).astype(bf16)
            store(rows, 0, g, dq)
        if mode == 0:
            return
        for g in range(G):
            dsz = dot_rows(buf_a[m, :, fq_at[g]], buf_b[m, :, pl.ds(D + 512 * g, 512)])
            u[sz_at(m, g)] = jnp.where(pair_mask, dsz, 0.0).astype(bf16)
        for part, rows in enumerate(halves if mode == 1 else (whole,)):
            valid = valid_rows(m, rows)
            for g in range(G):
                dsz = u[sz_at(m, g)]
                fk = buf_a[m, rows, fk_at[g]]
                dfk = dot_cols(with_ones(buf_a[m, rows, v_at[g]]), dsz)
                duk = jnp.where(valid, dfk, 0.0) * (1.0 - jnp.exp(-fk.astype(f32)))
                dk = (dot_cols(duk.astype(bf16), fmap_ref[g]) * fscale).astype(bf16)
                store(rows, 1, g, dk)
                store(rows, 2, g, dot(fk, dsz[:, :256]).astype(bf16))
            inner = pl.ds(0, 3 * D)
            dx = nbuf[m, rows, :] + dot(buf_b[m, rows, inner], wt[inner, :])
            dxo[m, rows, :] = dx.astype(bf16)
            for h in (part,) if mode == 1 else (0, 1):
                send_back(m, h)

    def feed_backward(m, mode):
        rows = (halves + (whole,))[mode]
        dpre = norm_backward(m, rows)
        db = dbr[m, rows, :]
        tile = 512
        for j in range(FF // tile):
            c = pl.ds(j * tile, tile)
            da = (dot(db, u[:, c]) * buf_b[m, rows, c].astype(f32)).astype(bf16)
            buf_b[m, rows, c] = da
            bias_grad_ref[:, c] += jnp.sum(da.astype(f32), axis=0, keepdims=True)
        dx = dpre + dot(buf_b[m, rows, :], wt[...])
        dxo[m, rows, :] = dx.astype(bf16)
        for h in (mode,) if mode < 2 else (0, 1):
            send_back(m, h)

    def out_copy(m):
        return pltpu.make_async_copy(out_stage, out_hbm.at[m], stage_sem.at[0])

    def grad_copy(m):
        return pltpu.make_async_copy(grad_stage, grad_hbm.at[m], stage_sem.at[1])

    def write_out(copy, rows, staged, m):
        @pl.when(m >= 1)
        def _():
            copy(m - 1).wait()

        staged[...] = rows[m, pl.ds(0, L), :]
        copy(m).start()

    pad_zero = jnp.zeros((LP - L, D), bf16)
    eye = lax.broadcasted_iota(jnp.int32, (L, L), 0) == lax.broadcasted_iota(jnp.int32, (L, L), 1)

    def forward_step(m, mode):
        if mode != 1:
            @pl.when(first)
            def _():
                land_copy(x_hbm, m).wait()
                xin[m] = jnp.concatenate([land[lax.rem(m, 2)], pad_zero], axis=0)

                @pl.when(m + 2 < M)
                def _():
                    land_copy(x_hbm, m + 2).start()

        @pl.when(s > 0)
        def _():
            for h in (mode,) if mode < 2 else (0, 1):
                next_copy(m, h).wait_recv()

        @pl.when(is_attn)
        def _():
            attend_forward(m, mode)

        @pl.when(is_ff)
        def _():
            feed_forward(m, mode)

        if mode > 0:
            write_out(out_copy, out, out_stage, m)
        if mode == 1:
            @pl.when(first & (m == M - 1))
            def _():
                turn(w, wt, 0, 3 * D // 256)

    def backward_step(m, mode):
        if mode != 1:
            @pl.when(last)
            def _():
                land_copy(cot_hbm, m).wait()
                row = jnp.where(
                    lax.broadcasted_iota(jnp.int32, (1, L), 1) < len_ref[m],
                    pred_ref[pl.ds(m, 1), :].astype(f32),
                    0.0,
                )
                col = jnp.sum(jnp.where(eye, row, 0.0), axis=1, keepdims=True)
                masked = (land[lax.rem(m, 2)].astype(f32) * col).astype(bf16)
                dyin[m] = jnp.concatenate([masked, pad_zero], axis=0)

                @pl.when(m + 2 < M)
                def _():
                    land_copy(cot_hbm, m + 2).start()

        @pl.when(s < NS - 1)
        def _():
            for h in (mode,) if mode < 2 else (0, 1):
                back_copy(m, h).wait_recv()

        @pl.when(is_attn)
        def _():
            attend_backward(m, mode)

        @pl.when(is_ff)
        def _():
            feed_backward(m, mode)

        if mode > 0:
            write_out(grad_copy, dxo, grad_stage, m)

    back_start = jnp.where(s == 0, 16, jnp.where(s == 1, 12, jnp.where(s == 2, 10, 6)))
    relay_start = 12

    def when_due(start, act):
        def at(t):
            i = t - start
            m = i // 2

            apart = i < 0
            for n in SPLIT:
                apart = apart | (m == n % M)
            here = (i >= 0) & (i < 2 * M)

            @pl.when(here & jnp.logical_not(apart) & (lax.rem(i, 2) == 1))
            def _():
                act(m, 2)

            for h in range(2):
                @pl.when(here & apart & (lax.rem(i, 2) == h))
                def _():
                    act(m, h)

        return at

    forward_at = when_due(2 * s, forward_step)
    backward_at = when_due(back_start, backward_step)

    def tick(t, carry):
        forward_at(t)
        if relayed > 0:
            i = t - relay_start
            for h in range(2):
                @pl.when((s == 0) & (i >= 0) & (i < 2 * relayed) & (lax.rem(i, 2) == h))
                def _():
                    relay_in(relay_lo + i // 2, h).wait_recv()
                    relay_on(relay_lo + i // 2, h).start()
        backward_at(t)
        return carry

    lax.fori_loop(0, 28, tick, 0)

    if relayed > 0:
        @pl.when(s == 0)
        def _():
            for m in range(relay_lo, relay_hi):
                for h in range(2):
                    relay_on(m, h).wait_send()

    @pl.when(is_ff)
    def _():
        for i in range(pieces):
            u_copy_to(q0, i, 1, mate).wait_send()
            u_copy_to(q0, i, 2, sib).wait_send()
            u_copy_to(q1, i, 3, sib).wait_send()

    if in_kernel:
        reduce_gradients(
            cfg,
            s,
            d,
            odd,
            w,
            u,
            wt,
            ut,
            xin,
            dbr,
            buf_a,
            buf_b,
            g_hbm,
            small_ref,
            small_outs,
            *reduce_refs,
        )
    else:
        plain_gradients(cfg, odd, xin, dbr, buf_a, buf_b, g_hbm, g_sem, *reduce_refs)

    for m in range(M):
        for h in range(2):
            @pl.when(s < NS - 1)
            def _():
                next_copy(m, h).wait_send()

            @pl.when(s > 0)
            def _():
                back_copy(m, h).wait_send()

    out_copy(M - 1).wait()
    grad_copy(M - 1).wait()


def shards(
    block_input, cotangent, lengths, predicted, slab, in_bias, norm_gain, norm_bias, feature_draws
):
    NS = lax.axis_size("section")
    ND = lax.axis_size("dp")
    M, L, D = block_input.shape
    FF = in_bias.shape[1]
    H, HD, FE = feature_draws.shape
    LP = (L + 15) // 16 * 16
    GH = 256 // HD
    G = D // 256
    GF = GH * FE
    fscale = float((3.0 / (20.0 * HD)) ** 0.5)
    in_kernel = D // ND % 32 == 0 and NS == 4
    C = CHUNK if in_kernel else D
    cfg = (M, L, LP, D, FF, HD, FE, NS, ND, fscale, in_kernel, C)
    hbm = pl.BlockSpec(memory_space=pl.ANY)
    vmem = pl.BlockSpec(memory_space=pltpu.VMEM)
    smem = pl.BlockSpec(memory_space=pltpu.SMEM)
    dma = pltpu.SemaphoreType.DMA
    rows_bf = pltpu.VMEM((M, LP, D), bf16)
    wide_bf = pltpu.VMEM((M, LP, FF), bf16)
    small_size = FF + 2 * D
    smalls = [FF // ND, D // ND, D // ND] if in_kernel else [small_size]
    scratch = [pltpu.VMEM((1, small_size), f32)] if in_kernel else []
    scratch += [
        pltpu.VMEM((G, GH * HD, GF), bf16),
        pltpu.VMEM((D, FF), bf16),
        pltpu.VMEM((D, FF), bf16),
        pltpu.VMEM((FF, D), bf16),
        pltpu.VMEM((FF, D), bf16),
        rows_bf,
        rows_bf,
        rows_bf,
        rows_bf,
        rows_bf,
        pltpu.VMEM((M, LP, D), f32),
        pltpu.VMEM((M, LP, 1), f32),
        wide_bf,
        wide_bf,
        pltpu.VMEM((2, L, D), bf16),
        pltpu.VMEM((L, D), bf16),
        pltpu.VMEM((L, D), bf16),
        dma((2,)),
        dma((2,)),
        dma((4, 4)),
        dma((4, 4)),
        dma((M, 2)),
        dma((M, 2)),
        dma((M, 2)),
        dma((M, 2)),
        dma((2,)),
        dma((1,)),
    ]
    if in_kernel:
        Z, B, chunks = ND // 2, D // ND, 2 * FF // C
        cross = FF // C // 2
        lines = chunks
        scratch += [
            pltpu.SemaphoreType.REGULAR((3,)),
            pltpu.VMEM((Z + 1, Z * B, C), f32),
            pltpu.VMEM((2, Z * B, C), bf16),
            pltpu.VMEM((cross, Z * B, C), bf16),
            pltpu.VMEM((2, Z, B, C), bf16),
            pltpu.VMEM((2, B, C), f32),
            pltpu.VMEM((ND, 1, small_size), f32),
            dma((2,)),
            dma((chunks,)),
            dma((2, Z)),
            dma((lines, Z)),
            dma((lines, Z)),
            dma((2,)),
            dma((cross,)),
            dma((cross,)),
            dma((cross,)),
            dma((cross,)),
            dma((ND,)),
            dma((ND,)),
        ]
        g_shape = (B, FF + FF // 2)
    else:
        scratch += [pltpu.VMEM((D, D), f32)]
        g_shape = (D, 2 * FF)
    section_out, section_grad, grads, *small = pl.pallas_call(
        functools.partial(pipeline_kernel, cfg),
        out_shape=[
            jax.ShapeDtypeStruct((M, L, D), bf16),
            jax.ShapeDtypeStruct((M, L, D), bf16),
            jax.ShapeDtypeStruct(g_shape, f32),
        ]
        + [jax.ShapeDtypeStruct((1, n), f32) for n in smalls],
        in_specs=[smem, hbm, hbm, vmem, hbm, vmem, vmem, vmem, vmem],
        out_specs=[hbm, hbm, hbm] + [vmem] * len(smalls),
        scratch_shapes=scratch,
        compiler_params=pltpu.CompilerParams(
            collective_id=0, has_side_effects=True, vmem_limit_bytes=62 * 2**20
        ),
        name="pipeline",
    )(
        lengths,
        block_input,
        cotangent,
        predicted,
        slab,
        in_bias,
        norm_gain,
        norm_bias,
        feature_draws,
    )
    if in_kernel:
        own = grads
        parts = small
    else:
        def scatter(value):
            return lax.psum_scatter(value, "dp", scatter_dimension=0, tiled=True)

        HALF = FF // 2
        both = scatter(grads)
        sums = small[0][0]
        parts = [scatter(v)[None] for v in (sums[:FF], sums[FF : FF + D], sums[FF + D :])]
        is_attention = lax.axis_index("section") % 2 == 0
        turned = jnp.where(
            is_attention,
            jnp.concatenate([both[:, D:FF], both[:, :D], both[:, FF:]], axis=1),
            jnp.concatenate([both[:, FF:], both[:, :FF]], axis=1),
        )
        pairs = [(i, i - 1) for i in range(1, NS, 2)]
        arrived = lax.ppermute(turned[:, FF : FF + HALF], "section", pairs)
        rest = jnp.where(is_attention, arrived, turned[:, FF + HALF :])
        own = jnp.concatenate([turned[:, :FF], rest], axis=1)
    return (
        section_out[None],
        section_grad[None],
        own[None],
        *parts,
    )


def solution(mesh):
    placed = (
        P("dp", None, None),
        P("dp", None, None),
        P("dp"),
        P("dp", None),
        P("section", None, None),
        P("section", None),
        P("section", None),
        P("section", None),
        P(),
    )
    return jax.shard_map(
        shards,
        mesh=mesh,
        in_specs=placed,
        out_specs=(
            P("section", "dp", None, None),
            P("section", "dp", None, None),
            P("section", "dp", None),
            P("section", "dp"),
            P("section", "dp"),
            P("section", "dp"),
        ),
        check_vma=False,
    )
```

```python
import functools

import jax
import jax.numpy as jnp
from jax import lax
from jax.experimental import pallas as pl
from jax.experimental.pallas import tpu as pltpu
from jax.sharding import PartitionSpec as P

MESH = pl.DeviceIdType.MESH
CHUNK = 384
RELAYED = (0, 3)
SPLIT = ()
norm_epsilon = 1e-05
bf16 = jnp.bfloat16
f32 = jnp.float32


def dot(a, b):
    return lax.dot_general(a, b, (((1,), (0,)), ((), ())), preferred_element_type=f32)


def dot_cols(a, b):
    return lax.dot_general(a, b, (((1,), (1,)), ((), ())), preferred_element_type=f32)


def dot_rows(a, b):
    return lax.dot_general(a, b, (((0,), (0,)), ((), ())), preferred_element_type=f32)


def softplus(u):
    return jnp.maximum(u, 0.0) + jnp.log1p(jnp.exp(-jnp.abs(u)))


def block_mask(feature_rows, value_cols, features, head_dim):
    r = lax.broadcasted_iota(jnp.int32, (feature_rows, value_cols), 0) // features
    c = lax.broadcasted_iota(jnp.int32, (feature_rows, value_cols), 1) // head_dim
    return r == c


def flat(ref, c):
    return ref[:, :, c].reshape(ref.shape[0] * ref.shape[1], c.size)


def column(k, D):
    return pl.ds(pl.multiple_of(k * D, D), D)


def chunk_counts(cfg, odd):
    D, FF, C = cfg[3], cfg[4], cfg[-1]
    wide = FF // C
    return D // C + (wide - D // C) * odd, wide + wide * odd


def plain_gradients(cfg, odd, xin, dbr, buf_a, buf_b, g_hbm, g_sem, stage):
    D, FF, C = cfg[3], cfg[4], cfg[-1]
    first_kind, count = chunk_counts(cfg, odd)
    wide = FF // C
    own = D // C

    def store(k):
        cp = pltpu.make_async_copy(stage, g_hbm.at[:, column(k, C)], g_sem.at[0])
        cp.start()
        cp.wait()

    def one(k, carry):
        @pl.when(k < first_kind)
        def _():
            src = column(k + (wide - own) * (1 - odd), C)
            stage[...] = dot_rows(flat(dbr, pl.ds(0, D)), flat(buf_a, src))
            store(k)

        @pl.when(k >= first_kind)
        def _():
            stage[...] = dot_rows(flat(xin, pl.ds(0, D)), flat(buf_b, column(k - first_kind, C)))
            store(k)

        return carry

    lax.fori_loop(0, count, one, 0)

    @pl.when(odd == 0)
    def _():
        stage[...] = jnp.zeros_like(stage)

        def rest(k, carry):
            store(k)
            return carry

        lax.fori_loop(wide, 2 * wide, rest, 0)


def reduce_gradients(
    cfg,
    s,
    d,
    odd,
    w,
    u,
    wt,
    ut,
    xin,
    dbr,
    buf_a,
    buf_b,
    g_hbm,
    small_ref,
    small_outs,
    ready,
    keep,
    core_out,
    cross_out,
    line_out,
    final,
    small_in,
    core_send,
    core_recv,
    line_send,
    up_recv,
    down_recv,
    final_sem,
    cross_send,
    cross_recv,
    away_send,
    away_recv,
    small_send,
    small_recv,
):
    M, L, LP, D, FF, HD, FE, NS, ND, fscale, in_kernel, C = cfg
    Z = ND // 2
    B = D // ND
    R = Z * B
    K = M * LP
    wide = FF // C
    own = D // C
    fold = D // C
    keeps = keep.shape[0]
    p = lax.rem(d, 2)
    z = d // 2
    sib = d + 1 - 2 * p
    first_kind, count = chunk_counts(cfg, odd)
    cross = wide // 2
    shipped = cross + 1
    pre = jnp.where(s == 1, shipped, 0)
    came = jnp.where(s == 2, shipped, 0)
    lines = count - pre + came
    dma_to = functools.partial(pltpu.make_async_remote_copy, device_id_type=MESH)

    pl.semaphore_signal(ready.at[0], inc=1, device_id=(s, sib), device_id_type=MESH)

    @pl.when(z > 0)
    def _():
        pl.semaphore_signal(ready.at[2], inc=1, device_id=(s, d - 2), device_id_type=MESH)

    @pl.when(z < Z - 1)
    def _():
        pl.semaphore_signal(ready.at[1], inc=1, device_id=(s, d + 2), device_id_type=MESH)

    def small_copy(o):
        return dma_to(
            small_ref,
            small_in.at[d],
            small_send.at[o],
            small_recv.at[d],
            device_id=(s, lax.rem(d + o, ND)),
        )

    def small_wait(o):
        j = lax.rem(d + o, ND)
        return dma_to(
            small_ref, small_in.at[j], small_send.at[o], small_recv.at[j], device_id=(s, j)
        )

    for o in range(1, ND):
        small_copy(o).start()
    small_in[d] = small_ref[...]

    place_d = pl.ds(0, K)
    place_x = pl.ds((K + 127) // 128 * 128, K)
    for src, at_cols in ((dbr, place_d), (xin, place_x)):
        for i in range(D // 256):
            turned = flat(src, pl.ds(256 * i, 256)).T
            for q in range(8):
                t = 8 * i + q
                block = t * 32 // B
                at = block % 2 * R + block // 2 * B + t * 32 - block * B
                u[pl.ds(at, 32), at_cols] = turned[32 * q : 32 * q + 32]

    per = D // R

    def slot(j):
        return (pl.ds(pl.multiple_of(lax.rem(j, per) * R, 16), R), column(j // per, C))

    def slot_block(j, zt):
        r = pl.multiple_of(lax.rem(j, per) * R + zt * B, 16)
        return (pl.ds(r, B), column(j // per, C))

    def line_place(n, zt):
        r = pl.multiple_of(n // fold * R + zt * B, 16)
        return (pl.ds(r, B), column(lax.rem(n, fold), C))

    def cross_place(c):
        n = 2 * wide - cross + c
        r = pl.multiple_of(n // fold * R, 16)
        return (pl.ds(r, R), column(lax.rem(n, fold), C))

    spare = (pl.ds(0, R), pl.ds(FF - (C + 127) // 128 * 128, C))

    def core_copy(j):
        return dma_to(
            core_out.at[lax.rem(j, 2)],
            w.at[slot(j)],
            core_send.at[lax.rem(j, 2)],
            core_recv.at[j],
            device_id=(s, sib),
        )

    def cross_copy(c):
        return dma_to(
            cross_out.at[c],
            ut.at[cross_place(c)],
            cross_send.at[c],
            cross_recv.at[c],
            device_id=(2, d),
        )

    def spare_copy():
        return dma_to(
            cross_out.at[cross],
            u.at[spare],
            cross_send.at[cross],
            cross_recv.at[cross],
            device_id=(2, d),
        )

    def up_copy(n, zt):
        return dma_to(
            line_out.at[lax.rem(n, 2), zt],
            ut.at[line_place(n, zt)],
            line_send.at[lax.rem(n, 2), zt],
            up_recv.at[n, zt],
            device_id=(s, d + 2),
        )

    def down_copy(n, zt):
        return dma_to(
            line_out.at[lax.rem(n, 2), zt],
            wt.at[line_place(n, zt)],
            line_send.at[lax.rem(n, 2), zt],
            down_recv.at[n, zt],
            device_id=(s, d - 2),
        )

    def final_copy(n):
        j = n + pre
        early = j + cross * odd + (wide - own) * (1 - odd)
        at = jnp.where(j < first_kind, early, j - first_kind)
        return pltpu.make_async_copy(
            final.at[lax.rem(n, 2)], g_hbm.at[:, column(at, C)], final_sem.at[lax.rem(n, 2)]
        )

    def away(n):
        return ((s == 3) & (n < cross)) | ((s == 2) & (n >= count))

    def away_copy(n):
        c = n - jnp.where(s == 2, count, 0)
        to = jnp.where(s == 3, 2, c // cross)
        return dma_to(
            final.at[lax.rem(n, 2)],
            g_hbm.at[:, column(wide + lax.rem(c, cross), C)],
            away_send.at[lax.rem(n, 2)],
            away_recv.at[c],
            device_id=(to, d),
        )

    def away_arrival(c):
        return dma_to(
            final.at[0],
            g_hbm.at[:, column(wide + c % cross, C)],
            away_send.at[0],
            away_recv.at[c],
            device_id=(jnp.where(s == 3, 2, 0), d),
        )

    def final_wait(n):
        @pl.when(away(n))
        def _():
            away_copy(n).wait_send()

        @pl.when(jnp.logical_not(away(n)))
        def _():
            final_copy(n).wait()

    def total(n, zt):
        j = n + pre
        return keep[lax.rem(j, keeps), pl.ds(zt * B, B), :] + w[slot_block(j, zt)].astype(f32)

    near = jnp.minimum(z, Z - 1 - z)
    far = jnp.maximum(z, Z - 1 - z)

    def make(k):
        sl = lax.rem(k, 2)

        def products(place, right):
            @pl.when(k >= 2)
            def _():
                core_copy(k - 2).wait_send()

            theirs = pl.ds(pl.multiple_of((1 - p) * R, 16), R)
            mine = pl.ds(pl.multiple_of(p * R, 16), R)
            core_out[sl] = dot(u[theirs, place], right).astype(bf16)

            @pl.when(k == 0)
            def _():
                pl.semaphore_wait(ready.at[0], 1)

            core_copy(k).start()
            keep[lax.rem(k, keeps)] = dot(u[mine, place], right)

        @pl.when(k < first_kind)
        def _():
            products(place_d, flat(buf_a, column(k + (wide - own) * (1 - odd), C)))

        @pl.when(k >= first_kind)
        def _():
            products(place_x, flat(buf_b, column(k - first_kind, C)))

    def fetch(k):
        c = k - count

        @pl.when(c < cross)
        def _():
            cross_copy(c).wait_recv()
            keep[lax.rem(k, keeps)] = ut[cross_place(c)].astype(f32)

        @pl.when(c == cross)
        def _():
            spare_copy().wait_recv()
            keep[lax.rem(k, keeps)] = u[spare].astype(f32)

        w[slot(k)] = jnp.zeros((R, C), bf16)

    def ship(c):
        core_copy(c).wait_recv()
        both = keep[lax.rem(c, keeps)] + w[slot(c)].astype(f32)
        cross_out[c] = both.astype(bf16)

        @pl.when(c < cross)
        def _():
            cross_copy(c).start()

        @pl.when(c == cross)
        def _():
            spare_copy().start()

    def step(own_pass, lo, hi, k, carry):
        if own_pass:
            @pl.when(k < count)
            def _():
                make(k)

            @pl.when((k >= 1) & (k - 1 < pre))
            def _():
                ship(k - 1)
        else:
            @pl.when(k < count + came)
            def _():
                fetch(k)

        n_near = k - 1 - pre - near

        if own_pass:
            @pl.when((n_near >= lo) & (n_near < hi))
            def _():
                core_copy(n_near + pre).wait_recv()

        n_up = k - 1 - pre - z

        @pl.when((n_up >= lo) & (n_up < hi) & (z < Z - 1))
        def _():
            @pl.when(n_up == 0)
            def _():
                pl.semaphore_wait(ready.at[2], 1)

            for zt in range(Z - 1, 0, -1):
                @pl.when(zt > z)
                def _():
                    @pl.when(n_up >= 2)
                    def _():
                        up_copy(n_up - 2, zt).wait_send()

                    @pl.when(z > 0)
                    def _():
                        up_copy(n_up, zt).wait_recv()
                        line_out[lax.rem(n_up, 2), zt] = (
                            total(n_up, zt) + ut[line_place(n_up, zt)].astype(f32)
                        ).astype(bf16)

                    @pl.when(z == 0)
                    def _():
                        line_out[lax.rem(n_up, 2), zt] = total(n_up, zt).astype(bf16)

                    up_copy(n_up, zt).start()

        n_down = k - 1 - pre - (Z - 1 - z)

        @pl.when((n_down >= lo) & (n_down < hi) & (z > 0))
        def _():
            @pl.when(n_down == 0)
            def _():
                pl.semaphore_wait(ready.at[1], 1)

            for zt in range(Z - 1):
                @pl.when(zt < z)
                def _():
                    @pl.when(n_down >= 2)
                    def _():
                        down_copy(n_down - 2, zt).wait_send()

                    @pl.when(z < Z - 1)
                    def _():
                        down_copy(n_down, zt).wait_recv()
                        line_out[lax.rem(n_down, 2), zt] = (
                            total(n_down, zt) + wt[line_place(n_down, zt)].astype(f32)
                        ).astype(bf16)

                    @pl.when(z == Z - 1)
                    def _():
                        line_out[lax.rem(n_down, 2), zt] = total(n_down, zt).astype(bf16)

                    down_copy(n_down, zt).start()

        n_own = k - 1 - pre - far

        @pl.when((n_own >= lo) & (n_own < hi))
        def _():
            sl = lax.rem(n_own, 2)

            @pl.when(n_own >= 2)
            def _():
                final_wait(n_own - 2)

            final[sl] = total(n_own, z)

            @pl.when(z > 0)
            def _():
                up_copy(n_own, z).wait_recv()
                final[sl] += ut[line_place(n_own, z)].astype(f32)

            @pl.when(z < Z - 1)
            def _():
                down_copy(n_own, z).wait_recv()
                final[sl] += wt[line_place(n_own, z)].astype(f32)

            @pl.when(away(n_own))
            def _():
                away_copy(n_own).start()

            @pl.when(jnp.logical_not(away(n_own)))
            def _():
                final_copy(n_own).start()

        return carry

    own_lines = count - pre
    lax.fori_loop(0, count + 1 + far, functools.partial(step, True, 0, own_lines), 0)
    later = jnp.where(s == 2, count + came + 1 + far, count)
    lax.fori_loop(count, later, functools.partial(step, False, count, count + came), 0)

    for back in (2, 1):
        core_copy(count - back).wait_send()
        n = lines - back
        for zt in range(Z):
            @pl.when(zt > z)
            def _():
                up_copy(n, zt).wait_send()

            @pl.when(zt < z)
            def _():
                down_copy(n, zt).wait_send()

        final_wait(n)

    @pl.when(s == 1)
    def _():
        for c in range(cross):
            cross_copy(c).wait_send()
        spare_copy().wait_send()
        away_arrival(cross).wait_recv()

    @pl.when(odd == 0)
    def _():
        for c in range(cross):
            away_arrival(c).wait_recv()

    for o in range(1, ND):
        small_wait(o).wait_recv()
        small_copy(o).wait_send()
    acc = small_in[0]
    for j in range(1, ND):
        acc = acc + small_in[j]
    small_ref[...] = acc
    bias_out, gain_out, shift_out = small_outs
    P = FF // ND
    bias_out[...] = small_ref[:, pl.ds(pl.multiple_of(d * P, 128), P)]
    for j in range(ND):
        @pl.when(d == j)
        def _():
            gain_out[...] = acc[:, FF + B * j : FF + B * j + B]
            shift_out[...] = acc[:, FF + D + B * j : FF + D + B * j + B]


def pipeline_kernel(
    cfg,
    len_ref,
    x_hbm,
    cot_hbm,
    pred_ref,
    slab_hbm,
    bias_ref,
    gain_ref,
    shift_ref,
    draws_hbm,
    out_hbm,
    grad_hbm,
    g_hbm,
    *refs,
):
    M, L, LP, D, FF, HD, FE, NS, ND, fscale, in_kernel, C = cfg
    small_outs = refs[:3] if in_kernel else ()
    small_ref = refs[3] if in_kernel else refs[0]
    fmap_ref, draws_ref = refs[4:6] if in_kernel else refs[1:3]
    (
        w,
        u,
        wt,
        ut,
        xin,
        out,
        dyin,
        dxo,
        dbr,
        nbuf,
        rbuf,
        buf_a,
        buf_b,
        land,
        out_stage,
        grad_stage,
        load_sem,
        x_sem,
        u_send,
        u_recv,
        f_send,
        f_recv,
        b_send,
        b_recv,
        stage_sem,
        g_sem,
        *reduce_refs,
    ) = refs[6:] if in_kernel else refs[3:]
    HALF = FF // 2
    GH = 256 // HD
    G = D // 256
    GF = GH * FE
    top = (LP // 2 + 15) // 16 * 16
    halves = (pl.ds(0, top), pl.ds(top, LP - top))
    whole = pl.ds(0, LP)
    relay_lo, relay_hi = RELAYED if NS == 4 else (0, 0)
    relayed = relay_hi - relay_lo
    s = lax.axis_index("section")
    d = lax.axis_index("dp")
    odd = lax.rem(s, 2)
    is_attn = odd == 0
    is_ff = odd == 1
    first = s == 0
    last = s == NS - 1
    sib = d + 1 - 2 * lax.rem(d, 2)
    mate = d + 2 - 4 * lax.rem(d // 2, 2)
    pieces = 4
    piece = D // 12

    barrier = pltpu.get_barrier_semaphore()

    def greet(cond, ts, td):
        @pl.when(cond)
        def _():
            pl.semaphore_signal(barrier, inc=1, device_id=(ts, td), device_id_type=MESH)

    always = s >= 0
    partners = 2
    if in_kernel:
        partners = ND - 1
        for o in range(1, ND):
            greet(always, s, lax.rem(d + o, ND))
    else:
        greet(always, s, sib)
        greet(always, s, mate)
    greet(s > 0, s - 1, d)
    greet(s < NS - 1, s + 1, d)
    if relayed > 0 or in_kernel:
        greet(s == 0, 2, d)
        greet(s == 2, 0, d)
        extra = jnp.where(lax.rem(s, 2) == 0, 1, 0)
    else:
        extra = 0

    w_copy = pltpu.make_async_copy(slab_hbm.at[0, :, pl.ds(0, FF)], w, load_sem.at[0])
    u_copy = pltpu.make_async_copy(
        slab_hbm.at[0, :, pl.ds(FF, HALF)], u.at[:, pl.ds(HALF, HALF)], load_sem.at[1]
    )
    w_copy.start()
    draws_copy = pltpu.make_async_copy(draws_hbm, draws_ref, load_sem.at[2])

    @pl.when(is_attn)
    def _():
        draws_copy.start()


    def land_copy(ref, m):
        sl = lax.rem(m, 2)
        return pltpu.make_async_copy(ref.at[m], land.at[sl], x_sem.at[sl])

    @pl.when(first)
    def _():
        for m in range(2):
            land_copy(x_hbm, m).start()

    @pl.when(last)
    def _():
        for m in range(2):
            land_copy(cot_hbm, m).start()

    @pl.when(is_ff)
    def _():
        u_copy.start()

    small_ref[...] = jnp.zeros_like(small_ref)
    bias_grad_ref = small_ref.at[:, pl.ds(0, FF)]
    gain_grad_ref = small_ref.at[:, pl.ds(FF, D)]
    shift_grad_ref = small_ref.at[:, pl.ds(FF + D, D)]

    @pl.when(first | last)
    def _():
        pl.semaphore_wait(barrier, partners + 1 + extra)

    @pl.when((s > 0) & (s < NS - 1))
    def _():
        pl.semaphore_wait(barrier, partners + 2 + extra)

    left = pl.ds(0, HALF)
    core = lax.rem(d, 2)
    side = lax.rem(d // 2, 2)

    def u_rows(i, side=side):
        n = jnp.where(i < 2, 8 * side, 0) + 2 * i + core
        return pl.ds(pl.multiple_of(n * piece, piece), piece)

    def u_from_section(i):
        return pltpu.make_async_remote_copy(
            slab_hbm.at[0, u_rows(i), pl.ds(FF, HALF)],
            u.at[u_rows(i), left],
            u_send.at[0, i],
            u_recv.at[0, i],
            device_id=(s + 1, d),
            device_id_type=MESH,
        )

    def u_copy_to(rows, i, k, to):
        return pltpu.make_async_remote_copy(
            u.at[rows, left],
            u.at[rows, left],
            u_send.at[k, i],
            u_recv.at[k, i],
            device_id=(s, to),
            device_id_type=MESH,
        )

    detour = (2, 3) if NS == 4 else ()

    def u_aside(i, to, k):
        src = slab_hbm.at[0, u_rows(i), pl.ds(FF, HALF)] if k == 0 else u.at[u_rows(i), left]
        return pltpu.make_async_remote_copy(
            src,
            u.at[u_rows(i), left],
            u_send.at[k, i],
            u_recv.at[0, i],
            device_id=(to, d),
            device_id_type=MESH,
        )

    @pl.when(first)
    def _():
        for i in range(pieces):
            if i in detour:
                u_aside(i, 2, 0).start()
            else:
                u_from_section(i).start()

    @pl.when(is_attn & (s > 0) & (s < NS - 1))
    def _():
        for i in detour:
            u_aside(i, 1, 1).wait_recv()
            u_aside(i, 1, 1).start()
        for i in detour:
            u_aside(i, 1, 1).wait_send()
        for i in range(pieces):
            u_from_section(i).start()

    def turn(src, dst, start, count):
        for i in range(start, start + count):
            dst[pl.ds(256 * i, 256), :] = src[:, pl.ds(256 * i, 256)].T

    w_copy.wait()
    late_turn = first

    @pl.when(is_attn)
    def _():
        turn(w, wt, 3 * D // 256, D // 256)
        draws_copy.wait()
        f_row = lax.broadcasted_iota(jnp.int32, (FE, GF), 0)
        f_col = lax.broadcasted_iota(jnp.int32, (FE, GF), 1)
        for n in range(G * GH):
            shift = jnp.where(f_col == f_row + n % GH * FE, 1.0, 0.0).astype(bf16)
            spread = dot(draws_ref[n].astype(f32).astype(bf16), shift)
            fmap_ref[n // GH, pl.ds(n % GH * HD, HD), :] = spread.astype(bf16)

    @pl.when(s == 2)
    def _():
        turn(w, wt, 0, 3 * D // 256)

    @pl.when(is_ff)
    def _():
        turn(w, wt, 0, FF // 256)
        u_copy.wait()
        turn(u, ut, HALF // 256, HALF // 256)
        for i in range(pieces):
            u_from_section(i).wait_recv()
            if i < 2:
                u_copy_to(u_rows(i), i, 1, mate).start()
            u_copy_to(u_rows(i), i, 2, sib).start()
            if i >= 2:
                u_copy_to(u_rows(i - 2, 1 - side), i - 2, 1, mate).wait_recv()
                u_copy_to(u_rows(i - 2, 1 - side), i - 2, 3, sib).start()
        for i in range(pieces):
            u_copy_to(u_rows(i), i, 2, sib).wait_recv()
        for i in range(2):
            u_copy_to(u_rows(i, 1 - side), i, 3, sib).wait_recv()
        turn(u, ut, 0, HALF // 256)

    g_row = gain_ref[...]
    b_row = shift_ref[...]
    head_mask = block_mask(GF, 256, FE, HD)
    pair_mask = jnp.concatenate([head_mask, head_mask], axis=1)

    def sz_at(m, g):
        n = m * G + g
        r = pl.multiple_of(lax.rem(n, D // GF) * GF, GF)
        c = pl.multiple_of(n // (D // GF) * 512, 512)
        return (pl.ds(r, GF), pl.ds(c, 512))

    def valid_rows(m, rows):
        at = lax.broadcasted_iota(jnp.int32, (rows.size, GF), 0) + rows.start
        return at < len_ref[m]

    def with_ones(v):
        return jnp.concatenate([v, jnp.ones(v.shape, bf16)], axis=1)

    def norm_forward(m, rows, pre):
        mean = jnp.mean(pre, axis=-1, keepdims=True)
        cen = pre - mean
        r = lax.rsqrt(jnp.mean(cen * cen, axis=-1, keepdims=True) + norm_epsilon)
        n = cen * r
        nbuf[m, rows, :] = n
        rbuf[m, rows, :] = r
        out[m, rows, :] = (n * g_row + b_row).astype(bf16)

    def norm_backward(m, rows):
        dy = dyin[m, rows, :].astype(f32)
        n = nbuf[m, rows, :]
        dn = dy * g_row
        m1 = jnp.mean(dn, axis=-1, keepdims=True)
        m2 = jnp.mean(dn * n, axis=-1, keepdims=True)
        gain_grad_ref[...] += jnp.sum(dy * n, axis=0, keepdims=True)
        shift_grad_ref[...] += jnp.sum(dy, axis=0, keepdims=True)
        dpre = rbuf[m, rows, :] * (dn - m1 - n * m2)
        dbr[m, rows, :] = dpre.astype(bf16)
        return dpre

    def next_copy(m, h):
        return pltpu.make_async_remote_copy(
            out.at[m, halves[h]],
            xin.at[m, halves[h]],
            f_send.at[m, h],
            f_recv.at[m, h],
            device_id=(s + 1, d),
            device_id_type=MESH,
        )

    def back_copy(m, h):
        return pltpu.make_async_remote_copy(
            dxo.at[m, halves[h]],
            dyin.at[m, halves[h]],
            b_send.at[m, h],
            b_recv.at[m, h],
            device_id=(s - 1, d),
            device_id_type=MESH,
        )

    def relay_at(m, h):
        start = pl.multiple_of(m * LP + halves[h].start, 16)
        return ut.at[pl.ds(start, halves[h].size)]

    def relay_in(m, h):
        return pltpu.make_async_remote_copy(
            dxo.at[m, halves[h]],
            relay_at(m, h),
            b_send.at[m, h],
            f_recv.at[m, h],
            device_id=(0, d),
            device_id_type=MESH,
        )

    def relay_on(m, h):
        return pltpu.make_async_remote_copy(
            relay_at(m, h),
            dyin.at[m, halves[h]],
            b_send.at[m, h],
            b_recv.at[m, h],
            device_id=(1, d),
            device_id_type=MESH,
        )

    def send_next(m, h):
        if h == 0:
            @pl.when(is_attn & (m == 0))
            def _():
                for i in range(pieces):
                    u_from_section(i).wait_send()

        @pl.when(s < NS - 1)
        def _():
            next_copy(m, h).start()

    def by_relay(m):
        return (s == 2) & (m >= relay_lo) & (m < relay_hi)

    def send_back(m, h):
        @pl.when((s > 0) & jnp.logical_not(by_relay(m)))
        def _():
            back_copy(m, h).start()

        @pl.when(by_relay(m))
        def _():
            relay_in(m, h).start()

    v_at = [pl.ds(256 * g, 256) for g in range(G)]
    fq_at = [pl.ds(D + GF * g, GF) for g in range(G)]
    fk_at = [pl.ds(D + GF * (G + g), GF) for g in range(G)]
    out_at = pl.ds(3 * D, D)

    def attend_features(m, rows):
        x = xin[m, rows, :]
        valid = valid_rows(m, rows)
        for g in range(G):
            qkv = [
                (dot(x, w[:, c]) + bias_ref[:, c]).astype(bf16)
                for c in (pl.ds(k * D + 256 * g, 256) for k in range(3))
            ]
            fq = softplus(dot(qkv[0], fmap_ref[g]) * fscale).astype(bf16)
            fk = softplus(dot(qkv[1], fmap_ref[g]) * fscale)
            buf_a[m, rows, v_at[g]] = qkv[2]
            buf_a[m, rows, fq_at[g]] = fq
            buf_a[m, rows, fk_at[g]] = jnp.where(valid, fk, 0.0).astype(bf16)

    def summaries(m):
        for g in range(G):
            sz = dot_rows(buf_a[m, :, fk_at[g]], with_ones(buf_a[m, :, v_at[g]]))
            u[sz_at(m, g)] = jnp.where(pair_mask, sz, 0.0).astype(bf16)

    def attend_mix(m, rows):
        for g in range(G):
            nd = dot(buf_a[m, rows, fq_at[g]], u[sz_at(m, g)])
            mixed = (nd[:, :256] / nd[:, 256:]).astype(bf16)
            buf_a[m, rows, pl.ds(3 * D + 256 * g, 256)] = mixed
        branch = dot(buf_a[m, rows, out_at], wt[out_at, :]) + bias_ref[:, out_at]
        norm_forward(m, rows, xin[m, rows, :].astype(f32) + branch)

    def attend_forward(m, mode):
        if mode == 2:
            attend_features(m, whole)
            summaries(m)
            attend_mix(m, whole)
            send_next(m, 0)
            send_next(m, 1)
            return
        attend_features(m, halves[mode])
        if mode == 1:
            summaries(m)
            for part, rows in enumerate(halves):
                attend_mix(m, rows)
                send_next(m, part)

    def feed_forward(m, mode):
        rows = (halves + (whole,))[mode]
        x = xin[m, rows, :]
        tile = 512
        for j in range(FF // tile):
            c = pl.ds(j * tile, tile)
            a = dot(x, w[:, c]) + bias_ref[:, c]
            cdf = 0.5 + 0.5 * lax.erf(a * 0.7071067811865476)
            pdf = jnp.exp(a * a * -0.5) * 0.3989422804014327
            buf_a[m, rows, c] = (a * cdf).astype(bf16)
            buf_b[m, rows, c] = (cdf + a * pdf).astype(bf16)
        branch = dot(buf_a[m, rows, :], ut[...])
        norm_forward(m, rows, x.astype(f32) + branch)
        for h in (mode,) if mode < 2 else (0, 1):
            send_next(m, h)

    def attend_backward(m, mode):
        rows = (halves + (whole,))[mode]
        dpre = norm_backward(m, rows)
        nbuf[m, rows, :] = dpre
        db = dbr[m, rows, :]
        bias_grad_ref[:, out_at] += jnp.sum(db.astype(f32), axis=0, keepdims=True)

        def store(rows, k, g, val):
            c = pl.ds(k * D + 256 * g, 256)
            buf_b[m, rows, c] = val
            bias_grad_ref[:, c] += jnp.sum(val.astype(f32), axis=0, keepdims=True)

        for g in range(G):
            dmix = dot(db, w[:, pl.ds(3 * D + 256 * g, 256)])
            fq = buf_a[m, rows, fq_at[g]]
            sz = u[sz_at(m, g)]
            nd = dot(fq, sz)
            rden = 1.0 / nd[:, 256:]
            dnum = dmix * rden
            dden = -dnum * (nd[:, :256] * rden)
            de = jnp.concatenate([dnum, dden], axis=1).astype(bf16)
            buf_b[m, rows, pl.ds(D + 512 * g, 512)] = de
            duq = dot_cols(de, sz) * (1.0 - jnp.exp(-fq.astype(f32)))
            dq = (dot_cols(duq.astype(bf16), fmap_ref[g]) * fscale).astype(bf16)
            store(rows, 0, g, dq)
        if mode == 0:
            return
        for g in range(G):
            dsz = dot_rows(buf_a[m, :, fq_at[g]], buf_b[m, :, pl.ds(D + 512 * g, 512)])
            u[sz_at(m, g)] = jnp.where(pair_mask, dsz, 0.0).astype(bf16)
        for part, rows in enumerate(halves if mode == 1 else (whole,)):
            valid = valid_rows(m, rows)
            for g in range(G):
                dsz = u[sz_at(m, g)]
                fk = buf_a[m, rows, fk_at[g]]
                dfk = dot_cols(with_ones(buf_a[m, rows, v_at[g]]), dsz)
                duk = jnp.where(valid, dfk, 0.0) * (1.0 - jnp.exp(-fk.astype(f32)))
                dk = (dot_cols(duk.astype(bf16), fmap_ref[g]) * fscale).astype(bf16)
                store(rows, 1, g, dk)
                store(rows, 2, g, dot(fk, dsz[:, :256]).astype(bf16))
            inner = pl.ds(0, 3 * D)
            dx = nbuf[m, rows, :] + dot(buf_b[m, rows, inner], wt[inner, :])
            dxo[m, rows, :] = dx.astype(bf16)
            for h in (part,) if mode == 1 else (0, 1):
                send_back(m, h)

    def feed_backward(m, mode):
        rows = (halves + (whole,))[mode]
        dpre = norm_backward(m, rows)
        db = dbr[m, rows, :]
        tile = 512
        for j in range(FF // tile):
            c = pl.ds(j * tile, tile)
            da = (dot(db, u[:, c]) * buf_b[m, rows, c].astype(f32)).astype(bf16)
            buf_b[m, rows, c] = da
            bias_grad_ref[:, c] += jnp.sum(da.astype(f32), axis=0, keepdims=True)
        dx = dpre + dot(buf_b[m, rows, :], wt[...])
        dxo[m, rows, :] = dx.astype(bf16)
        for h in (mode,) if mode < 2 else (0, 1):
            send_back(m, h)

    def out_copy(m):
        return pltpu.make_async_copy(out_stage, out_hbm.at[m], stage_sem.at[0])

    def grad_copy(m):
        return pltpu.make_async_copy(grad_stage, grad_hbm.at[m], stage_sem.at[1])

    def write_out(copy, rows, staged, m):
        @pl.when(m >= 1)
        def _():
            copy(m - 1).wait()

        staged[...] = rows[m, pl.ds(0, L), :]
        copy(m).start()

    pad_zero = jnp.zeros((LP - L, D), bf16)
    eye = lax.broadcasted_iota(jnp.int32, (L, L), 0) == lax.broadcasted_iota(jnp.int32, (L, L), 1)

    def forward_step(m, mode):
        if mode != 1:
            @pl.when(first)
            def _():
                land_copy(x_hbm, m).wait()
                xin[m] = jnp.concatenate([land[lax.rem(m, 2)], pad_zero], axis=0)

                @pl.when(m + 2 < M)
                def _():
                    land_copy(x_hbm, m + 2).start()

        @pl.when(s > 0)
        def _():
            for h in (mode,) if mode < 2 else (0, 1):
                next_copy(m, h).wait_recv()

        @pl.when(is_attn)
        def _():
            attend_forward(m, mode)

        @pl.when(is_ff)
        def _():
            feed_forward(m, mode)

        if mode > 0:
            write_out(out_copy, out, out_stage, m)
        if mode > 0:
            @pl.when(first & (m == M - 1))
            def _():
                turn(w, wt, 0, 3 * D // 256)

    def backward_step(m, mode):
        if mode != 1:
            @pl.when(last)
            def _():
                land_copy(cot_hbm, m).wait()
                row = jnp.where(
                    lax.broadcasted_iota(jnp.int32, (1, L), 1) < len_ref[m],
                    pred_ref[pl.ds(m, 1), :].astype(f32),
                    0.0,
                )
                col = jnp.sum(jnp.where(eye, row, 0.0), axis=1, keepdims=True)
                masked = (land[lax.rem(m, 2)].astype(f32) * col).astype(bf16)
                dyin[m] = jnp.concatenate([masked, pad_zero], axis=0)

                @pl.when(m + 2 < M)
                def _():
                    land_copy(cot_hbm, m + 2).start()

        @pl.when(s < NS - 1)
        def _():
            for h in (mode,) if mode < 2 else (0, 1):
                back_copy(m, h).wait_recv()

        @pl.when(is_attn)
        def _():
            attend_backward(m, mode)

        @pl.when(is_ff)
        def _():
            feed_backward(m, mode)

        if mode > 0:
            write_out(grad_copy, dxo, grad_stage, m)

    back_start = jnp.where(s == 0, 16, jnp.where(s == 1, 12, jnp.where(s == 2, 10, 6)))
    relay_start = 12

    def when_due(start, act):
        def at(t):
            i = t - start
            m = i // 2

            apart = i < 0
            for n in SPLIT:
                apart = apart | (m == n % M)
            here = (i >= 0) & (i < 2 * M)

            @pl.when(here & jnp.logical_not(apart) & (lax.rem(i, 2) == 1))
            def _():
                act(m, 2)

            for h in range(2 if SPLIT else 0):
                @pl.when(here & apart & (lax.rem(i, 2) == h))
                def _():
                    act(m, h)

        return at

    forward_at = when_due(2 * s, forward_step)
    backward_at = when_due(back_start, backward_step)

    def tick(t, carry):
        forward_at(t)
        if relayed > 0:
            i = t - relay_start
            for h in range(2):
                @pl.when((s == 0) & (i >= 0) & (i < 2 * relayed) & (lax.rem(i, 2) == h))
                def _():
                    relay_in(relay_lo + i // 2, h).wait_recv()
                    relay_on(relay_lo + i // 2, h).start()
        backward_at(t)
        return carry

    lax.fori_loop(0, 28, tick, 0)

    if relayed > 0:
        @pl.when(s == 0)
        def _():
            for m in range(relay_lo, relay_hi):
                for h in range(2):
                    relay_on(m, h).wait_send()

    @pl.when(is_ff)
    def _():
        for i in range(pieces):
            u_copy_to(u_rows(i), i, 2, sib).wait_send()
        for i in range(2):
            u_copy_to(u_rows(i), i, 1, mate).wait_send()
            u_copy_to(u_rows(i, 1 - side), i, 3, sib).wait_send()

    if in_kernel:
        reduce_gradients(
            cfg,
            s,
            d,
            odd,
            w,
            u,
            wt,
            ut,
            xin,
            dbr,
            buf_a,
            buf_b,
            g_hbm,
            small_ref,
            small_outs,
            *reduce_refs,
        )
    else:
        plain_gradients(cfg, odd, xin, dbr, buf_a, buf_b, g_hbm, g_sem, *reduce_refs)

    for m in range(M):
        for h in range(2):
            @pl.when(s < NS - 1)
            def _():
                next_copy(m, h).wait_send()

            @pl.when(s > 0)
            def _():
                back_copy(m, h).wait_send()

    out_copy(M - 1).wait()
    grad_copy(M - 1).wait()


def shards(
    block_input, cotangent, lengths, predicted, slab, in_bias, norm_gain, norm_bias, feature_draws
):
    NS = lax.axis_size("section")
    ND = lax.axis_size("dp")
    M, L, D = block_input.shape
    FF = in_bias.shape[1]
    H, HD, FE = feature_draws.shape
    LP = (L + 15) // 16 * 16
    GH = 256 // HD
    G = D // 256
    GF = GH * FE
    fscale = float((3.0 / (20.0 * HD)) ** 0.5)
    in_kernel = D // ND % 32 == 0 and NS == 4
    C = CHUNK if in_kernel else D
    cfg = (M, L, LP, D, FF, HD, FE, NS, ND, fscale, in_kernel, C)
    hbm = pl.BlockSpec(memory_space=pl.ANY)
    vmem = pl.BlockSpec(memory_space=pltpu.VMEM)
    smem = pl.BlockSpec(memory_space=pltpu.SMEM)
    dma = pltpu.SemaphoreType.DMA
    rows_bf = pltpu.VMEM((M, LP, D), bf16)
    wide_bf = pltpu.VMEM((M, LP, FF), bf16)
    small_size = FF + 2 * D
    smalls = [FF // ND, D // ND, D // ND] if in_kernel else [small_size]
    scratch = [pltpu.VMEM((1, small_size), f32)] if in_kernel else []
    scratch += [
        pltpu.VMEM((G, GH * HD, GF), bf16),
        pltpu.VMEM((H, HD, FE), jnp.int32),
        pltpu.VMEM((D, FF), bf16),
        pltpu.VMEM((D, FF), bf16),
        pltpu.VMEM((FF, D), bf16),
        pltpu.VMEM((FF, D), bf16),
        rows_bf,
        rows_bf,
        rows_bf,
        rows_bf,
        rows_bf,
        pltpu.VMEM((M, LP, D), f32),
        pltpu.VMEM((M, LP, 1), f32),
        wide_bf,
        wide_bf,
        pltpu.VMEM((2, L, D), bf16),
        pltpu.VMEM((L, D), bf16),
        pltpu.VMEM((L, D), bf16),
        dma((3,)),
        dma((2,)),
        dma((4, 4)),
        dma((4, 4)),
        dma((M, 2)),
        dma((M, 2)),
        dma((M, 2)),
        dma((M, 2)),
        dma((2,)),
        dma((1,)),
    ]
    if in_kernel:
        Z, B, chunks = ND // 2, D // ND, 2 * FF // C
        cross = FF // C // 2
        lines = chunks
        scratch += [
            pltpu.SemaphoreType.REGULAR((3,)),
            pltpu.VMEM((Z + 1, Z * B, C), f32),
            pltpu.VMEM((2, Z * B, C), bf16),
            pltpu.VMEM((cross + 1, Z * B, C), bf16),
            pltpu.VMEM((2, Z, B, C), bf16),
            pltpu.VMEM((2, B, C), f32),
            pltpu.VMEM((ND, 1, small_size), f32),
            dma((2,)),
            dma((chunks,)),
            dma((2, Z)),
            dma((lines, Z)),
            dma((lines, Z)),
            dma((2,)),
            dma((cross + 1,)),
            dma((cross + 1,)),
            dma((cross + 1,)),
            dma((cross + 1,)),
            dma((ND,)),
            dma((ND,)),
        ]
        g_shape = (B, FF + FF // 2)
    else:
        scratch += [pltpu.VMEM((D, D), f32)]
        g_shape = (D, 2 * FF)
    section_out, section_grad, grads, *small = pl.pallas_call(
        functools.partial(pipeline_kernel, cfg),
        out_shape=[
            jax.ShapeDtypeStruct((M, L, D), bf16),
            jax.ShapeDtypeStruct((M, L, D), bf16),
            jax.ShapeDtypeStruct(g_shape, f32),
        ]
        + [jax.ShapeDtypeStruct((1, n), f32) for n in smalls],
        in_specs=[smem, hbm, hbm, vmem, hbm, vmem, vmem, vmem, hbm],
        out_specs=[hbm, hbm, hbm] + [vmem] * len(smalls),
        scratch_shapes=scratch,
        compiler_params=pltpu.CompilerParams(
            collective_id=0, has_side_effects=True, vmem_limit_bytes=62 * 2**20
        ),
        name="pipeline",
    )(
        lengths,
        block_input,
        cotangent,
        predicted,
        slab,
        in_bias,
        norm_gain,
        norm_bias,
        feature_draws,
    )
    if in_kernel:
        own = grads
        parts = small
    else:
        def scatter(value):
            return lax.psum_scatter(value, "dp", scatter_dimension=0, tiled=True)

        HALF = FF // 2
        both = scatter(grads)
        sums = small[0][0]
        parts = [scatter(v)[None] for v in (sums[:FF], sums[FF : FF + D], sums[FF + D :])]
        is_attention = lax.axis_index("section") % 2 == 0
        turned = jnp.where(
            is_attention,
            jnp.concatenate([both[:, D:FF], both[:, :D], both[:, FF:]], axis=1),
            jnp.concatenate([both[:, FF:], both[:, :FF]], axis=1),
        )
        pairs = [(i, i - 1) for i in range(1, NS, 2)]
        arrived = lax.ppermute(turned[:, FF : FF + HALF], "section", pairs)
        rest = jnp.where(is_attention, arrived, turned[:, FF + HALF :])
        own = jnp.concatenate([turned[:, :FF], rest], axis=1)
    return (
        section_out[None],
        section_grad[None],
        own[None],
        *parts,
    )


def solution(mesh):
    placed = (
        P("dp", None, None),
        P("dp", None, None),
        P("dp"),
        P("dp", None),
        P("section", None, None),
        P("section", None),
        P("section", None),
        P("section", None),
        P(),
    )
    return jax.shard_map(
        shards,
        mesh=mesh,
        in_specs=placed,
        out_specs=(
            P("section", "dp", None, None),
            P("section", "dp", None, None),
            P("section", "dp", None),
            P("section", "dp"),
            P("section", "dp"),
            P("section", "dp"),
        ),
        check_vma=False,
    )
```

```python
import functools

import jax
import jax.numpy as jnp
from jax import lax
from jax.experimental import pallas as pl
from jax.experimental.pallas import tpu as pltpu
from jax.sharding import PartitionSpec as P

MESH = pl.DeviceIdType.MESH
CHUNK = 384
RELAYED = (0, 3)
SPLIT = ()
norm_epsilon = 1e-05
bf16 = jnp.bfloat16
f32 = jnp.float32


def dot(a, b):
    return lax.dot_general(a, b, (((1,), (0,)), ((), ())), preferred_element_type=f32)


def dot_cols(a, b):
    return lax.dot_general(a, b, (((1,), (1,)), ((), ())), preferred_element_type=f32)


def dot_rows(a, b):
    return lax.dot_general(a, b, (((0,), (0,)), ((), ())), preferred_element_type=f32)


def softplus(u):
    return jnp.maximum(u, 0.0) + jnp.log1p(jnp.exp(-jnp.abs(u)))


def block_mask(feature_rows, value_cols, features, head_dim):
    r = lax.broadcasted_iota(jnp.int32, (feature_rows, value_cols), 0) // features
    c = lax.broadcasted_iota(jnp.int32, (feature_rows, value_cols), 1) // head_dim
    return r == c


def flat(ref, c):
    return ref[:, :, c].reshape(ref.shape[0] * ref.shape[1], c.size)


def column(k, D):
    return pl.ds(pl.multiple_of(k * D, D), D)


def chunk_counts(cfg, odd):
    D, FF, C = cfg[3], cfg[4], cfg[-1]
    wide = FF // C
    return D // C + (wide - D // C) * odd, wide + wide * odd


def plain_gradients(cfg, odd, xin, dbr, buf_a, buf_b, g_hbm, g_sem, stage):
    D, FF, C = cfg[3], cfg[4], cfg[-1]
    first_kind, count = chunk_counts(cfg, odd)
    wide = FF // C
    own = D // C

    def store(k):
        cp = pltpu.make_async_copy(stage, g_hbm.at[:, column(k, C)], g_sem.at[0])
        cp.start()
        cp.wait()

    def one(k, carry):
        @pl.when(k < first_kind)
        def _():
            src = column(k + (wide - own) * (1 - odd), C)
            stage[...] = dot_rows(flat(dbr, pl.ds(0, D)), flat(buf_a, src))
            store(k)

        @pl.when(k >= first_kind)
        def _():
            stage[...] = dot_rows(flat(xin, pl.ds(0, D)), flat(buf_b, column(k - first_kind, C)))
            store(k)

        return carry

    lax.fori_loop(0, count, one, 0)

    @pl.when(odd == 0)
    def _():
        stage[...] = jnp.zeros_like(stage)

        def rest(k, carry):
            store(k)
            return carry

        lax.fori_loop(wide, 2 * wide, rest, 0)


def reduce_gradients(
    cfg,
    s,
    d,
    odd,
    w,
    u,
    wt,
    ut,
    xin,
    dbr,
    buf_a,
    buf_b,
    g_hbm,
    small_ref,
    small_outs,
    ready,
    keep,
    core_out,
    cross_out,
    line_out,
    final,
    small_in,
    core_send,
    core_recv,
    line_send,
    up_recv,
    down_recv,
    final_sem,
    cross_send,
    cross_recv,
    away_send,
    away_recv,
    small_send,
    small_recv,
):
    M, L, LP, D, FF, HD, FE, NS, ND, fscale, in_kernel, C = cfg
    Z = ND // 2
    B = D // ND
    R = Z * B
    K = M * LP
    wide = FF // C
    own = D // C
    fold = D // C
    keeps = keep.shape[0]
    p = lax.rem(d, 2)
    z = d // 2
    sib = d + 1 - 2 * p
    first_kind, count = chunk_counts(cfg, odd)
    cross = wide // 2
    shipped = cross + 1
    pre = jnp.where(s == 1, shipped, 0)
    came = jnp.where(s == 2, shipped, 0)
    lines = count - pre + came
    dma_to = functools.partial(pltpu.make_async_remote_copy, device_id_type=MESH)

    pl.semaphore_signal(ready.at[0], inc=1, device_id=(s, sib), device_id_type=MESH)

    @pl.when(z > 0)
    def _():
        pl.semaphore_signal(ready.at[2], inc=1, device_id=(s, d - 2), device_id_type=MESH)

    @pl.when(z < Z - 1)
    def _():
        pl.semaphore_signal(ready.at[1], inc=1, device_id=(s, d + 2), device_id_type=MESH)

    def small_copy(o):
        return dma_to(
            small_ref,
            small_in.at[d],
            small_send.at[o],
            small_recv.at[d],
            device_id=(s, lax.rem(d + o, ND)),
        )

    def small_wait(o):
        j = lax.rem(d + o, ND)
        return dma_to(
            small_ref, small_in.at[j], small_send.at[o], small_recv.at[j], device_id=(s, j)
        )

    for o in range(1, ND):
        small_copy(o).start()
    small_in[d] = small_ref[...]

    place_d = pl.ds(0, K)
    place_x = pl.ds((K + 127) // 128 * 128, K)
    for src, at_cols in ((dbr, place_d), (xin, place_x)):
        for i in range(D // 256):
            turned = flat(src, pl.ds(256 * i, 256)).T
            for q in range(8):
                t = 8 * i + q
                block = t * 32 // B
                at = block % 2 * R + block // 2 * B + t * 32 - block * B
                u[pl.ds(at, 32), at_cols] = turned[32 * q : 32 * q + 32]

    per = D // R

    def slot(j):
        return (pl.ds(pl.multiple_of(lax.rem(j, per) * R, 16), R), column(j // per, C))

    def slot_block(j, zt):
        r = pl.multiple_of(lax.rem(j, per) * R + zt * B, 16)
        return (pl.ds(r, B), column(j // per, C))

    def line_place(n, zt):
        r = pl.multiple_of(n // fold * R + zt * B, 16)
        return (pl.ds(r, B), column(lax.rem(n, fold), C))

    def cross_place(c):
        n = 2 * wide - cross + c
        r = pl.multiple_of(n // fold * R, 16)
        return (pl.ds(r, R), column(lax.rem(n, fold), C))

    spare = (pl.ds(0, R), pl.ds(FF - (C + 127) // 128 * 128, C))

    def core_copy(j):
        return dma_to(
            core_out.at[lax.rem(j, 2)],
            w.at[slot(j)],
            core_send.at[lax.rem(j, 2)],
            core_recv.at[j],
            device_id=(s, sib),
        )

    def cross_copy(c):
        return dma_to(
            cross_out.at[c],
            ut.at[cross_place(c)],
            cross_send.at[c],
            cross_recv.at[c],
            device_id=(2, d),
        )

    def spare_copy():
        return dma_to(
            cross_out.at[cross],
            u.at[spare],
            cross_send.at[cross],
            cross_recv.at[cross],
            device_id=(2, d),
        )

    def up_copy(n, zt):
        return dma_to(
            line_out.at[lax.rem(n, 2), zt],
            ut.at[line_place(n, zt)],
            line_send.at[lax.rem(n, 2), zt],
            up_recv.at[n, zt],
            device_id=(s, d + 2),
        )

    def down_copy(n, zt):
        return dma_to(
            line_out.at[lax.rem(n, 2), zt],
            wt.at[line_place(n, zt)],
            line_send.at[lax.rem(n, 2), zt],
            down_recv.at[n, zt],
            device_id=(s, d - 2),
        )

    def final_copy(n):
        j = n + pre
        early = j + cross * odd + (wide - own) * (1 - odd)
        at = jnp.where(j < first_kind, early, j - first_kind)
        return pltpu.make_async_copy(
            final.at[lax.rem(n, 2)], g_hbm.at[:, column(at, C)], final_sem.at[lax.rem(n, 2)]
        )

    def away(n):
        return ((s == 3) & (n < cross)) | ((s == 2) & (n >= count))

    def away_copy(n):
        c = n - jnp.where(s == 2, count, 0)
        to = jnp.where(s == 3, 2, c // cross)
        return dma_to(
            final.at[lax.rem(n, 2)],
            g_hbm.at[:, column(wide + lax.rem(c, cross), C)],
            away_send.at[lax.rem(n, 2)],
            away_recv.at[c],
            device_id=(to, d),
        )

    def away_arrival(c):
        return dma_to(
            final.at[0],
            g_hbm.at[:, column(wide + c % cross, C)],
            away_send.at[0],
            away_recv.at[c],
            device_id=(jnp.where(s == 3, 2, 0), d),
        )

    def final_wait(n):
        @pl.when(away(n))
        def _():
            away_copy(n).wait_send()

        @pl.when(jnp.logical_not(away(n)))
        def _():
            final_copy(n).wait()

    def total(n, zt):
        j = n + pre
        return keep[lax.rem(j, keeps), pl.ds(zt * B, B), :] + w[slot_block(j, zt)].astype(f32)

    near = jnp.minimum(z, Z - 1 - z)
    far = jnp.maximum(z, Z - 1 - z)

    def make(k):
        sl = lax.rem(k, 2)

        def products(place, right):
            @pl.when(k >= 2)
            def _():
                core_copy(k - 2).wait_send()

            theirs = pl.ds(pl.multiple_of((1 - p) * R, 16), R)
            mine = pl.ds(pl.multiple_of(p * R, 16), R)
            core_out[sl] = dot(u[theirs, place], right).astype(bf16)

            @pl.when(k == 0)
            def _():
                pl.semaphore_wait(ready.at[0], 1)

            core_copy(k).start()
            keep[lax.rem(k, keeps)] = dot(u[mine, place], right)

        @pl.when(k < first_kind)
        def _():
            products(place_d, flat(buf_a, column(k + (wide - own) * (1 - odd), C)))

        @pl.when(k >= first_kind)
        def _():
            products(place_x, flat(buf_b, column(k - first_kind, C)))

    def fetch(k):
        c = k - count

        @pl.when(c < cross)
        def _():
            cross_copy(c).wait_recv()
            keep[lax.rem(k, keeps)] = ut[cross_place(c)].astype(f32)

        @pl.when(c == cross)
        def _():
            spare_copy().wait_recv()
            keep[lax.rem(k, keeps)] = u[spare].astype(f32)

        w[slot(k)] = jnp.zeros((R, C), bf16)

    def ship(c):
        core_copy(c).wait_recv()
        both = keep[lax.rem(c, keeps)] + w[slot(c)].astype(f32)
        cross_out[c] = both.astype(bf16)

        @pl.when(c < cross)
        def _():
            cross_copy(c).start()

        @pl.when(c == cross)
        def _():
            spare_copy().start()

    def step(own_pass, lo, hi, k, carry):
        if own_pass:
            @pl.when(k < count)
            def _():
                make(k)

            @pl.when((k >= 1) & (k - 1 < pre))
            def _():
                ship(k - 1)
        else:
            @pl.when(k < count + came)
            def _():
                fetch(k)

        n_near = k - 1 - pre - near

        if own_pass:
            @pl.when((n_near >= lo) & (n_near < hi))
            def _():
                core_copy(n_near + pre).wait_recv()

        n_up = k - 1 - pre - z

        @pl.when((n_up >= lo) & (n_up < hi) & (z < Z - 1))
        def _():
            @pl.when(n_up == 0)
            def _():
                pl.semaphore_wait(ready.at[2], 1)

            for zt in range(Z - 1, 0, -1):
                @pl.when(zt > z)
                def _():
                    @pl.when(n_up >= 2)
                    def _():
                        up_copy(n_up - 2, zt).wait_send()

                    @pl.when(z > 0)
                    def _():
                        up_copy(n_up, zt).wait_recv()
                        line_out[lax.rem(n_up, 2), zt] = (
                            total(n_up, zt) + ut[line_place(n_up, zt)].astype(f32)
                        ).astype(bf16)

                    @pl.when(z == 0)
                    def _():
                        line_out[lax.rem(n_up, 2), zt] = total(n_up, zt).astype(bf16)

                    up_copy(n_up, zt).start()

        n_down = k - 1 - pre - (Z - 1 - z)

        @pl.when((n_down >= lo) & (n_down < hi) & (z > 0))
        def _():
            @pl.when(n_down == 0)
            def _():
                pl.semaphore_wait(ready.at[1], 1)

            for zt in range(Z - 1):
                @pl.when(zt < z)
                def _():
                    @pl.when(n_down >= 2)
                    def _():
                        down_copy(n_down - 2, zt).wait_send()

                    @pl.when(z < Z - 1)
                    def _():
                        down_copy(n_down, zt).wait_recv()
                        line_out[lax.rem(n_down, 2), zt] = (
                            total(n_down, zt) + wt[line_place(n_down, zt)].astype(f32)
                        ).astype(bf16)

                    @pl.when(z == Z - 1)
                    def _():
                        line_out[lax.rem(n_down, 2), zt] = total(n_down, zt).astype(bf16)

                    down_copy(n_down, zt).start()

        n_own = k - 1 - pre - far

        @pl.when((n_own >= lo) & (n_own < hi))
        def _():
            sl = lax.rem(n_own, 2)

            @pl.when(n_own >= 2)
            def _():
                final_wait(n_own - 2)

            final[sl] = total(n_own, z)

            @pl.when(z > 0)
            def _():
                up_copy(n_own, z).wait_recv()
                final[sl] += ut[line_place(n_own, z)].astype(f32)

            @pl.when(z < Z - 1)
            def _():
                down_copy(n_own, z).wait_recv()
                final[sl] += wt[line_place(n_own, z)].astype(f32)

            @pl.when(away(n_own))
            def _():
                away_copy(n_own).start()

            @pl.when(jnp.logical_not(away(n_own)))
            def _():
                final_copy(n_own).start()

        return carry

    own_lines = count - pre
    lax.fori_loop(0, count + 1 + far, functools.partial(step, True, 0, own_lines), 0)
    later = jnp.where(s == 2, count + came + 1 + far, count)
    lax.fori_loop(count, later, functools.partial(step, False, count, count + came), 0)

    for back in (2, 1):
        core_copy(count - back).wait_send()
        n = lines - back
        for zt in range(Z):
            @pl.when(zt > z)
            def _():
                up_copy(n, zt).wait_send()

            @pl.when(zt < z)
            def _():
                down_copy(n, zt).wait_send()

        final_wait(n)

    @pl.when(s == 1)
    def _():
        for c in range(cross):
            cross_copy(c).wait_send()
        spare_copy().wait_send()
        away_arrival(cross).wait_recv()

    @pl.when(odd == 0)
    def _():
        for c in range(cross):
            away_arrival(c).wait_recv()

    for o in range(1, ND):
        small_wait(o).wait_recv()
        small_copy(o).wait_send()
    acc = small_in[0]
    for j in range(1, ND):
        acc = acc + small_in[j]
    small_ref[...] = acc
    bias_out, gain_out, shift_out = small_outs
    P = FF // ND
    bias_out[...] = small_ref[:, pl.ds(pl.multiple_of(d * P, 128), P)]
    for j in range(ND):
        @pl.when(d == j)
        def _():
            gain_out[...] = acc[:, FF + B * j : FF + B * j + B]
            shift_out[...] = acc[:, FF + D + B * j : FF + D + B * j + B]


def pipeline_kernel(
    cfg,
    len_ref,
    x_hbm,
    cot_hbm,
    pred_ref,
    slab_hbm,
    bias_ref,
    gain_ref,
    shift_ref,
    draws_hbm,
    out_hbm,
    grad_hbm,
    g_hbm,
    *refs,
):
    M, L, LP, D, FF, HD, FE, NS, ND, fscale, in_kernel, C = cfg
    small_outs = refs[:3] if in_kernel else ()
    small_ref = refs[3] if in_kernel else refs[0]
    fmap_ref, draws_ref = refs[4:6] if in_kernel else refs[1:3]
    (
        w,
        u,
        wt,
        ut,
        xin,
        out,
        dyin,
        dxo,
        dbr,
        nbuf,
        rbuf,
        buf_a,
        buf_b,
        land,
        out_stage,
        grad_stage,
        load_sem,
        x_sem,
        u_send,
        u_recv,
        f_send,
        f_recv,
        b_send,
        b_recv,
        stage_sem,
        g_sem,
        *reduce_refs,
    ) = refs[6:] if in_kernel else refs[3:]
    HALF = FF // 2
    GH = 256 // HD
    G = D // 256
    GF = GH * FE
    top = (LP // 2 + 15) // 16 * 16
    halves = (pl.ds(0, top), pl.ds(top, LP - top))
    whole = pl.ds(0, LP)
    relay_lo, relay_hi = RELAYED if NS == 4 else (0, 0)
    relayed = relay_hi - relay_lo
    s = lax.axis_index("section")
    d = lax.axis_index("dp")
    odd = lax.rem(s, 2)
    is_attn = odd == 0
    is_ff = odd == 1
    first = s == 0
    last = s == NS - 1
    sib = d + 1 - 2 * lax.rem(d, 2)
    mate = d + 2 - 4 * lax.rem(d // 2, 2)
    pieces = 4
    piece = D // 12

    barrier = pltpu.get_barrier_semaphore()

    def greet(cond, ts, td):
        @pl.when(cond)
        def _():
            pl.semaphore_signal(barrier, inc=1, device_id=(ts, td), device_id_type=MESH)

    always = s >= 0
    partners = 2
    if in_kernel:
        partners = ND - 1
        for o in range(1, ND):
            greet(always, s, lax.rem(d + o, ND))
    else:
        greet(always, s, sib)
        greet(always, s, mate)
    greet(s > 0, s - 1, d)
    greet(s < NS - 1, s + 1, d)
    if relayed > 0 or in_kernel:
        greet(s == 0, 2, d)
        greet(s == 2, 0, d)
        extra = jnp.where(lax.rem(s, 2) == 0, 1, 0)
    else:
        extra = 0

    w_copy = pltpu.make_async_copy(slab_hbm.at[0, :, pl.ds(0, FF)], w, load_sem.at[0])
    u_copy = pltpu.make_async_copy(
        slab_hbm.at[0, :, pl.ds(FF, HALF)], u.at[:, pl.ds(HALF, HALF)], load_sem.at[1]
    )
    w_copy.start()
    draws_copy = pltpu.make_async_copy(draws_hbm, draws_ref, load_sem.at[2])

    @pl.when(is_attn)
    def _():
        draws_copy.start()


    def land_copy(ref, m):
        sl = lax.rem(m, 2)
        return pltpu.make_async_copy(ref.at[m], land.at[sl], x_sem.at[sl])

    @pl.when(first)
    def _():
        for m in range(2):
            land_copy(x_hbm, m).start()

    @pl.when(last)
    def _():
        for m in range(2):
            land_copy(cot_hbm, m).start()

    @pl.when(is_ff)
    def _():
        u_copy.start()

    small_ref[...] = jnp.zeros_like(small_ref)
    bias_grad_ref = small_ref.at[:, pl.ds(0, FF)]
    gain_grad_ref = small_ref.at[:, pl.ds(FF, D)]
    shift_grad_ref = small_ref.at[:, pl.ds(FF + D, D)]

    @pl.when(first | last)
    def _():
        pl.semaphore_wait(barrier, partners + 1 + extra)

    @pl.when((s > 0) & (s < NS - 1))
    def _():
        pl.semaphore_wait(barrier, partners + 2 + extra)

    left = pl.ds(0, HALF)
    core = lax.rem(d, 2)
    side = lax.rem(d // 2, 2)

    def u_rows(i, side=side):
        n = jnp.where(i < 2, 8 * side, 0) + 2 * i + core
        return pl.ds(pl.multiple_of(n * piece, piece), piece)

    def u_from_section(i):
        return pltpu.make_async_remote_copy(
            slab_hbm.at[0, u_rows(i), pl.ds(FF, HALF)],
            u.at[u_rows(i), left],
            u_send.at[0, i],
            u_recv.at[0, i],
            device_id=(s + 1, d),
            device_id_type=MESH,
        )

    def u_copy_to(rows, i, k, to):
        return pltpu.make_async_remote_copy(
            u.at[rows, left],
            u.at[rows, left],
            u_send.at[k, i],
            u_recv.at[k, i],
            device_id=(s, to),
            device_id_type=MESH,
        )

    detour = (2, 3) if NS == 4 else ()

    def u_aside(i, to, k):
        src = slab_hbm.at[0, u_rows(i), pl.ds(FF, HALF)] if k == 0 else u.at[u_rows(i), left]
        return pltpu.make_async_remote_copy(
            src,
            u.at[u_rows(i), left],
            u_send.at[k, i],
            u_recv.at[0, i],
            device_id=(to, d),
            device_id_type=MESH,
        )

    @pl.when(first)
    def _():
        for i in range(pieces):
            if i in detour:
                u_aside(i, 2, 0).start()
            else:
                u_from_section(i).start()

    @pl.when(is_attn & (s > 0) & (s < NS - 1))
    def _():
        for i in detour:
            u_aside(i, 1, 1).wait_recv()
            u_aside(i, 1, 1).start()
        for i in detour:
            u_aside(i, 1, 1).wait_send()
        for i in range(pieces):
            u_from_section(i).start()

    def turn(src, dst, start, count):
        for i in range(start, start + count):
            dst[pl.ds(256 * i, 256), :] = src[:, pl.ds(256 * i, 256)].T

    w_copy.wait()
    late_turn = first

    @pl.when(is_attn)
    def _():
        turn(w, wt, 3 * D // 256, D // 256)
        draws_copy.wait()
        f_row = lax.broadcasted_iota(jnp.int32, (FE, GF), 0)
        f_col = lax.broadcasted_iota(jnp.int32, (FE, GF), 1)
        for n in range(G * GH):
            shift = jnp.where(f_col == f_row + n % GH * FE, 1.0, 0.0).astype(bf16)
            spread = dot_rows(draws_ref[n].astype(f32).astype(bf16), shift)
            fmap_ref[n // GH, pl.ds(n % GH * HD, HD), :] = spread.astype(bf16)

    @pl.when(s == 2)
    def _():
        turn(w, wt, 0, 3 * D // 256)

    @pl.when(is_ff)
    def _():
        turn(w, wt, 0, FF // 256)
        u_copy.wait()
        turn(u, ut, HALF // 256, HALF // 256)
        for i in range(pieces):
            u_from_section(i).wait_recv()
            if i < 2:
                u_copy_to(u_rows(i), i, 1, mate).start()
            u_copy_to(u_rows(i), i, 2, sib).start()
            if i >= 2:
                u_copy_to(u_rows(i - 2, 1 - side), i - 2, 1, mate).wait_recv()
                u_copy_to(u_rows(i - 2, 1 - side), i - 2, 3, sib).start()
        for i in range(pieces):
            u_copy_to(u_rows(i), i, 2, sib).wait_recv()
        for i in range(2):
            u_copy_to(u_rows(i, 1 - side), i, 3, sib).wait_recv()
        turn(u, ut, 0, HALF // 256)

    g_row = gain_ref[...]
    b_row = shift_ref[...]
    head_mask = block_mask(GF, 256, FE, HD)
    pair_mask = jnp.concatenate([head_mask, head_mask], axis=1)

    def sz_at(m, g):
        n = m * G + g
        r = pl.multiple_of(lax.rem(n, D // GF) * GF, GF)
        c = pl.multiple_of(n // (D // GF) * 512, 512)
        return (pl.ds(r, GF), pl.ds(c, 512))

    def valid_rows(m, rows):
        at = lax.broadcasted_iota(jnp.int32, (rows.size, GF), 0) + rows.start
        return at < len_ref[m]

    def with_ones(v):
        return jnp.concatenate([v, jnp.ones(v.shape, bf16)], axis=1)

    def norm_forward(m, rows, pre):
        mean = jnp.mean(pre, axis=-1, keepdims=True)
        cen = pre - mean
        r = lax.rsqrt(jnp.mean(cen * cen, axis=-1, keepdims=True) + norm_epsilon)
        n = cen * r
        nbuf[m, rows, :] = n
        rbuf[m, rows, :] = r
        out[m, rows, :] = (n * g_row + b_row).astype(bf16)

    def norm_backward(m, rows):
        dy = dyin[m, rows, :].astype(f32)
        n = nbuf[m, rows, :]
        dn = dy * g_row
        m1 = jnp.mean(dn, axis=-1, keepdims=True)
        m2 = jnp.mean(dn * n, axis=-1, keepdims=True)
        gain_grad_ref[...] += jnp.sum(dy * n, axis=0, keepdims=True)
        shift_grad_ref[...] += jnp.sum(dy, axis=0, keepdims=True)
        dpre = rbuf[m, rows, :] * (dn - m1 - n * m2)
        dbr[m, rows, :] = dpre.astype(bf16)
        return dpre

    def next_copy(m, h):
        return pltpu.make_async_remote_copy(
            out.at[m, halves[h]],
            xin.at[m, halves[h]],
            f_send.at[m, h],
            f_recv.at[m, h],
            device_id=(s + 1, d),
            device_id_type=MESH,
        )

    def back_copy(m, h):
        return pltpu.make_async_remote_copy(
            dxo.at[m, halves[h]],
            dyin.at[m, halves[h]],
            b_send.at[m, h],
            b_recv.at[m, h],
            device_id=(s - 1, d),
            device_id_type=MESH,
        )

    def relay_at(m, h):
        start = pl.multiple_of(m * LP + halves[h].start, 16)
        return ut.at[pl.ds(start, halves[h].size)]

    def relay_in(m, h):
        return pltpu.make_async_remote_copy(
            dxo.at[m, halves[h]],
            relay_at(m, h),
            b_send.at[m, h],
            f_recv.at[m, h],
            device_id=(0, d),
            device_id_type=MESH,
        )

    def relay_on(m, h):
        return pltpu.make_async_remote_copy(
            relay_at(m, h),
            dyin.at[m, halves[h]],
            b_send.at[m, h],
            b_recv.at[m, h],
            device_id=(1, d),
            device_id_type=MESH,
        )

    def send_next(m, h):
        if h == 0:
            @pl.when(is_attn & (m == 0))
            def _():
                for i in range(pieces):
                    u_from_section(i).wait_send()

        @pl.when(s < NS - 1)
        def _():
            next_copy(m, h).start()

    def by_relay(m):
        return (s == 2) & (m >= relay_lo) & (m < relay_hi)

    def send_back(m, h):
        @pl.when((s > 0) & jnp.logical_not(by_relay(m)))
        def _():
            back_copy(m, h).start()

        @pl.when(by_relay(m))
        def _():
            relay_in(m, h).start()

    v_at = [pl.ds(256 * g, 256) for g in range(G)]
    fq_at = [pl.ds(D + GF * g, GF) for g in range(G)]
    fk_at = [pl.ds(D + GF * (G + g), GF) for g in range(G)]
    out_at = pl.ds(3 * D, D)

    def attend_features(m, rows):
        x = xin[m, rows, :]
        valid = valid_rows(m, rows)
        for g in range(G):
            qkv = [
                (dot(x, w[:, c]) + bias_ref[:, c]).astype(bf16)
                for c in (pl.ds(k * D + 256 * g, 256) for k in range(3))
            ]
            fq = softplus(dot(qkv[0], fmap_ref[g]) * fscale).astype(bf16)
            fk = softplus(dot(qkv[1], fmap_ref[g]) * fscale)
            buf_a[m, rows, v_at[g]] = qkv[2]
            buf_a[m, rows, fq_at[g]] = fq
            buf_a[m, rows, fk_at[g]] = jnp.where(valid, fk, 0.0).astype(bf16)

    def summaries(m):
        for g in range(G):
            sz = dot_rows(buf_a[m, :, fk_at[g]], with_ones(buf_a[m, :, v_at[g]]))
            u[sz_at(m, g)] = jnp.where(pair_mask, sz, 0.0).astype(bf16)

    def attend_mix(m, rows):
        for g in range(G):
            nd = dot(buf_a[m, rows, fq_at[g]], u[sz_at(m, g)])
            mixed = (nd[:, :256] / nd[:, 256:]).astype(bf16)
            buf_a[m, rows, pl.ds(3 * D + 256 * g, 256)] = mixed
        branch = dot(buf_a[m, rows, out_at], wt[out_at, :]) + bias_ref[:, out_at]
        norm_forward(m, rows, xin[m, rows, :].astype(f32) + branch)

    def attend_forward(m, mode):
        if mode == 2:
            attend_features(m, whole)
            summaries(m)
            attend_mix(m, whole)
            send_next(m, 0)
            send_next(m, 1)
            return
        attend_features(m, halves[mode])
        if mode == 1:
            summaries(m)
            for part, rows in enumerate(halves):
                attend_mix(m, rows)
                send_next(m, part)

    def feed_forward(m, mode):
        rows = (halves + (whole,))[mode]
        x = xin[m, rows, :]
        tile = 512
        for j in range(FF // tile):
            c = pl.ds(j * tile, tile)
            a = dot(x, w[:, c]) + bias_ref[:, c]
            cdf = 0.5 + 0.5 * lax.erf(a * 0.7071067811865476)
            pdf = jnp.exp(a * a * -0.5) * 0.3989422804014327
            buf_a[m, rows, c] = (a * cdf).astype(bf16)
            buf_b[m, rows, c] = (cdf + a * pdf).astype(bf16)
        branch = dot(buf_a[m, rows, :], ut[...])
        norm_forward(m, rows, x.astype(f32) + branch)
        for h in (mode,) if mode < 2 else (0, 1):
            send_next(m, h)

    def attend_backward(m, mode):
        rows = (halves + (whole,))[mode]
        dpre = norm_backward(m, rows)
        nbuf[m, rows, :] = dpre
        db = dbr[m, rows, :]
        bias_grad_ref[:, out_at] += jnp.sum(db.astype(f32), axis=0, keepdims=True)

        def store(rows, k, g, val):
            c = pl.ds(k * D + 256 * g, 256)
            buf_b[m, rows, c] = val
            bias_grad_ref[:, c] += jnp.sum(val.astype(f32), axis=0, keepdims=True)

        for g in range(G):
            dmix = dot(db, w[:, pl.ds(3 * D + 256 * g, 256)])
            fq = buf_a[m, rows, fq_at[g]]
            sz = u[sz_at(m, g)]
            nd = dot(fq, sz)
            rden = 1.0 / nd[:, 256:]
            dnum = dmix * rden
            dden = -dnum * (nd[:, :256] * rden)
            de = jnp.concatenate([dnum, dden], axis=1).astype(bf16)
            buf_b[m, rows, pl.ds(D + 512 * g, 512)] = de
            duq = dot_cols(de, sz) * (1.0 - jnp.exp(-fq.astype(f32)))
            dq = (dot_cols(duq.astype(bf16), fmap_ref[g]) * fscale).astype(bf16)
            store(rows, 0, g, dq)
        if mode == 0:
            return
        for g in range(G):
            dsz = dot_rows(buf_a[m, :, fq_at[g]], buf_b[m, :, pl.ds(D + 512 * g, 512)])
            u[sz_at(m, g)] = jnp.where(pair_mask, dsz, 0.0).astype(bf16)
        for part, rows in enumerate(halves if mode == 1 else (whole,)):
            valid = valid_rows(m, rows)
            for g in range(G):
                dsz = u[sz_at(m, g)]
                fk = buf_a[m, rows, fk_at[g]]
                dfk = dot_cols(with_ones(buf_a[m, rows, v_at[g]]), dsz)
                duk = jnp.where(valid, dfk, 0.0) * (1.0 - jnp.exp(-fk.astype(f32)))
                dk = (dot_cols(duk.astype(bf16), fmap_ref[g]) * fscale).astype(bf16)
                store(rows, 1, g, dk)
                store(rows, 2, g, dot(fk, dsz[:, :256]).astype(bf16))
            inner = pl.ds(0, 3 * D)
            dx = nbuf[m, rows, :] + dot(buf_b[m, rows, inner], wt[inner, :])
            dxo[m, rows, :] = dx.astype(bf16)
            for h in (part,) if mode == 1 else (0, 1):
                send_back(m, h)

    def feed_backward(m, mode):
        rows = (halves + (whole,))[mode]
        dpre = norm_backward(m, rows)
        db = dbr[m, rows, :]
        tile = 512
        for j in range(FF // tile):
            c = pl.ds(j * tile, tile)
            da = (dot(db, u[:, c]) * buf_b[m, rows, c].astype(f32)).astype(bf16)
            buf_b[m, rows, c] = da
            bias_grad_ref[:, c] += jnp.sum(da.astype(f32), axis=0, keepdims=True)
        dx = dpre + dot(buf_b[m, rows, :], wt[...])
        dxo[m, rows, :] = dx.astype(bf16)
        for h in (mode,) if mode < 2 else (0, 1):
            send_back(m, h)

    def out_copy(m):
        return pltpu.make_async_copy(out_stage, out_hbm.at[m], stage_sem.at[0])

    def grad_copy(m):
        return pltpu.make_async_copy(grad_stage, grad_hbm.at[m], stage_sem.at[1])

    def write_out(copy, rows, staged, m):
        @pl.when(m >= 1)
        def _():
            copy(m - 1).wait()

        staged[...] = rows[m, pl.ds(0, L), :]
        copy(m).start()

    pad_zero = jnp.zeros((LP - L, D), bf16)
    eye = lax.broadcasted_iota(jnp.int32, (L, L), 0) == lax.broadcasted_iota(jnp.int32, (L, L), 1)

    def forward_step(m, mode):
        if mode != 1:
            @pl.when(first)
            def _():
                land_copy(x_hbm, m).wait()
                xin[m] = jnp.concatenate([land[lax.rem(m, 2)], pad_zero], axis=0)

                @pl.when(m + 2 < M)
                def _():
                    land_copy(x_hbm, m + 2).start()

        @pl.when(s > 0)
        def _():
            for h in (mode,) if mode < 2 else (0, 1):
                next_copy(m, h).wait_recv()

        @pl.when(is_attn)
        def _():
            attend_forward(m, mode)

        @pl.when(is_ff)
        def _():
            feed_forward(m, mode)

        if mode > 0:
            write_out(out_copy, out, out_stage, m)
        if mode > 0:
            @pl.when(first & (m == M - 1))
            def _():
                turn(w, wt, 0, 3 * D // 256)

    def backward_step(m, mode):
        if mode != 1:
            @pl.when(last)
            def _():
                land_copy(cot_hbm, m).wait()
                row = jnp.where(
                    lax.broadcasted_iota(jnp.int32, (1, L), 1) < len_ref[m],
                    pred_ref[pl.ds(m, 1), :].astype(f32),
                    0.0,
                )
                col = jnp.sum(jnp.where(eye, row, 0.0), axis=1, keepdims=True)
                masked = (land[lax.rem(m, 2)].astype(f32) * col).astype(bf16)
                dyin[m] = jnp.concatenate([masked, pad_zero], axis=0)

                @pl.when(m + 2 < M)
                def _():
                    land_copy(cot_hbm, m + 2).start()

        @pl.when(s < NS - 1)
        def _():
            for h in (mode,) if mode < 2 else (0, 1):
                back_copy(m, h).wait_recv()

        @pl.when(is_attn)
        def _():
            attend_backward(m, mode)

        @pl.when(is_ff)
        def _():
            feed_backward(m, mode)

        if mode > 0:
            write_out(grad_copy, dxo, grad_stage, m)

    back_start = jnp.where(s == 0, 16, jnp.where(s == 1, 12, jnp.where(s == 2, 10, 6)))
    relay_start = 12

    def when_due(start, act):
        def at(t):
            i = t - start
            m = i // 2

            apart = i < 0
            for n in SPLIT:
                apart = apart | (m == n % M)
            here = (i >= 0) & (i < 2 * M)

            @pl.when(here & jnp.logical_not(apart) & (lax.rem(i, 2) == 1))
            def _():
                act(m, 2)

            for h in range(2 if SPLIT else 0):
                @pl.when(here & apart & (lax.rem(i, 2) == h))
                def _():
                    act(m, h)

        return at

    forward_at = when_due(2 * s, forward_step)
    backward_at = when_due(back_start, backward_step)

    def tick(t, carry):
        forward_at(t)
        if relayed > 0:
            i = t - relay_start
            for h in range(2):
                @pl.when((s == 0) & (i >= 0) & (i < 2 * relayed) & (lax.rem(i, 2) == h))
                def _():
                    relay_in(relay_lo + i // 2, h).wait_recv()
                    relay_on(relay_lo + i // 2, h).start()
        backward_at(t)
        return carry

    lax.fori_loop(0, 28, tick, 0)

    if relayed > 0:
        @pl.when(s == 0)
        def _():
            for m in range(relay_lo, relay_hi):
                for h in range(2):
                    relay_on(m, h).wait_send()

    @pl.when(is_ff)
    def _():
        for i in range(pieces):
            u_copy_to(u_rows(i), i, 2, sib).wait_send()
        for i in range(2):
            u_copy_to(u_rows(i), i, 1, mate).wait_send()
            u_copy_to(u_rows(i, 1 - side), i, 3, sib).wait_send()

    if in_kernel:
        reduce_gradients(
            cfg,
            s,
            d,
            odd,
            w,
            u,
            wt,
            ut,
            xin,
            dbr,
            buf_a,
            buf_b,
            g_hbm,
            small_ref,
            small_outs,
            *reduce_refs,
        )
    else:
        plain_gradients(cfg, odd, xin, dbr, buf_a, buf_b, g_hbm, g_sem, *reduce_refs)

    for m in range(M):
        for h in range(2):
            @pl.when(s < NS - 1)
            def _():
                next_copy(m, h).wait_send()

            @pl.when(s > 0)
            def _():
                back_copy(m, h).wait_send()

    out_copy(M - 1).wait()
    grad_copy(M - 1).wait()


def place_results(*refs):
    count = (len(refs) - 1) // 3
    sems = refs[-1]
    inward, outward = [], []
    for src, dst, mid in zip(refs[:count], refs[count : 2 * count], refs[2 * count : 3 * count]):
        parts = [(slice(None),)]
        if src.shape[0] > 1:
            step = src.shape[0] // 6
            parts = [(pl.ds(i * step, step),) for i in range(6)]
        for part in parts:
            n = len(inward)
            inward.append(pltpu.make_async_copy(src.at[part], mid.at[part], sems.at[0, n]))
            outward.append(pltpu.make_async_copy(mid.at[part], dst.at[part], sems.at[1, n]))
    for copy in inward:
        copy.start()
    for first, second in zip(inward, outward):
        first.wait()
        second.start()
    for copy in outward:
        copy.wait()


def shards(
    block_input, cotangent, lengths, predicted, slab, in_bias, norm_gain, norm_bias, feature_draws
):
    NS = lax.axis_size("section")
    ND = lax.axis_size("dp")
    M, L, D = block_input.shape
    FF = in_bias.shape[1]
    H, HD, FE = feature_draws.shape
    LP = (L + 15) // 16 * 16
    GH = 256 // HD
    G = D // 256
    GF = GH * FE
    fscale = float((3.0 / (20.0 * HD)) ** 0.5)
    in_kernel = D // ND % 32 == 0 and NS == 4
    C = CHUNK if in_kernel else D
    cfg = (M, L, LP, D, FF, HD, FE, NS, ND, fscale, in_kernel, C)
    hbm = pl.BlockSpec(memory_space=pl.ANY)
    vmem = pl.BlockSpec(memory_space=pltpu.VMEM)
    smem = pl.BlockSpec(memory_space=pltpu.SMEM)
    dma = pltpu.SemaphoreType.DMA
    rows_bf = pltpu.VMEM((M, LP, D), bf16)
    wide_bf = pltpu.VMEM((M, LP, FF), bf16)
    small_size = FF + 2 * D
    smalls = [FF // ND, D // ND, D // ND] if in_kernel else [small_size]
    scratch = [pltpu.VMEM((1, small_size), f32)] if in_kernel else []
    scratch += [
        pltpu.VMEM((G, GH * HD, GF), bf16),
        pltpu.VMEM((H, FE, HD), jnp.int32),
        pltpu.VMEM((D, FF), bf16),
        pltpu.VMEM((D, FF), bf16),
        pltpu.VMEM((FF, D), bf16),
        pltpu.VMEM((FF, D), bf16),
        rows_bf,
        rows_bf,
        rows_bf,
        rows_bf,
        rows_bf,
        pltpu.VMEM((M, LP, D), f32),
        pltpu.VMEM((M, LP, 1), f32),
        wide_bf,
        wide_bf,
        pltpu.VMEM((2, L, D), bf16),
        pltpu.VMEM((L, D), bf16),
        pltpu.VMEM((L, D), bf16),
        dma((3,)),
        dma((2,)),
        dma((4, 4)),
        dma((4, 4)),
        dma((M, 2)),
        dma((M, 2)),
        dma((M, 2)),
        dma((M, 2)),
        dma((2,)),
        dma((1,)),
    ]
    if in_kernel:
        Z, B, chunks = ND // 2, D // ND, 2 * FF // C
        cross = FF // C // 2
        lines = chunks
        scratch += [
            pltpu.SemaphoreType.REGULAR((3,)),
            pltpu.VMEM((Z + 1, Z * B, C), f32),
            pltpu.VMEM((2, Z * B, C), bf16),
            pltpu.VMEM((cross + 1, Z * B, C), bf16),
            pltpu.VMEM((2, Z, B, C), bf16),
            pltpu.VMEM((2, B, C), f32),
            pltpu.VMEM((ND, 1, small_size), f32),
            dma((2,)),
            dma((chunks,)),
            dma((2, Z)),
            dma((lines, Z)),
            dma((lines, Z)),
            dma((2,)),
            dma((cross + 1,)),
            dma((cross + 1,)),
            dma((cross + 1,)),
            dma((cross + 1,)),
            dma((ND,)),
            dma((ND,)),
        ]
        g_shape = (B, FF + FF // 2)
    else:
        scratch += [pltpu.VMEM((D, D), f32)]
        g_shape = (D, 2 * FF)
    section_out, section_grad, grads, *small = pl.pallas_call(
        functools.partial(pipeline_kernel, cfg),
        out_shape=[
            jax.ShapeDtypeStruct((M, L, D), bf16),
            jax.ShapeDtypeStruct((M, L, D), bf16),
            jax.ShapeDtypeStruct(g_shape, f32),
        ]
        + [jax.ShapeDtypeStruct((1, n), f32) for n in smalls],
        in_specs=[smem, hbm, hbm, vmem, hbm, vmem, vmem, vmem, hbm],
        out_specs=[hbm, hbm, hbm] + [vmem] * len(smalls),
        scratch_shapes=scratch,
        compiler_params=pltpu.CompilerParams(
            collective_id=0, has_side_effects=True, vmem_limit_bytes=62 * 2**20
        ),
        name="pipeline",
    )(
        lengths,
        block_input,
        cotangent,
        predicted,
        slab,
        in_bias,
        norm_gain,
        norm_bias,
        jnp.swapaxes(feature_draws, 1, 2),
    )
    if in_kernel:
        results = (section_out, section_grad, grads, *small)
        section_out, section_grad, own, *parts = pl.pallas_call(
            place_results,
            out_shape=[jax.ShapeDtypeStruct(r.shape, r.dtype) for r in results],
            in_specs=[hbm] * len(results),
            out_specs=[hbm] * len(results),
            scratch_shapes=[pltpu.VMEM(r.shape, r.dtype) for r in results] + [dma((2, 6 * len(results)))],
            compiler_params=pltpu.CompilerParams(vmem_limit_bytes=62 * 2**20),
            name="place_results",
        )(*results)
    else:
        def scatter(value):
            return lax.psum_scatter(value, "dp", scatter_dimension=0, tiled=True)

        HALF = FF // 2
        both = scatter(grads)
        sums = small[0][0]
        parts = [scatter(v)[None] for v in (sums[:FF], sums[FF : FF + D], sums[FF + D :])]
        is_attention = lax.axis_index("section") % 2 == 0
        turned = jnp.where(
            is_attention,
            jnp.concatenate([both[:, D:FF], both[:, :D], both[:, FF:]], axis=1),
            jnp.concatenate([both[:, FF:], both[:, :FF]], axis=1),
        )
        pairs = [(i, i - 1) for i in range(1, NS, 2)]
        arrived = lax.ppermute(turned[:, FF : FF + HALF], "section", pairs)
        rest = jnp.where(is_attention, arrived, turned[:, FF + HALF :])
        own = jnp.concatenate([turned[:, :FF], rest], axis=1)
    return (
        section_out[None],
        section_grad[None],
        own[None],
        *parts,
    )


def solution(mesh):
    placed = (
        P("dp", None, None),
        P("dp", None, None),
        P("dp"),
        P("dp", None),
        P("section", None, None),
        P("section", None),
        P("section", None),
        P("section", None),
        P(),
    )
    return jax.shard_map(
        shards,
        mesh=mesh,
        in_specs=placed,
        out_specs=(
            P("section", "dp", None, None),
            P("section", "dp", None, None),
            P("section", "dp", None),
            P("section", "dp"),
            P("section", "dp"),
            P("section", "dp"),
        ),
        check_vma=False,
    )
```

```python
import functools

import jax
import jax.numpy as jnp
from jax import lax
from jax.experimental import pallas as pl
from jax.experimental.pallas import tpu as pltpu
from jax.sharding import PartitionSpec as P

MESH = pl.DeviceIdType.MESH
CHUNK = 384
RELAYED = (0, 3)
SPLIT = ()
norm_epsilon = 1e-05
bf16 = jnp.bfloat16
f32 = jnp.float32


def dot(a, b):
    return lax.dot_general(a, b, (((1,), (0,)), ((), ())), preferred_element_type=f32)


def dot_cols(a, b):
    return lax.dot_general(a, b, (((1,), (1,)), ((), ())), preferred_element_type=f32)


def dot_rows(a, b):
    return lax.dot_general(a, b, (((0,), (0,)), ((), ())), preferred_element_type=f32)


def softplus(u):
    return jnp.maximum(u, 0.0) + jnp.log1p(jnp.exp(-jnp.abs(u)))


def block_mask(feature_rows, value_cols, features, head_dim):
    r = lax.broadcasted_iota(jnp.int32, (feature_rows, value_cols), 0) // features
    c = lax.broadcasted_iota(jnp.int32, (feature_rows, value_cols), 1) // head_dim
    return r == c


def flat(ref, c):
    return ref[:, :, c].reshape(ref.shape[0] * ref.shape[1], c.size)


def column(k, D):
    return pl.ds(pl.multiple_of(k * D, D), D)


def chunk_counts(cfg, odd):
    D, FF, C = cfg[3], cfg[4], cfg[-1]
    wide = FF // C
    return D // C + (wide - D // C) * odd, wide + wide * odd


def plain_gradients(cfg, odd, xin, dbr, buf_a, buf_b, g_hbm, g_sem, stage):
    D, FF, C = cfg[3], cfg[4], cfg[-1]
    first_kind, count = chunk_counts(cfg, odd)
    wide = FF // C
    own = D // C

    def store(k):
        cp = pltpu.make_async_copy(stage, g_hbm.at[:, column(k, C)], g_sem.at[0])
        cp.start()
        cp.wait()

    def one(k, carry):
        @pl.when(k < first_kind)
        def _():
            src = column(k + (wide - own) * (1 - odd), C)
            stage[...] = dot_rows(flat(dbr, pl.ds(0, D)), flat(buf_a, src))
            store(k)

        @pl.when(k >= first_kind)
        def _():
            stage[...] = dot_rows(flat(xin, pl.ds(0, D)), flat(buf_b, column(k - first_kind, C)))
            store(k)

        return carry

    lax.fori_loop(0, count, one, 0)

    @pl.when(odd == 0)
    def _():
        stage[...] = jnp.zeros_like(stage)

        def rest(k, carry):
            store(k)
            return carry

        lax.fori_loop(wide, 2 * wide, rest, 0)


def reduce_gradients(
    cfg,
    s,
    d,
    odd,
    w,
    u,
    wt,
    ut,
    xin,
    dbr,
    buf_a,
    buf_b,
    g_hbm,
    small_ref,
    small_outs,
    ready,
    keep,
    core_out,
    cross_out,
    line_out,
    final,
    small_in,
    core_send,
    core_recv,
    line_send,
    up_recv,
    down_recv,
    final_sem,
    cross_send,
    cross_recv,
    away_send,
    away_recv,
    small_send,
    small_recv,
):
    M, L, LP, D, FF, HD, FE, NS, ND, fscale, in_kernel, C = cfg
    Z = ND // 2
    B = D // ND
    R = Z * B
    K = M * LP
    wide = FF // C
    own = D // C
    fold = D // C
    keeps = keep.shape[0]
    p = lax.rem(d, 2)
    z = d // 2
    sib = d + 1 - 2 * p
    first_kind, count = chunk_counts(cfg, odd)
    cross = wide // 2
    shipped = cross + 1
    pre = jnp.where(s == 1, shipped, 0)
    came = jnp.where(s == 2, shipped, 0)
    lines = count - pre + came
    dma_to = functools.partial(pltpu.make_async_remote_copy, device_id_type=MESH)

    pl.semaphore_signal(ready.at[0], inc=1, device_id=(s, sib), device_id_type=MESH)

    @pl.when(z > 0)
    def _():
        pl.semaphore_signal(ready.at[2], inc=1, device_id=(s, d - 2), device_id_type=MESH)

    @pl.when(z < Z - 1)
    def _():
        pl.semaphore_signal(ready.at[1], inc=1, device_id=(s, d + 2), device_id_type=MESH)

    def small_copy(o):
        return dma_to(
            small_ref,
            small_in.at[d],
            small_send.at[o],
            small_recv.at[d],
            device_id=(s, lax.rem(d + o, ND)),
        )

    def small_wait(o):
        j = lax.rem(d + o, ND)
        return dma_to(
            small_ref, small_in.at[j], small_send.at[o], small_recv.at[j], device_id=(s, j)
        )

    for o in range(1, ND):
        small_copy(o).start()
    small_in[d] = small_ref[...]

    place_d = pl.ds(0, K)
    place_x = pl.ds((K + 127) // 128 * 128, K)
    for src, at_cols in ((dbr, place_d), (xin, place_x)):
        for i in range(D // 256):
            turned = flat(src, pl.ds(256 * i, 256)).T
            for q in range(8):
                t = 8 * i + q
                block = t * 32 // B
                at = block % 2 * R + block // 2 * B + t * 32 - block * B
                u[pl.ds(at, 32), at_cols] = turned[32 * q : 32 * q + 32]

    per = D // R

    def slot(j):
        return (pl.ds(pl.multiple_of(lax.rem(j, per) * R, 16), R), column(j // per, C))

    def slot_block(j, zt):
        r = pl.multiple_of(lax.rem(j, per) * R + zt * B, 16)
        return (pl.ds(r, B), column(j // per, C))

    def line_place(n, zt):
        r = pl.multiple_of(n // fold * R + zt * B, 16)
        return (pl.ds(r, B), column(lax.rem(n, fold), C))

    def cross_place(c):
        n = 2 * wide - cross + c
        r = pl.multiple_of(n // fold * R, 16)
        return (pl.ds(r, R), column(lax.rem(n, fold), C))

    spare = (pl.ds(0, R), pl.ds(FF - (C + 127) // 128 * 128, C))

    def core_copy(j):
        return dma_to(
            core_out.at[lax.rem(j, 2)],
            w.at[slot(j)],
            core_send.at[lax.rem(j, 2)],
            core_recv.at[j],
            device_id=(s, sib),
        )

    def cross_copy(c):
        return dma_to(
            cross_out.at[c],
            ut.at[cross_place(c)],
            cross_send.at[c],
            cross_recv.at[c],
            device_id=(2, d),
        )

    def spare_copy():
        return dma_to(
            cross_out.at[cross],
            u.at[spare],
            cross_send.at[cross],
            cross_recv.at[cross],
            device_id=(2, d),
        )

    def up_copy(n, zt):
        return dma_to(
            line_out.at[lax.rem(n, 3), zt],
            ut.at[line_place(n, zt)],
            line_send.at[lax.rem(n, 3), zt],
            up_recv.at[n, zt],
            device_id=(s, d + 2),
        )

    def down_copy(n, zt):
        return dma_to(
            line_out.at[lax.rem(n, 3), zt],
            wt.at[line_place(n, zt)],
            line_send.at[lax.rem(n, 3), zt],
            down_recv.at[n, zt],
            device_id=(s, d - 2),
        )

    def final_copy(n):
        j = n + pre
        early = j + cross * odd + (wide - own) * (1 - odd)
        at = jnp.where(j < first_kind, early, j - first_kind)
        return pltpu.make_async_copy(
            final.at[lax.rem(n, 2)], g_hbm.at[:, column(at, C)], final_sem.at[lax.rem(n, 2)]
        )

    def away(n):
        return ((s == 3) & (n < cross)) | ((s == 2) & (n >= count))

    def away_copy(n):
        c = n - jnp.where(s == 2, count, 0)
        to = jnp.where(s == 3, 2, c // cross)
        return dma_to(
            final.at[lax.rem(n, 2)],
            g_hbm.at[:, column(wide + lax.rem(c, cross), C)],
            away_send.at[lax.rem(n, 2)],
            away_recv.at[c],
            device_id=(to, d),
        )

    def away_arrival(c):
        return dma_to(
            final.at[0],
            g_hbm.at[:, column(wide + c % cross, C)],
            away_send.at[0],
            away_recv.at[c],
            device_id=(jnp.where(s == 3, 2, 0), d),
        )

    def final_wait(n):
        @pl.when(away(n))
        def _():
            away_copy(n).wait_send()

        @pl.when(jnp.logical_not(away(n)))
        def _():
            final_copy(n).wait()

    def total(n, zt):
        j = n + pre
        return keep[lax.rem(j, keeps), pl.ds(zt * B, B), :] + w[slot_block(j, zt)].astype(f32)

    near = jnp.minimum(z, Z - 1 - z)
    far = jnp.maximum(z, Z - 1 - z)

    def make(k):
        sl = lax.rem(k, 2)

        def products(place, right):
            @pl.when(k >= 2)
            def _():
                core_copy(k - 2).wait_send()

            theirs = pl.ds(pl.multiple_of((1 - p) * R, 16), R)
            mine = pl.ds(pl.multiple_of(p * R, 16), R)
            core_out[sl] = dot(u[theirs, place], right).astype(bf16)

            @pl.when(k == 0)
            def _():
                pl.semaphore_wait(ready.at[0], 1)

            core_copy(k).start()
            keep[lax.rem(k, keeps)] = dot(u[mine, place], right)

        @pl.when(k < first_kind)
        def _():
            products(place_d, flat(buf_a, column(k + (wide - own) * (1 - odd), C)))

        @pl.when(k >= first_kind)
        def _():
            products(place_x, flat(buf_b, column(k - first_kind, C)))

    def fetch(k):
        c = k - count

        @pl.when(c < cross)
        def _():
            cross_copy(c).wait_recv()
            keep[lax.rem(k, keeps)] = ut[cross_place(c)].astype(f32)

        @pl.when(c == cross)
        def _():
            spare_copy().wait_recv()
            keep[lax.rem(k, keeps)] = u[spare].astype(f32)

        w[slot(k)] = jnp.zeros((R, C), bf16)

    def ship(c):
        core_copy(c).wait_recv()
        both = keep[lax.rem(c, keeps)] + w[slot(c)].astype(f32)
        cross_out[c] = both.astype(bf16)

        @pl.when(c < cross)
        def _():
            cross_copy(c).start()

        @pl.when(c == cross)
        def _():
            spare_copy().start()

    def step(own_pass, lo, hi, k, carry):
        if own_pass:
            @pl.when(k < count)
            def _():
                make(k)

            @pl.when((k >= 1) & (k - 1 < pre))
            def _():
                ship(k - 1)
        else:
            @pl.when(k < count + came)
            def _():
                fetch(k)

        n_near = k - 1 - pre - near

        if own_pass:
            @pl.when((n_near >= lo) & (n_near < hi))
            def _():
                core_copy(n_near + pre).wait_recv()

        n_up = k - 1 - pre - z

        @pl.when((n_up >= lo) & (n_up < hi) & (z < Z - 1))
        def _():
            @pl.when(n_up == 0)
            def _():
                pl.semaphore_wait(ready.at[2], 1)

            for zt in range(Z - 1, 0, -1):
                @pl.when(zt > z)
                def _():
                    @pl.when(n_up >= 3)
                    def _():
                        up_copy(n_up - 3, zt).wait_send()

                    @pl.when(z > 0)
                    def _():
                        up_copy(n_up, zt).wait_recv()
                        line_out[lax.rem(n_up, 3), zt] = (
                            total(n_up, zt) + ut[line_place(n_up, zt)].astype(f32)
                        ).astype(bf16)

                    @pl.when(z == 0)
                    def _():
                        line_out[lax.rem(n_up, 3), zt] = total(n_up, zt).astype(bf16)

                    up_copy(n_up, zt).start()

        n_down = k - 1 - pre - (Z - 1 - z)

        @pl.when((n_down >= lo) & (n_down < hi) & (z > 0))
        def _():
            @pl.when(n_down == 0)
            def _():
                pl.semaphore_wait(ready.at[1], 1)

            for zt in range(Z - 1):
                @pl.when(zt < z)
                def _():
                    @pl.when(n_down >= 3)
                    def _():
                        down_copy(n_down - 3, zt).wait_send()

                    @pl.when(z < Z - 1)
                    def _():
                        down_copy(n_down, zt).wait_recv()
                        line_out[lax.rem(n_down, 3), zt] = (
                            total(n_down, zt) + wt[line_place(n_down, zt)].astype(f32)
                        ).astype(bf16)

                    @pl.when(z == Z - 1)
                    def _():
                        line_out[lax.rem(n_down, 3), zt] = total(n_down, zt).astype(bf16)

                    down_copy(n_down, zt).start()

        n_own = k - 1 - pre - far

        @pl.when((n_own >= lo) & (n_own < hi))
        def _():
            sl = lax.rem(n_own, 2)

            @pl.when(n_own >= 2)
            def _():
                final_wait(n_own - 2)

            final[sl] = total(n_own, z)

            @pl.when(z > 0)
            def _():
                up_copy(n_own, z).wait_recv()
                final[sl] += ut[line_place(n_own, z)].astype(f32)

            @pl.when(z < Z - 1)
            def _():
                down_copy(n_own, z).wait_recv()
                final[sl] += wt[line_place(n_own, z)].astype(f32)

            @pl.when(away(n_own))
            def _():
                away_copy(n_own).start()

            @pl.when(jnp.logical_not(away(n_own)))
            def _():
                final_copy(n_own).start()

        return carry

    own_lines = count - pre
    lax.fori_loop(0, count + 1 + far, functools.partial(step, True, 0, own_lines), 0)
    later = jnp.where(s == 2, count + came + 1 + far, count)
    lax.fori_loop(count, later, functools.partial(step, False, count, count + came), 0)

    for back in (3, 2, 1):
        n = lines - back
        for zt in range(Z):
            @pl.when(zt > z)
            def _():
                up_copy(n, zt).wait_send()

            @pl.when(zt < z)
            def _():
                down_copy(n, zt).wait_send()

    for back in (2, 1):
        core_copy(count - back).wait_send()
        final_wait(lines - back)

    @pl.when(s == 1)
    def _():
        for c in range(cross):
            cross_copy(c).wait_send()
        spare_copy().wait_send()
        away_arrival(cross).wait_recv()

    @pl.when(odd == 0)
    def _():
        for c in range(cross):
            away_arrival(c).wait_recv()

    for o in range(1, ND):
        small_wait(o).wait_recv()
        small_copy(o).wait_send()
    acc = small_in[0]
    for j in range(1, ND):
        acc = acc + small_in[j]
    small_ref[...] = acc
    bias_out, gain_out, shift_out = small_outs
    P = FF // ND
    bias_out[...] = small_ref[:, pl.ds(pl.multiple_of(d * P, 128), P)]
    for j in range(ND):
        @pl.when(d == j)
        def _():
            gain_out[...] = acc[:, FF + B * j : FF + B * j + B]
            shift_out[...] = acc[:, FF + D + B * j : FF + D + B * j + B]


def pipeline_kernel(
    cfg,
    len_ref,
    x_hbm,
    cot_hbm,
    pred_ref,
    slab_hbm,
    bias_ref,
    gain_ref,
    shift_ref,
    draws_hbm,
    out_hbm,
    grad_hbm,
    g_hbm,
    *refs,
):
    M, L, LP, D, FF, HD, FE, NS, ND, fscale, in_kernel, C = cfg
    small_outs = refs[:3] if in_kernel else ()
    small_ref = refs[3] if in_kernel else refs[0]
    fmap_ref, draws_ref = refs[4:6] if in_kernel else refs[1:3]
    (
        w,
        u,
        wt,
        ut,
        xin,
        out,
        dyin,
        dxo,
        dbr,
        nbuf,
        rbuf,
        buf_a,
        buf_b,
        land,
        out_stage,
        grad_stage,
        load_sem,
        x_sem,
        u_send,
        u_recv,
        f_send,
        f_recv,
        b_send,
        b_recv,
        stage_sem,
        g_sem,
        *reduce_refs,
    ) = refs[6:] if in_kernel else refs[3:]
    HALF = FF // 2
    GH = 256 // HD
    G = D // 256
    GF = GH * FE
    top = (LP // 2 + 15) // 16 * 16
    halves = (pl.ds(0, top), pl.ds(top, LP - top))
    whole = pl.ds(0, LP)
    relay_lo, relay_hi = RELAYED if NS == 4 else (0, 0)
    relayed = relay_hi - relay_lo
    s = lax.axis_index("section")
    d = lax.axis_index("dp")
    odd = lax.rem(s, 2)
    is_attn = odd == 0
    is_ff = odd == 1
    first = s == 0
    last = s == NS - 1
    sib = d + 1 - 2 * lax.rem(d, 2)
    mate = d + 2 - 4 * lax.rem(d // 2, 2)
    pieces = 4
    piece = D // 12

    barrier = pltpu.get_barrier_semaphore()

    def greet(cond, ts, td):
        @pl.when(cond)
        def _():
            pl.semaphore_signal(barrier, inc=1, device_id=(ts, td), device_id_type=MESH)

    always = s >= 0
    partners = 2
    if in_kernel:
        partners = ND - 1
        for o in range(1, ND):
            greet(always, s, lax.rem(d + o, ND))
    else:
        greet(always, s, sib)
        greet(always, s, mate)
    greet(s > 0, s - 1, d)
    greet(s < NS - 1, s + 1, d)
    if relayed > 0 or in_kernel:
        greet(s == 0, 2, d)
        greet(s == 2, 0, d)
        extra = jnp.where(lax.rem(s, 2) == 0, 1, 0)
    else:
        extra = 0

    w_copy = pltpu.make_async_copy(slab_hbm.at[0, :, pl.ds(0, FF)], w, load_sem.at[0])
    u_copy = pltpu.make_async_copy(
        slab_hbm.at[0, :, pl.ds(FF, HALF)], u.at[:, pl.ds(HALF, HALF)], load_sem.at[1]
    )
    w_copy.start()
    draws_copy = pltpu.make_async_copy(draws_hbm, draws_ref, load_sem.at[2])

    @pl.when(is_attn)
    def _():
        draws_copy.start()


    def land_copy(ref, m):
        sl = lax.rem(m, 2)
        return pltpu.make_async_copy(ref.at[m], land.at[sl], x_sem.at[sl])

    @pl.when(first)
    def _():
        for m in range(2):
            land_copy(x_hbm, m).start()

    @pl.when(last)
    def _():
        for m in range(2):
            land_copy(cot_hbm, m).start()

    @pl.when(is_ff)
    def _():
        u_copy.start()

    small_ref[...] = jnp.zeros_like(small_ref)
    bias_grad_ref = small_ref.at[:, pl.ds(0, FF)]
    gain_grad_ref = small_ref.at[:, pl.ds(FF, D)]
    shift_grad_ref = small_ref.at[:, pl.ds(FF + D, D)]

    @pl.when(first | last)
    def _():
        pl.semaphore_wait(barrier, partners + 1 + extra)

    @pl.when((s > 0) & (s < NS - 1))
    def _():
        pl.semaphore_wait(barrier, partners + 2 + extra)

    left = pl.ds(0, HALF)
    core = lax.rem(d, 2)
    side = lax.rem(d // 2, 2)

    def u_rows(i, side=side):
        n = jnp.where(i < 2, 8 * side, 0) + 2 * i + core
        return pl.ds(pl.multiple_of(n * piece, piece), piece)

    def u_from_section(i):
        return pltpu.make_async_remote_copy(
            slab_hbm.at[0, u_rows(i), pl.ds(FF, HALF)],
            u.at[u_rows(i), left],
            u_send.at[0, i],
            u_recv.at[0, i],
            device_id=(s + 1, d),
            device_id_type=MESH,
        )

    def u_copy_to(rows, i, k, to):
        return pltpu.make_async_remote_copy(
            u.at[rows, left],
            u.at[rows, left],
            u_send.at[k, i],
            u_recv.at[k, i],
            device_id=(s, to),
            device_id_type=MESH,
        )

    detour = (2, 3) if NS == 4 else ()

    def u_aside(i, to, k):
        src = slab_hbm.at[0, u_rows(i), pl.ds(FF, HALF)] if k == 0 else u.at[u_rows(i), left]
        return pltpu.make_async_remote_copy(
            src,
            u.at[u_rows(i), left],
            u_send.at[k, i],
            u_recv.at[0, i],
            device_id=(to, d),
            device_id_type=MESH,
        )

    @pl.when(first)
    def _():
        for i in range(pieces):
            if i in detour:
                u_aside(i, 2, 0).start()
            else:
                u_from_section(i).start()

    @pl.when(is_attn & (s > 0) & (s < NS - 1))
    def _():
        for i in detour:
            u_aside(i, 1, 1).wait_recv()
            u_aside(i, 1, 1).start()
        for i in detour:
            u_aside(i, 1, 1).wait_send()
        for i in range(pieces):
            u_from_section(i).start()

    def turn(src, dst, start, count):
        for i in range(start, start + count):
            dst[pl.ds(256 * i, 256), :] = src[:, pl.ds(256 * i, 256)].T

    w_copy.wait()
    late_turn = first

    @pl.when(is_attn)
    def _():
        turn(w, wt, 3 * D // 256, D // 256)
        draws_copy.wait()
        f_row = lax.broadcasted_iota(jnp.int32, (FE, GF), 0)
        f_col = lax.broadcasted_iota(jnp.int32, (FE, GF), 1)
        for n in range(G * GH):
            shift = jnp.where(f_col == f_row + n % GH * FE, 1.0, 0.0).astype(bf16)
            spread = dot_rows(draws_ref[n].astype(f32).astype(bf16), shift)
            fmap_ref[n // GH, pl.ds(n % GH * HD, HD), :] = spread.astype(bf16)

    @pl.when(s == 2)
    def _():
        turn(w, wt, 0, 3 * D // 256)

    @pl.when(is_ff)
    def _():
        turn(w, wt, 0, FF // 256)
        u_copy.wait()
        turn(u, ut, HALF // 256, HALF // 256)
        for i in range(pieces):
            u_from_section(i).wait_recv()
            if i < 2:
                u_copy_to(u_rows(i), i, 1, mate).start()
            u_copy_to(u_rows(i), i, 2, sib).start()
            if i >= 2:
                u_copy_to(u_rows(i - 2, 1 - side), i - 2, 1, mate).wait_recv()
                u_copy_to(u_rows(i - 2, 1 - side), i - 2, 3, sib).start()
        for i in range(pieces):
            u_copy_to(u_rows(i), i, 2, sib).wait_recv()
        for i in range(2):
            u_copy_to(u_rows(i, 1 - side), i, 3, sib).wait_recv()
        turn(u, ut, 0, HALF // 256)

    g_row = gain_ref[...]
    b_row = shift_ref[...]
    head_mask = block_mask(GF, 256, FE, HD)
    pair_mask = jnp.concatenate([head_mask, head_mask], axis=1)

    def sz_at(m, g):
        n = m * G + g
        r = pl.multiple_of(lax.rem(n, D // GF) * GF, GF)
        c = pl.multiple_of(n // (D // GF) * 512, 512)
        return (pl.ds(r, GF), pl.ds(c, 512))

    def valid_rows(m, rows):
        at = lax.broadcasted_iota(jnp.int32, (rows.size, GF), 0) + rows.start
        return at < len_ref[m]

    def with_ones(v):
        return jnp.concatenate([v, jnp.ones(v.shape, bf16)], axis=1)

    def norm_forward(m, rows, pre):
        mean = jnp.mean(pre, axis=-1, keepdims=True)
        cen = pre - mean
        r = lax.rsqrt(jnp.mean(cen * cen, axis=-1, keepdims=True) + norm_epsilon)
        n = cen * r
        nbuf[m, rows, :] = n
        rbuf[m, rows, :] = r
        out[m, rows, :] = (n * g_row + b_row).astype(bf16)

    def norm_backward(m, rows):
        dy = dyin[m, rows, :].astype(f32)
        n = nbuf[m, rows, :]
        dn = dy * g_row
        m1 = jnp.mean(dn, axis=-1, keepdims=True)
        m2 = jnp.mean(dn * n, axis=-1, keepdims=True)
        gain_grad_ref[...] += jnp.sum(dy * n, axis=0, keepdims=True)
        shift_grad_ref[...] += jnp.sum(dy, axis=0, keepdims=True)
        dpre = rbuf[m, rows, :] * (dn - m1 - n * m2)
        dbr[m, rows, :] = dpre.astype(bf16)
        return dpre

    def next_copy(m, h):
        return pltpu.make_async_remote_copy(
            out.at[m, halves[h]],
            xin.at[m, halves[h]],
            f_send.at[m, h],
            f_recv.at[m, h],
            device_id=(s + 1, d),
            device_id_type=MESH,
        )

    def back_copy(m, h):
        return pltpu.make_async_remote_copy(
            dxo.at[m, halves[h]],
            dyin.at[m, halves[h]],
            b_send.at[m, h],
            b_recv.at[m, h],
            device_id=(s - 1, d),
            device_id_type=MESH,
        )

    def relay_at(m, h):
        start = pl.multiple_of(m * LP + halves[h].start, 16)
        return ut.at[pl.ds(start, halves[h].size)]

    def relay_in(m, h):
        return pltpu.make_async_remote_copy(
            dxo.at[m, halves[h]],
            relay_at(m, h),
            b_send.at[m, h],
            f_recv.at[m, h],
            device_id=(0, d),
            device_id_type=MESH,
        )

    def relay_on(m, h):
        return pltpu.make_async_remote_copy(
            relay_at(m, h),
            dyin.at[m, halves[h]],
            b_send.at[m, h],
            b_recv.at[m, h],
            device_id=(1, d),
            device_id_type=MESH,
        )

    def send_next(m, h):
        if h == 0:
            @pl.when(is_attn & (m == 0))
            def _():
                for i in range(pieces):
                    u_from_section(i).wait_send()

        @pl.when(s < NS - 1)
        def _():
            next_copy(m, h).start()

    def by_relay(m):
        return (s == 2) & (m >= relay_lo) & (m < relay_hi)

    def send_back(m, h):
        @pl.when((s > 0) & jnp.logical_not(by_relay(m)))
        def _():
            back_copy(m, h).start()

        @pl.when(by_relay(m))
        def _():
            relay_in(m, h).start()

    v_at = [pl.ds(256 * g, 256) for g in range(G)]
    fq_at = [pl.ds(D + GF * g, GF) for g in range(G)]
    fk_at = [pl.ds(D + GF * (G + g), GF) for g in range(G)]
    out_at = pl.ds(3 * D, D)

    def attend_features(m, rows):
        x = xin[m, rows, :]
        valid = valid_rows(m, rows)
        for g in range(G):
            qkv = [
                (dot(x, w[:, c]) + bias_ref[:, c]).astype(bf16)
                for c in (pl.ds(k * D + 256 * g, 256) for k in range(3))
            ]
            fq = softplus(dot(qkv[0], fmap_ref[g]) * fscale).astype(bf16)
            fk = softplus(dot(qkv[1], fmap_ref[g]) * fscale)
            buf_a[m, rows, v_at[g]] = qkv[2]
            buf_a[m, rows, fq_at[g]] = fq
            buf_a[m, rows, fk_at[g]] = jnp.where(valid, fk, 0.0).astype(bf16)

    def summaries(m):
        for g in range(G):
            sz = dot_rows(buf_a[m, :, fk_at[g]], with_ones(buf_a[m, :, v_at[g]]))
            u[sz_at(m, g)] = jnp.where(pair_mask, sz, 0.0).astype(bf16)

    def attend_mix(m, rows):
        for g in range(G):
            nd = dot(buf_a[m, rows, fq_at[g]], u[sz_at(m, g)])
            mixed = (nd[:, :256] / nd[:, 256:]).astype(bf16)
            buf_a[m, rows, pl.ds(3 * D + 256 * g, 256)] = mixed
        branch = dot(buf_a[m, rows, out_at], wt[out_at, :]) + bias_ref[:, out_at]
        norm_forward(m, rows, xin[m, rows, :].astype(f32) + branch)

    def attend_forward(m, mode):
        if mode == 2:
            attend_features(m, whole)
            summaries(m)
            attend_mix(m, whole)
            send_next(m, 0)
            send_next(m, 1)
            return
        attend_features(m, halves[mode])
        if mode == 1:
            summaries(m)
            for part, rows in enumerate(halves):
                attend_mix(m, rows)
                send_next(m, part)

    def feed_forward(m, mode):
        rows = (halves + (whole,))[mode]
        x = xin[m, rows, :]
        tile = 512
        for j in range(FF // tile):
            c = pl.ds(j * tile, tile)
            a = dot(x, w[:, c]) + bias_ref[:, c]
            cdf = 0.5 + 0.5 * lax.erf(a * 0.7071067811865476)
            pdf = jnp.exp(a * a * -0.5) * 0.3989422804014327
            buf_a[m, rows, c] = (a * cdf).astype(bf16)
            buf_b[m, rows, c] = (cdf + a * pdf).astype(bf16)
        branch = dot(buf_a[m, rows, :], ut[...])
        norm_forward(m, rows, x.astype(f32) + branch)
        for h in (mode,) if mode < 2 else (0, 1):
            send_next(m, h)

    def attend_backward(m, mode):
        rows = (halves + (whole,))[mode]
        dpre = norm_backward(m, rows)
        nbuf[m, rows, :] = dpre
        db = dbr[m, rows, :]
        bias_grad_ref[:, out_at] += jnp.sum(db.astype(f32), axis=0, keepdims=True)

        def store(rows, k, g, val):
            c = pl.ds(k * D + 256 * g, 256)
            buf_b[m, rows, c] = val
            bias_grad_ref[:, c] += jnp.sum(val.astype(f32), axis=0, keepdims=True)

        for g in range(G):
            dmix = dot(db, w[:, pl.ds(3 * D + 256 * g, 256)])
            fq = buf_a[m, rows, fq_at[g]]
            sz = u[sz_at(m, g)]
            nd = dot(fq, sz)
            rden = 1.0 / nd[:, 256:]
            dnum = dmix * rden
            dden = -dnum * (nd[:, :256] * rden)
            de = jnp.concatenate([dnum, dden], axis=1).astype(bf16)
            buf_b[m, rows, pl.ds(D + 512 * g, 512)] = de
            duq = dot_cols(de, sz) * (1.0 - jnp.exp(-fq.astype(f32)))
            dq = (dot_cols(duq.astype(bf16), fmap_ref[g]) * fscale).astype(bf16)
            store(rows, 0, g, dq)
        if mode == 0:
            return
        for g in range(G):
            dsz = dot_rows(buf_a[m, :, fq_at[g]], buf_b[m, :, pl.ds(D + 512 * g, 512)])
            u[sz_at(m, g)] = jnp.where(pair_mask, dsz, 0.0).astype(bf16)
        for part, rows in enumerate(halves if mode == 1 else (whole,)):
            valid = valid_rows(m, rows)
            for g in range(G):
                dsz = u[sz_at(m, g)]
                fk = buf_a[m, rows, fk_at[g]]
                dfk = dot_cols(with_ones(buf_a[m, rows, v_at[g]]), dsz)
                duk = jnp.where(valid, dfk, 0.0) * (1.0 - jnp.exp(-fk.astype(f32)))
                dk = (dot_cols(duk.astype(bf16), fmap_ref[g]) * fscale).astype(bf16)
                store(rows, 1, g, dk)
                store(rows, 2, g, dot(fk, dsz[:, :256]).astype(bf16))
            inner = pl.ds(0, 3 * D)
            dx = nbuf[m, rows, :] + dot(buf_b[m, rows, inner], wt[inner, :])
            dxo[m, rows, :] = dx.astype(bf16)
            for h in (part,) if mode == 1 else (0, 1):
                send_back(m, h)

    def feed_backward(m, mode):
        rows = (halves + (whole,))[mode]
        dpre = norm_backward(m, rows)
        db = dbr[m, rows, :]
        tile = 512
        for j in range(FF // tile):
            c = pl.ds(j * tile, tile)
            da = (dot(db, u[:, c]) * buf_b[m, rows, c].astype(f32)).astype(bf16)
            buf_b[m, rows, c] = da
            bias_grad_ref[:, c] += jnp.sum(da.astype(f32), axis=0, keepdims=True)
        dx = dpre + dot(buf_b[m, rows, :], wt[...])
        dxo[m, rows, :] = dx.astype(bf16)
        for h in (mode,) if mode < 2 else (0, 1):
            send_back(m, h)

    def out_copy(m):
        return pltpu.make_async_copy(out_stage, out_hbm.at[m], stage_sem.at[0])

    def grad_copy(m):
        return pltpu.make_async_copy(grad_stage, grad_hbm.at[m], stage_sem.at[1])

    def write_out(copy, rows, staged, m):
        @pl.when(m >= 1)
        def _():
            copy(m - 1).wait()

        staged[...] = rows[m, pl.ds(0, L), :]
        copy(m).start()

    pad_zero = jnp.zeros((LP - L, D), bf16)
    eye = lax.broadcasted_iota(jnp.int32, (L, L), 0) == lax.broadcasted_iota(jnp.int32, (L, L), 1)

    def forward_step(m, mode):
        if mode != 1:
            @pl.when(first)
            def _():
                land_copy(x_hbm, m).wait()
                xin[m] = jnp.concatenate([land[lax.rem(m, 2)], pad_zero], axis=0)

                @pl.when(m + 2 < M)
                def _():
                    land_copy(x_hbm, m + 2).start()

        @pl.when(s > 0)
        def _():
            for h in (mode,) if mode < 2 else (0, 1):
                next_copy(m, h).wait_recv()

        @pl.when(is_attn)
        def _():
            attend_forward(m, mode)

        @pl.when(is_ff)
        def _():
            feed_forward(m, mode)

        if mode > 0:
            write_out(out_copy, out, out_stage, m)
        if mode > 0:
            @pl.when(first & (m == M - 1))
            def _():
                turn(w, wt, 0, 3 * D // 256)

    def backward_step(m, mode):
        if mode != 1:
            @pl.when(last)
            def _():
                land_copy(cot_hbm, m).wait()
                row = jnp.where(
                    lax.broadcasted_iota(jnp.int32, (1, L), 1) < len_ref[m],
                    pred_ref[pl.ds(m, 1), :].astype(f32),
                    0.0,
                )
                col = jnp.sum(jnp.where(eye, row, 0.0), axis=1, keepdims=True)
                masked = (land[lax.rem(m, 2)].astype(f32) * col).astype(bf16)
                dyin[m] = jnp.concatenate([masked, pad_zero], axis=0)

                @pl.when(m + 2 < M)
                def _():
                    land_copy(cot_hbm, m + 2).start()

        @pl.when(s < NS - 1)
        def _():
            for h in (mode,) if mode < 2 else (0, 1):
                back_copy(m, h).wait_recv()

        @pl.when(is_attn)
        def _():
            attend_backward(m, mode)

        @pl.when(is_ff)
        def _():
            feed_backward(m, mode)

        if mode > 0:
            write_out(grad_copy, dxo, grad_stage, m)

    back_start = jnp.where(s == 0, 16, jnp.where(s == 1, 12, jnp.where(s == 2, 10, 6)))
    relay_start = 12

    def when_due(start, act):
        def at(t):
            i = t - start
            m = i // 2

            apart = i < 0
            for n in SPLIT:
                apart = apart | (m == n % M)
            here = (i >= 0) & (i < 2 * M)

            @pl.when(here & jnp.logical_not(apart) & (lax.rem(i, 2) == 1))
            def _():
                act(m, 2)

            for h in range(2 if SPLIT else 0):
                @pl.when(here & apart & (lax.rem(i, 2) == h))
                def _():
                    act(m, h)

        return at

    forward_at = when_due(2 * s, forward_step)
    backward_at = when_due(back_start, backward_step)

    def tick(t, carry):
        forward_at(t)
        if relayed > 0:
            i = t - relay_start
            for h in range(2):
                @pl.when((s == 0) & (i >= 0) & (i < 2 * relayed) & (lax.rem(i, 2) == h))
                def _():
                    relay_in(relay_lo + i // 2, h).wait_recv()
                    relay_on(relay_lo + i // 2, h).start()
        backward_at(t)
        return carry

    lax.fori_loop(0, 28, tick, 0)

    if relayed > 0:
        @pl.when(s == 0)
        def _():
            for m in range(relay_lo, relay_hi):
                for h in range(2):
                    relay_on(m, h).wait_send()

    @pl.when(is_ff)
    def _():
        for i in range(pieces):
            u_copy_to(u_rows(i), i, 2, sib).wait_send()
        for i in range(2):
            u_copy_to(u_rows(i), i, 1, mate).wait_send()
            u_copy_to(u_rows(i, 1 - side), i, 3, sib).wait_send()

    if in_kernel:
        reduce_gradients(
            cfg,
            s,
            d,
            odd,
            w,
            u,
            wt,
            ut,
            xin,
            dbr,
            buf_a,
            buf_b,
            g_hbm,
            small_ref,
            small_outs,
            *reduce_refs,
        )
    else:
        plain_gradients(cfg, odd, xin, dbr, buf_a, buf_b, g_hbm, g_sem, *reduce_refs)

    for m in range(M):
        for h in range(2):
            @pl.when(s < NS - 1)
            def _():
                next_copy(m, h).wait_send()

            @pl.when(s > 0)
            def _():
                back_copy(m, h).wait_send()

    out_copy(M - 1).wait()
    grad_copy(M - 1).wait()


def place_results(*refs):
    count = (len(refs) - 1) // 3
    sems = refs[-1]
    inward, outward = [], []
    for src, dst, mid in zip(refs[:count], refs[count : 2 * count], refs[2 * count : 3 * count]):
        parts = [(slice(None),)]
        if src.shape[0] > 1:
            step = src.shape[0] // 6
            parts = [(pl.ds(i * step, step),) for i in range(6)]
        for part in parts:
            n = len(inward)
            inward.append(pltpu.make_async_copy(src.at[part], mid.at[part], sems.at[0, n]))
            outward.append(pltpu.make_async_copy(mid.at[part], dst.at[part], sems.at[1, n]))
    for copy in inward:
        copy.start()
    for first, second in zip(inward, outward):
        first.wait()
        second.start()
    for copy in outward:
        copy.wait()


def shards(
    block_input, cotangent, lengths, predicted, slab, in_bias, norm_gain, norm_bias, feature_draws
):
    NS = lax.axis_size("section")
    ND = lax.axis_size("dp")
    M, L, D = block_input.shape
    FF = in_bias.shape[1]
    H, HD, FE = feature_draws.shape
    LP = (L + 15) // 16 * 16
    GH = 256 // HD
    G = D // 256
    GF = GH * FE
    fscale = float((3.0 / (20.0 * HD)) ** 0.5)
    in_kernel = D // ND % 32 == 0 and NS == 4
    C = CHUNK if in_kernel else D
    cfg = (M, L, LP, D, FF, HD, FE, NS, ND, fscale, in_kernel, C)
    hbm = pl.BlockSpec(memory_space=pl.ANY)
    vmem = pl.BlockSpec(memory_space=pltpu.VMEM)
    smem = pl.BlockSpec(memory_space=pltpu.SMEM)
    dma = pltpu.SemaphoreType.DMA
    rows_bf = pltpu.VMEM((M, LP, D), bf16)
    wide_bf = pltpu.VMEM((M, LP, FF), bf16)
    small_size = FF + 2 * D
    smalls = [FF // ND, D // ND, D // ND] if in_kernel else [small_size]
    scratch = [pltpu.VMEM((1, small_size), f32)] if in_kernel else []
    scratch += [
        pltpu.VMEM((G, GH * HD, GF), bf16),
        pltpu.VMEM((H, FE, HD), jnp.int32),
        pltpu.VMEM((D, FF), bf16),
        pltpu.VMEM((D, FF), bf16),
        pltpu.VMEM((FF, D), bf16),
        pltpu.VMEM((FF, D), bf16),
        rows_bf,
        rows_bf,
        rows_bf,
        rows_bf,
        rows_bf,
        pltpu.VMEM((M, LP, D), f32),
        pltpu.VMEM((M, LP, 1), f32),
        wide_bf,
        wide_bf,
        pltpu.VMEM((2, L, D), bf16),
        pltpu.VMEM((L, D), bf16),
        pltpu.VMEM((L, D), bf16),
        dma((3,)),
        dma((2,)),
        dma((4, 4)),
        dma((4, 4)),
        dma((M, 2)),
        dma((M, 2)),
        dma((M, 2)),
        dma((M, 2)),
        dma((2,)),
        dma((1,)),
    ]
    if in_kernel:
        Z, B, chunks = ND // 2, D // ND, 2 * FF // C
        cross = FF // C // 2
        lines = chunks
        scratch += [
            pltpu.SemaphoreType.REGULAR((3,)),
            pltpu.VMEM((Z + 1, Z * B, C), f32),
            pltpu.VMEM((2, Z * B, C), bf16),
            pltpu.VMEM((cross + 1, Z * B, C), bf16),
            pltpu.VMEM((3, Z, B, C), bf16),
            pltpu.VMEM((2, B, C), f32),
            pltpu.VMEM((ND, 1, small_size), f32),
            dma((2,)),
            dma((chunks,)),
            dma((3, Z)),
            dma((lines, Z)),
            dma((lines, Z)),
            dma((2,)),
            dma((cross + 1,)),
            dma((cross + 1,)),
            dma((cross + 1,)),
            dma((cross + 1,)),
            dma((ND,)),
            dma((ND,)),
        ]
        g_shape = (B, FF + FF // 2)
    else:
        scratch += [pltpu.VMEM((D, D), f32)]
        g_shape = (D, 2 * FF)
    section_out, section_grad, grads, *small = pl.pallas_call(
        functools.partial(pipeline_kernel, cfg),
        out_shape=[
            jax.ShapeDtypeStruct((M, L, D), bf16),
            jax.ShapeDtypeStruct((M, L, D), bf16),
            jax.ShapeDtypeStruct(g_shape, f32),
        ]
        + [jax.ShapeDtypeStruct((1, n), f32) for n in smalls],
        in_specs=[smem, hbm, hbm, vmem, hbm, vmem, vmem, vmem, hbm],
        out_specs=[hbm, hbm, hbm] + [vmem] * len(smalls),
        scratch_shapes=scratch,
        compiler_params=pltpu.CompilerParams(
            collective_id=0, has_side_effects=True, vmem_limit_bytes=62 * 2**20
        ),
        name="pipeline",
    )(
        lengths,
        block_input,
        cotangent,
        predicted,
        slab,
        in_bias,
        norm_gain,
        norm_bias,
        jnp.swapaxes(feature_draws, 1, 2),
    )
    if in_kernel:
        results = (section_out, section_grad, grads, *small)
        section_out, section_grad, own, *parts = pl.pallas_call(
            place_results,
            out_shape=[jax.ShapeDtypeStruct(r.shape, r.dtype) for r in results],
            in_specs=[hbm] * len(results),
            out_specs=[hbm] * len(results),
            scratch_shapes=[pltpu.VMEM(r.shape, r.dtype) for r in results] + [dma((2, 6 * len(results)))],
            compiler_params=pltpu.CompilerParams(vmem_limit_bytes=62 * 2**20),
            name="place_results",
        )(*results)
    else:
        def scatter(value):
            return lax.psum_scatter(value, "dp", scatter_dimension=0, tiled=True)

        HALF = FF // 2
        both = scatter(grads)
        sums = small[0][0]
        parts = [scatter(v)[None] for v in (sums[:FF], sums[FF : FF + D], sums[FF + D :])]
        is_attention = lax.axis_index("section") % 2 == 0
        turned = jnp.where(
            is_attention,
            jnp.concatenate([both[:, D:FF], both[:, :D], both[:, FF:]], axis=1),
            jnp.concatenate([both[:, FF:], both[:, :FF]], axis=1),
        )
        pairs = [(i, i - 1) for i in range(1, NS, 2)]
        arrived = lax.ppermute(turned[:, FF : FF + HALF], "section", pairs)
        rest = jnp.where(is_attention, arrived, turned[:, FF + HALF :])
        own = jnp.concatenate([turned[:, :FF], rest], axis=1)
    return (
        section_out[None],
        section_grad[None],
        own[None],
        *parts,
    )


def solution(mesh):
    placed = (
        P("dp", None, None),
        P("dp", None, None),
        P("dp"),
        P("dp", None),
        P("section", None, None),
        P("section", None),
        P("section", None),
        P("section", None),
        P(),
    )
    return jax.shard_map(
        shards,
        mesh=mesh,
        in_specs=placed,
        out_specs=(
            P("section", "dp", None, None),
            P("section", "dp", None, None),
            P("section", "dp", None),
            P("section", "dp"),
            P("section", "dp"),
            P("section", "dp"),
        ),
        check_vma=False,
    )
```
